32 devices in a mesh: dp: 4 (over z), expert: 8 (over y, x, core).
Axes of the slice: x: 2, y: 2, z: 4, core: 2. Of those that a mesh axis runs over, the one named last changes fastest.
Arguments:
- layer_input: bfloat16 [8, 1024, 768], P('dp', 'expert'), may hold values from -6 to 6
- norm1_gain: float32 [768], replicated, may hold values from 0.5 to 1.5
- w_in: bfloat16 [768, 3072], replicated, may hold values from -0.21875 to 0.21875
- conv_weight: float32 [4, 1536], replicated, may hold values from -3 to 3
- conv_bias: float32 [1536], replicated, may hold values from -3 to 3
- w_xproj: bfloat16 [1536, 80], replicated, may hold values from -0.15625 to 0.15625
- w_dt: bfloat16 [48, 1536], replicated, may hold values from -0.875 to 0.875
- dt_bias: float32 [1536], replicated, may hold values from -7 to -2.3
- a_log: float32 [1536, 16], replicated, may hold values from -7 to 2.5
- d_skip: float32 [1536], replicated, may hold values from 0.5 to 1.5
- w_out: bfloat16 [1536, 768], replicated, may hold values from -0.3125 to 0.3125
- norm2_gain: float32 [768], replicated, may hold values from 0.5 to 1.5
- router_weight: bfloat16 [768, 8], replicated, may hold values from -0.125 to 0.125
- w_up: bfloat16 [8, 768, 3072], P('expert', None, 'dp'), may hold values from -0.21875 to 0.21875
- w_down: bfloat16 [8, 3072, 768], P('expert', 'dp'), may hold values from -1.25 to 1.25
- expert_route: int32 [8, 1024], P('dp', 'expert'), may hold values from 0 to 7
- capacity: int32 [8], replicated, may hold values from 30 to 40, as said below
- output_grad: bfloat16 [8, 1024, 768], P('dp', 'expert'), may hold values from -6 to 6
Outputs:
- layer_output: float32 [8, 1024, 768], P('dp', 'expert')
- grad_input: float32 [8, 1024, 768], P('dp', 'expert')
- grad_norm1_gain: float32 [768], replicated
- grad_w_in: float32 [768, 3072], replicated
- grad_conv_weight: float32 [4, 1536], replicated
- grad_conv_bias: float32 [1536], replicated
- grad_w_xproj: float32 [1536, 80], replicated
- grad_w_dt: float32 [48, 1536], replicated
- grad_dt_bias: float32 [1536], replicated
- grad_a_log: float32 [1536, 16], replicated
- grad_d_skip: float32 [1536], replicated
- grad_w_out: float32 [1536, 768], replicated
- grad_norm2_gain: float32 [768], replicated
- grad_w_router: float32 [768, 8], replicated
- grad_w_up: float32 [8, 768, 3072], P('expert', None, 'dp')
- grad_w_down: float32 [8, 3072, 768], P('expert', 'dp')
- expert_loads: float32 [2, 8], replicated
The draws below stay inside these ranges and needn't reach their ends.
Inputs may be any that keep to these rules, and one draw needn't show every extreme that they name: `capacity`: slots of each expert for the tokens of one group; 40 is reached in every draw.
All inputs are finite; a program needn't handle non-finite values.
Results may differ from the reference program's by a relative error of at most 0.012.
Values may be sent and summed in bfloat16 or wider, within the bound.
No kernel may reach another device: no remote copies, remote signals or barrier semaphores. Data moves between devices by JAX's collectives and lax.ppermute only.
A program may use at most 256 MiB of HBM per device.

```python
import math
from functools import partial
import jax
import jax.numpy as jnp
from jax import lax

D = 768
DI = 1536
NS = 16
R = 48
KCONV = 4
FF = 3072
EXPERTS = 8
SEQ_DEV = 2
SPAN = 128
SEQ_LEN = 1024
SEQS = 8
TOK_DEV = 256
CAP = 40
N_DP = 4
N_EXPERT = 8


def hot_experts(key):
    hot_count = max(1, EXPERTS // 8)
    return jax.random.permutation(jax.random.fold_in(key, 7), EXPERTS)[:hot_count].astype(jnp.int32)


def draw_expert_route(key, part):
    hot_count = max(1, EXPERTS // 8)
    hot_list = hot_experts(key)
    base_key = jax.random.fold_in(key, 11)
    grid_shape = (SEQS, SEQ_LEN)
    coin = jax.random.randint(jax.random.fold_in(base_key, 1), grid_shape, 0, 65536)
    hot_pick = jax.random.randint(jax.random.fold_in(base_key, 2), grid_shape, 0, hot_count)
    uniform_pick = jax.random.randint(jax.random.fold_in(base_key, 3), grid_shape, 0, EXPERTS)
    position = jnp.arange(SEQ_LEN, dtype=jnp.int32)[None, :]
    threshold = 16384 + 32768 * position // SEQ_LEN
    return jnp.where(coin < threshold, hot_list[hot_pick], uniform_pick).astype(jnp.int32)


def draw_capacity(key, part):
    hot_list = hot_experts(key)
    base_cap = jax.random.randint(jax.random.fold_in(key, 13), (EXPERTS,), 3 * CAP // 4, CAP + 1)
    is_hot = jnp.any(jnp.arange(EXPERTS, dtype=jnp.int32)[:, None] == hot_list[None, :], axis=1)
    return jnp.where(is_hot, CAP, base_cap).astype(jnp.int32)


def block_scale(own_key, dims, shards, least, largest):
    loudness = 1.0
    for dim, blocks in shards:
        draws = jax.random.uniform(jax.random.fold_in(jax.random.fold_in(own_key, 6), dim), (blocks,), jnp.float32, least / len(shards), largest / len(shards))
        loudness = loudness * jnp.repeat(jnp.exp(draws), dims[dim] // blocks).reshape((-1,) + (1,) * (len(dims) - 1 - dim))
    return loudness


def bell_draw(own_key, dims, spread, bound, cuts=(), kind=jnp.bfloat16):
    drawn = spread * jax.random.normal(own_key, dims, jnp.float32)
    if cuts:
        drawn = drawn * block_scale(own_key, dims, cuts, -0.22, 0.18)
    return jnp.clip(drawn, -bound, bound).astype(kind)


def setup_inputs(seed: int = 0) -> dict:
    seeds = jax.random.split(jax.random.key(seed), 19)
    layer_input = bell_draw(seeds[0], (SEQS, SEQ_LEN, D), 1.0, 6.0, ((0, 4), (1, 8)))
    norm1_gain = jnp.clip(1.0 + 0.1 * jax.random.normal(seeds[1], (D,), jnp.float32), 0.5, 1.5)
    w_in = bell_draw(seeds[2], (D, 2 * DI), D ** -0.5, 0.21875)
    conv_weight = bell_draw(seeds[3], (KCONV, DI), KCONV ** -0.5, 3.0, (), jnp.float32)
    conv_bias = bell_draw(seeds[4], (DI,), 0.5, 3.0, (), jnp.float32)
    w_xproj = bell_draw(seeds[5], (DI, R + 2 * NS), DI ** -0.5, 0.15625)
    w_dt = bell_draw(seeds[6], (R, DI), R ** -0.5, 0.875)
    dt_bias = jnp.clip(jax.random.uniform(seeds[7], (DI,), jnp.float32, -7.0, -2.3), -7.0, -2.3)
    a_log = jnp.clip(jax.random.uniform(seeds[8], (DI, NS), jnp.float32, -7.0, 2.5), -7.0, 2.5)
    d_skip = jnp.clip(jax.random.uniform(seeds[9], (DI,), jnp.float32, 0.5, 1.5), 0.5, 1.5)
    w_out = bell_draw(seeds[10], (DI, D), (DI // 4) ** -0.5, 0.3125)
    norm2_gain = jnp.clip(1.0 + 0.1 * jax.random.normal(seeds[11], (D,), jnp.float32), 0.5, 1.5)
    router_weight = bell_draw(seeds[12], (D, EXPERTS), (3 * D) ** -0.5, 0.125)
    w_up = bell_draw(seeds[13], (EXPERTS, D, FF), D ** -0.5, 0.21875, ((0, 8), (2, 4)))
    w_down = bell_draw(seeds[14], (EXPERTS, FF, D), (max(1, (2 * FF) // (5 * EXPERTS * EXPERTS))) ** -0.5, 1.25, ((0, 8), (1, 4)))
    expert_route = draw_expert_route(jax.random.fold_in(seeds[18], 71), 0)
    capacity = draw_capacity(jax.random.fold_in(seeds[18], 71), 0)
    output_grad = bell_draw(seeds[17], (SEQS, SEQ_LEN, D), 1.0, 6.0, ((0, 4), (1, 8)))
    return {"layer_input": layer_input, "norm1_gain": norm1_gain, "w_in": w_in, "conv_weight": conv_weight, "conv_bias": conv_bias, "w_xproj": w_xproj, "w_dt": w_dt, "dt_bias": dt_bias, "a_log": a_log, "d_skip": d_skip, "w_out": w_out, "norm2_gain": norm2_gain, "router_weight": router_weight, "w_up": w_up, "w_down": w_down, "expert_route": expert_route, "capacity": capacity, "output_grad": output_grad}


@jax.custom_vjp
def low(v):
    return lax.optimization_barrier(v.astype(jnp.bfloat16)).astype(jnp.float32)

@jax.custom_vjp
def low_back(v):
    return v

def low_keep(v):
    return (low(v), None)

def low_pass(kept, grad):
    return (grad,)

def back_keep(v):
    return (v, None)

def back_low(kept, grad):
    return (low(grad),)
low.defvjp(low_keep, low_pass)
low_back.defvjp(back_keep, back_low)
EXACT_PRECISION = lax.Precision.HIGHEST
EPSILON = 1e-05

def rms_norm(values, gain_vec):
    inv_rms = lax.rsqrt(lax.optimization_barrier(jnp.mean(values * values, axis=-1, keepdims=True)) + EPSILON)
    return values * inv_rms * gain_vec

def matmul_hi(left, right):
    return jnp.dot(left, right, precision=EXACT_PRECISION)

def pair_combine(earlier, latter):
    return (earlier[0] * latter[0], latter[0] * earlier[1] + latter[1])

def mamba_sequence(weights, seq_stream):
    gain_one, w_in, conv_weight, conv_bias, w_xproj, w_dt, dt_bias, a_log, d_skip, w_out = weights
    normed = low(rms_norm(seq_stream, gain_one))
    projected = low_back(matmul_hi(normed, w_in))
    conv_in = low(projected[:, :DI])
    gate_z = projected[:, DI:]
    padded = jnp.concatenate([jnp.zeros((KCONV - 1, DI), jnp.float32), conv_in], axis=0)
    pre_conv = conv_bias + sum((conv_weight[offset] * padded[offset:offset + SEQ_LEN] for offset in range(KCONV)))
    activation = low(jax.nn.silu(pre_conv))
    selection = low_back(matmul_hi(activation, w_xproj))
    dt_low = low(selection[:, :R])
    in_mat = selection[:, R:R + NS]
    out_mat = selection[:, R + NS:]
    step_size = jax.nn.softplus(low_back(matmul_hi(dt_low, w_dt)) + dt_bias)
    decay_rate = -jnp.exp(a_log)
    block_len = math.gcd(SEQ_LEN, 128)
    block_count = SEQ_LEN // block_len

    def scan_block(carry_state, pieces):
        step_blk, act_blk, in_blk, output_block_rows = pieces
        decays = jnp.exp(step_blk[:, :, None] * decay_rate[None, :, :])
        drive = (step_blk * act_blk)[:, :, None] * in_blk[:, None, :]
        drive = drive.at[0].add(decays[0] * carry_state)
        states = lax.associative_scan(pair_combine, (decays, drive))[1]
        block_out = jnp.einsum('tcn,tn->tc', states, output_block_rows, precision=EXACT_PRECISION)
        return (states[-1], block_out)
    start_state = jnp.zeros((DI, NS), jnp.float32)
    pieces = (step_size.reshape(block_count, block_len, DI), activation.reshape(block_count, block_len, DI), in_mat.reshape(block_count, block_len, NS), out_mat.reshape(block_count, block_len, NS))
    outputs = lax.scan(jax.checkpoint(scan_block), start_state, pieces)[1]
    scanned = outputs.reshape(SEQ_LEN, DI) + d_skip * activation
    gated = low(scanned * jax.nn.silu(gate_z))
    return low_back(matmul_hi(gated, w_out))

def to_groups(values):
    tail = values.shape[2:]
    grouped = values.reshape((N_DP, SEQ_DEV, N_EXPERT, SPAN) + tail)
    grouped = jnp.moveaxis(grouped, 2, 1)
    return grouped.reshape((N_DP * N_EXPERT, TOK_DEV) + tail)

def from_groups(values):
    tail = values.shape[2:]
    grouped = values.reshape((N_DP, N_EXPERT, SEQ_DEV, SPAN) + tail)
    grouped = jnp.moveaxis(grouped, 1, 2)
    return grouped.reshape((SEQS, SEQ_LEN) + tail)

def slot_table(expert_route, capacity):
    group_route = to_groups(expert_route)
    one_hot = (group_route[:, :, None] == jnp.arange(EXPERTS, dtype=jnp.int32)[None, None, :]).astype(jnp.int32)
    slot_rank = lax.optimization_barrier(jnp.sum((jnp.cumsum(one_hot, axis=1) - one_hot) * one_hot, axis=-1)).astype(jnp.int32)
    slot_limit = lax.optimization_barrier(jnp.sum(one_hot * capacity[None, None, :], axis=-1)).astype(jnp.int32)
    kept_mask = slot_rank < slot_limit
    slot_index = jnp.where(kept_mask, group_route * CAP + slot_rank, EXPERTS * CAP).astype(jnp.int32)
    return (one_hot, kept_mask, slot_index)

def moe_block(weights, stream_two, expert_route, slot_index):
    gain_two, router_weight, w_up, w_down = weights
    switch_input = low(rms_norm(stream_two, gain_two))
    router_scores = jnp.einsum('ocy,yw->ocw', switch_input, router_weight, precision=EXACT_PRECISION)
    router_prob = jax.nn.softmax(router_scores, axis=-1)
    choose = (expert_route[:, :, None] == jnp.arange(EXPERTS, dtype=jnp.int32)[None, None, :]).astype(jnp.float32)
    gate_prob = lax.optimization_barrier(jnp.sum(router_prob * choose, axis=-1))
    group_in = to_groups(switch_input)
    groups = N_DP * N_EXPERT

    def place_rows(row_block, target):
        return jnp.zeros((EXPERTS * CAP + 1, D), jnp.float32).at[target].add(row_block)[:EXPERTS * CAP]
    dispatched = jax.vmap(place_rows)(group_in, slot_index)
    dispatched = dispatched.reshape(groups, EXPERTS, CAP, D).transpose(1, 0, 2, 3).reshape(EXPERTS, groups * CAP, D)
    dispatched = low_back(dispatched)

    def run_expert(pieces):
        row_block, up_mat, down_mat = pieces
        pre_act = low_back(matmul_hi(row_block, up_mat))
        hidden = low(jax.nn.gelu(pre_act))
        return low_back(low(matmul_hi(hidden, down_mat)))
    expert_out = lax.map(jax.checkpoint(run_expert), (dispatched, w_up, w_down))
    expert_out = expert_out.reshape(EXPERTS, groups, CAP, D).transpose(1, 0, 2, 3).reshape(groups, EXPERTS * CAP, D)
    expert_out = jnp.concatenate([expert_out, jnp.zeros((groups, 1, D), jnp.float32)], axis=1)
    picked = jnp.take_along_axis(expert_out, slot_index[:, :, None], axis=1)
    return stream_two + gate_prob[:, :, None] * from_groups(picked)

def reference(layer_input, norm1_gain, w_in, conv_weight, conv_bias, w_xproj, w_dt, dt_bias, a_log, d_skip, w_out, norm2_gain, router_weight, w_up, w_down, expert_route, capacity, output_grad):
    one_hot, kept_mask, slot_index = slot_table(expert_route, capacity)
    floats = tuple((tensor.astype(jnp.float32) for tensor in (layer_input, norm1_gain, w_in, conv_weight, conv_bias, w_xproj, w_dt, dt_bias, a_log, d_skip, w_out, norm2_gain, router_weight, w_up, w_down)))

    def forward(stream, *weights):
        mamba_weights = weights[:10]
        moe_weights = weights[10:]
        mixer = lax.map(jax.checkpoint(partial(mamba_sequence, mamba_weights)), stream)
        return moe_block(moe_weights, stream + mixer, expert_route, slot_index)
    result, pullback = jax.vjp(forward, *floats)
    gradients = pullback(output_grad.astype(jnp.float32))
    kept_count = lax.optimization_barrier(jnp.sum(one_hot * kept_mask[:, :, None].astype(jnp.int32), axis=(0, 1))).astype(jnp.float32)
    total_token_count = lax.optimization_barrier(jnp.sum(one_hot, axis=(0, 1))).astype(jnp.float32)
    expert_loads = jnp.stack([kept_count, total_token_count - kept_count]) * (EXPERTS / (SEQS * SEQ_LEN))
    return (result, gradients[0], gradients[1], gradients[2], gradients[3], gradients[4], gradients[5], gradients[6], gradients[7], gradients[8], gradients[9], gradients[10], gradients[11], gradients[12], gradients[13], gradients[14], expert_loads)
```

```python
import jax
import jax.numpy as jnp
from jax import lax
from jax.experimental import pallas as pl
from jax.experimental.pallas import tpu as pltpu
from jax.sharding import PartitionSpec as P

f32 = jnp.float32
bf16 = jnp.bfloat16
LN=128
SUB=16
VM=pl.BlockSpec(memory_space=pltpu.VMEM)

def _lane_tiles(width): return width//LN

def _spread(src_ref, dst_ref, seq, span):
    ns=src_ref.shape[1]
    for base in range(0, span, LN):
        w=min(LN, span-base)
        v=src_ref[seq, :, base:base+w]
        for t in range(w):
            dst_ref[base+t]=jnp.broadcast_to(v[:, t:t+1], (ns, LN))

GROUP=4
BG=2
def _row(v, i, ns):
    return jnp.broadcast_to(v[i:i+1], (ns, LN))
def _groups(tiles):
    return [range(g, min(g+GROUP, tiles)) for g in range(0, tiles, GROUP)]
def _at(ref, seq, t0, j):
    return ref[seq, pl.ds(pl.multiple_of(t0,SUB), SUB), j*LN:(j+1)*LN]

def fwd_end_kernel(dt_ref, dx_ref, bt_ref, rate_ref, end_ref, cum_ref, bb_ref):
    seqs, span, width = dt_ref.shape
    ns=rate_ref.shape[0]
    tiles=width//LN
    for seq in range(seqs):
        _spread(bt_ref, bb_ref, seq, span)
        def step(k, state):
            t0=k*SUB
            state=list(state)
            for grp in _groups(tiles):
                dt={j:_at(dt_ref,seq,t0,j) for j in grp}; dx={j:_at(dx_ref,seq,t0,j) for j in grp}
                for i in range(SUB):
                    b=bb_ref[t0+i]
                    for j in grp:
                        a=jnp.exp2(_row(dt[j],i,ns)*rate_ref[:, j*LN:(j+1)*LN])
                        state[j]=a*state[j]+_row(dx[j],i,ns)*b
            return tuple(state)
        st=lax.fori_loop(0, span//SUB, step, tuple(jnp.zeros((ns,LN),f32) for _ in range(tiles)))
        for j in range(tiles): end_ref[seq,:,j*LN:(j+1)*LN]=st[j]
        cum_ref[seq:seq+1,:]=jnp.sum(dt_ref[seq],axis=0,keepdims=True)

def fwd_end(dt, dx, bt, rate2):
    s,t,w=dt.shape; n=rate2.shape[0]
    return pl.pallas_call(fwd_end_kernel, out_shape=(jax.ShapeDtypeStruct((s,n,w),f32), jax.ShapeDtypeStruct((s,w),f32)),
        in_specs=[VM]*4, out_specs=(VM,VM), scratch_shapes=[pltpu.VMEM((t,n,LN),f32)],
        compiler_params=pltpu.CompilerParams(vmem_limit_bytes=48<<20))(dt,dx,bt,rate2)

def fwd_out_kernel(dt_ref, dx_ref, bt_ref, rate_ref, start_ref, cd_ref, h_ref, y_ref, bb_ref, st_ref):
    _, span, width = dt_ref.shape
    ns=rate_ref.shape[0]
    tiles=width//LN
    _spread(bt_ref, bb_ref, 0, span)
    st_ref[...]=start_ref[0]
    h_ref[0, 0:ns, :]=start_ref[0].astype(bf16)
    def chunk(k, carry):
        t0=k*SUB
        for grp in _groups(tiles):
            state={j:st_ref[:, j*LN:(j+1)*LN] for j in grp}
            dt={j:_at(dt_ref,0,t0,j) for j in grp}; dx={j:_at(dx_ref,0,t0,j) for j in grp}
            for i in range(SUB):
                b=bb_ref[t0+i]
                for j in grp:
                    a=jnp.exp2(_row(dt[j],i,ns)*rate_ref[:, j*LN:(j+1)*LN])
                    state[j]=a*state[j]+_row(dx[j],i,ns)*b
                    h_ref[0, pl.ds(pl.multiple_of((t0+i+1)*ns,ns), ns), j*LN:(j+1)*LN]=state[j].astype(bf16)
            for j in grp: st_ref[:, j*LN:(j+1)*LN]=state[j]
        r=jnp.dot(cd_ref[0,k], h_ref[0, pl.ds(pl.multiple_of((t0+1)*ns,ns), SUB*ns), :], preferred_element_type=f32)
        y_ref[0, pl.ds(pl.multiple_of(t0,SUB), SUB), :]=r[:SUB]+r[SUB:]
        return carry
    lax.fori_loop(0, span//SUB, chunk, 0)

def fwd_out(dt, dx, bt, rate2, start, cd):
    s,t,w=dt.shape; n=rate2.shape[0]
    seqb=lambda *shape: pl.BlockSpec((1,)+shape, lambda i: (i,)+(0,)*len(shape))
    full=lambda *shape: pl.BlockSpec(shape, lambda i: (0,)*len(shape))
    return pl.pallas_call(fwd_out_kernel, grid=(s,),
        out_shape=(jax.ShapeDtypeStruct((s,(t+1)*n,w),bf16), jax.ShapeDtypeStruct((s,t,w),f32)),
        in_specs=[seqb(t,w),seqb(t,w),seqb(n,t),full(n,w),seqb(n,w),seqb(*cd.shape[1:])],
        out_specs=(seqb((t+1)*n,w),seqb(t,w)),
        scratch_shapes=[pltpu.VMEM((t,n,LN),f32), pltpu.VMEM((n,w),f32)],
        compiler_params=pltpu.CompilerParams(vmem_limit_bytes=56<<20))(dt,dx,bt,rate2,start,cd)

def bwd_head_kernel(dt_ref, yg_ref, ct_ref, rate_ref, head_ref, cb_ref):
    seqs, span, width = dt_ref.shape
    ns=rate_ref.shape[0]
    tiles=width//LN
    for seq in range(seqs):
        _spread(ct_ref, cb_ref, seq, span)
        def step(u, mu):
            t0=span-SUB-u*SUB
            mu=list(mu)
            for grp in _groups(tiles):
                dt={j:_at(dt_ref,seq,t0,j) for j in grp}; yg={j:_at(yg_ref,seq,t0,j) for j in grp}
                for i in reversed(range(SUB)):
                    c=cb_ref[t0+i]
                    for j in grp:
                        a=jnp.exp2(_row(dt[j],i,ns)*rate_ref[:, j*LN:(j+1)*LN])
                        mu[j]=a*(mu[j]+_row(yg[j],i,ns)*c)
            return tuple(mu)
        st=lax.fori_loop(0, span//SUB, step, tuple(jnp.zeros((ns,LN),f32) for _ in range(tiles)))
        for j in range(tiles): head_ref[seq,:,j*LN:(j+1)*LN]=st[j]

def bwd_head(dt, yg, ct, rate2):
    s,t,w=dt.shape; n=rate2.shape[0]
    return pl.pallas_call(bwd_head_kernel, out_shape=jax.ShapeDtypeStruct((s,n,w),f32),
        in_specs=[VM]*4, out_specs=VM, scratch_shapes=[pltpu.VMEM((t,n,LN),f32)],
        compiler_params=pltpu.CompilerParams(vmem_limit_bytes=48<<20))(dt,yg,ct,rate2)

NT=(((1,),(1,)),((),()))
def bwd_seq_kernel(dt_ref, dx_ref, yg_ref, ct_ref, rate_ref, rl_ref, tail_ref, bd_ref, one_ref, h_ref,
                   s1_ref, adj_ref, ig_ref, og_ref, al_ref, cb_ref, mu_ref, lam_ref, rdg_ref):
    _, span, width = dt_ref.shape
    ns=rate_ref.shape[0]
    tiles=width//LN
    _spread(ct_ref, cb_ref, 0, span)
    mu_ref[...]=tail_ref[0]
    al_ref[0]=jnp.zeros((ns,width),f32)
    nch=span//SUB
    def chunk(v, carry):
        k=nch-1-v
        t0=k*SUB
        for g in range(0,tiles,BG):
            grp=range(g,min(g+BG,tiles))
            S={j:slice(j*LN,(j+1)*LN) for j in grp}
            mu={j:mu_ref[:, S[j]] for j in grp}; al={j:al_ref[0,:,S[j]] for j in grp}
            dtc={j:_at(dt_ref,0,t0,j) for j in grp}; ygc={j:_at(yg_ref,0,t0,j) for j in grp}
            for i in reversed(range(SUB)):
                t=t0+i
                c=cb_ref[t]
                for j in grp:
                    sl=S[j]
                    dt=_row(dtc[j],i,ns); yg=_row(ygc[j],i,ns)
                    a=jnp.exp2(dt*rate_ref[:,sl])
                    lam=mu[j]+yg*c
                    mu[j]=a*lam
                    dg=mu[j]*h_ref[0, pl.ds(pl.multiple_of(t*ns,ns), ns), sl].astype(f32)
                    al[j]=al[j]+dt*dg
                    lam_ref[i*ns:(i+1)*ns, sl]=lam.astype(bf16)
                    rdg_ref[i*ns:(i+1)*ns, sl]=(rl_ref[:,sl]*dg).astype(bf16)
            for j in grp:
                mu_ref[:, S[j]]=mu[j]; al_ref[0,:,S[j]]=al[j]
        tt=pl.ds(pl.multiple_of(t0,SUB), SUB)
        lam=lam_ref[...]
        r=jnp.dot(bd_ref[0,k], lam, preferred_element_type=f32)
        adj_ref[0, tt, :]=r[:SUB]+r[SUB:]
        s1_ref[0, tt, :]=jnp.dot(one_ref[...], rdg_ref[...], preferred_element_type=f32)
        rows=lax.broadcasted_iota(jnp.int32,(SUB*ns,SUB),0)//ns
        cols=lax.broadcasted_iota(jnp.int32,(SUB*ns,SUB),1)
        own=rows==cols
        d=lax.dot_general(lam, dx_ref[0,tt,:].astype(bf16), NT, preferred_element_type=f32)
        ig_ref[0,k]=jnp.sum(jnp.where(own,d,0.0).reshape(SUB,ns,SUB),axis=0)
        hh=h_ref[0, pl.ds(pl.multiple_of((t0+1)*ns,ns), SUB*ns), :]
        d=lax.dot_general(hh, yg_ref[0,tt,:].astype(bf16), NT, preferred_element_type=f32)
        og_ref[0,k]=jnp.sum(jnp.where(own,d,0.0).reshape(SUB,ns,SUB),axis=0)
        return carry
    lax.fori_loop(0, nch, chunk, 0)

def bwd_seq(dt, dx, yg, ct, rate2, rate, tail, bd, one, h):
    s,t,w=dt.shape; n=rate2.shape[0]
    seqb=lambda *shape: pl.BlockSpec((1,)+shape, lambda i: (i,)+(0,)*len(shape))
    full=lambda *shape: pl.BlockSpec(shape, lambda i: (0,)*len(shape))
    nch=t//SUB
    return pl.pallas_call(bwd_seq_kernel, grid=(s,),
        out_shape=(jax.ShapeDtypeStruct((s,t,w),f32), jax.ShapeDtypeStruct((s,t,w),f32), jax.ShapeDtypeStruct((s,nch,n,SUB),f32), jax.ShapeDtypeStruct((s,nch,n,SUB),f32), jax.ShapeDtypeStruct((s,n,w),f32)),
        in_specs=[seqb(t,w),seqb(t,w),seqb(t,w),seqb(n,t),full(n,w),full(n,w),seqb(n,w),seqb(*bd.shape[1:]),full(*one.shape),seqb((t+1)*n,w)],
        out_specs=(seqb(t,w),seqb(t,w),seqb(nch,n,SUB),seqb(nch,n,SUB),seqb(n,w)),
        scratch_shapes=[pltpu.VMEM((t,n,LN),f32), pltpu.VMEM((n,w),f32), pltpu.VMEM((SUB*n,w),bf16), pltpu.VMEM((SUB*n,w),bf16)],
        compiler_params=pltpu.CompilerParams(vmem_limit_bytes=56<<20))(dt,dx,yg,ct,rate2,rate,tail,bd,one,h)

def block_diag(mat):
    s,t,n=mat.shape
    m=mat.reshape(s,t//SUB,1,SUB,n)
    eye=jnp.eye(SUB,dtype=f32).reshape(1,1,SUB,SUB,1)
    d=(eye*m).reshape(s,t//SUB,SUB,SUB*n)
    hi=d.astype(bf16); lo=(d-hi.astype(f32)).astype(bf16)
    return jnp.concatenate([hi,lo],axis=2)
def ones_diag(n):
    return jnp.repeat(jnp.eye(SUB,dtype=bf16),n,axis=1)

EXACT_PRECISION = lax.Precision.HIGHEST
EPSILON = 1e-05
LOG2E = 1.4426950408889634


def shifted(value, axis, steps):
    count = lax.axis_size(axis)
    leading, last = (max(0, -steps), min(count, count - steps))
    return lax.ppermute(value, axis, [(source, source + steps) for source in range(leading, last)])


def swapped(value, axis, mask):
    return lax.ppermute(value, axis, [(i, i ^ mask) for i in range(lax.axis_size(axis))])


def rms_forward(values, gain_vec):
    inv_rms = lax.rsqrt(jnp.mean(values * values, axis=-1, keepdims=True) + EPSILON)
    return (values * inv_rms * gain_vec, inv_rms)


def rms_backward(values, gain_vec, inv_rms, upstream):
    normal = values * inv_rms
    gain_grad = jnp.sum(upstream * normal, axis=(0, 1))
    weighted = upstream * gain_vec
    return (
        inv_rms * (weighted - normal * jnp.mean(weighted * normal, axis=-1, keepdims=True)),
        gain_grad,
    )


def silu_slope(values):
    logistic = jax.nn.sigmoid(values)
    return logistic * (1.0 + values * (1.0 - logistic))


def plain_dot(left, right):
    return jnp.dot(left, right, preferred_element_type=f32)


def inner_left(left, right):
    return lax.dot_general(left, right, (((0,), (0,)), ((), ())), preferred_element_type=f32)


def inner_right(left, right):
    return lax.dot_general(left, right, (((1,), (1,)), ((), ())), preferred_element_type=f32)


def gather_states(state, cum):
    s, n, w = state.shape
    hi = cum.astype(bf16)
    lo = (cum - hi.astype(f32)).astype(bf16)
    rows = jnp.concatenate([state.reshape(s * n, w).astype(bf16), hi, lo], axis=0)
    every = lax.all_gather(rows, "expert").astype(f32)
    count = every.shape[0]
    return (
        every[:, : s * n].reshape(count, s, n, w),
        every[:, s * n : s * n + s] + every[:, s * n + s :],
    )


def carried(states, cums, rate2, backward):
    count = states.shape[0]
    mine = lax.axis_index("expert")
    total = jnp.zeros_like(states[0])
    order = range(count - 1, 0, -1) if backward else range(count - 1)
    for place in order:
        longer = jnp.exp2(cums[place][:, None, :] * rate2[None]) * total + states[place]
        total = jnp.where(place > mine if backward else place < mine, longer, total)
    return total


def summed_rows(parts):
    experts, groups = (lax.axis_size("expert"), lax.axis_size("dp"))
    rows, cols = parts.shape
    low = parts.astype(bf16).reshape(experts, rows // experts, cols)
    mine = lax.all_to_all(low, "expert", split_axis=0, concat_axis=0, tiled=True)
    part = jnp.sum(mine.astype(f32), axis=0).astype(bf16)
    part = part.reshape(groups, rows // experts // groups, cols)
    mine = lax.all_to_all(part, "dp", split_axis=0, concat_axis=0, tiled=True)
    part = jnp.sum(mine.astype(f32), axis=0).astype(bf16)
    return lax.all_gather(part, ("expert", "dp"), axis=0, tiled=True)


def expert_math(rows, og_rows, up_mat, down_mat, router_weight):
    probs = jax.nn.softmax(plain_dot(rows, router_weight), axis=-1)
    own = (jnp.arange(probs.shape[1]) == lax.axis_index("expert")).astype(f32)[None]
    gate = jnp.sum(probs * own, axis=1, keepdims=True)
    og = og_rows.astype(f32)
    grads_low = (og * gate).astype(bf16)
    pre_act = plain_dot(rows, up_mat)
    hidden, gelu_pull = jax.vjp(jax.nn.gelu, pre_act)
    hidden_low = hidden.astype(bf16)
    forward_part = plain_dot(hidden_low, down_mat)
    pre_grad = gelu_pull(inner_right(grads_low, down_mat))[0].astype(bf16)
    gate_grad = jnp.sum(og * forward_part, axis=1, keepdims=True)
    logit_grad = gate_grad * gate * (own - probs)
    backward_part = inner_right(pre_grad, up_mat) + lax.dot_general(
        logit_grad,
        router_weight.astype(f32),
        (((1,), (1,)), ((), ())),
        precision=EXACT_PRECISION,
    )
    return (forward_part, backward_part, hidden_low, grads_low, pre_grad, logit_grad)


def body(
    layer_input,
    norm1_gain,
    w_in,
    conv_weight,
    conv_bias,
    w_xproj,
    w_dt,
    dt_bias,
    a_log,
    d_skip,
    w_out,
    norm2_gain,
    router_weight,
    w_up,
    w_down,
    expert_route,
    capacity,
    output_grad,
):
    seq_count, span_len, model_width = layer_input.shape
    inner_width = w_in.shape[1] // 2
    conv_taps = conv_weight.shape[0]
    rank_dt = w_dt.shape[0]
    state_width = a_log.shape[1]
    experts_all = router_weight.shape[1]
    tokens = seq_count * span_len
    groups, holders = (lax.axis_size("dp"), lax.axis_size("expert"))
    slot_count = max(2, 5 * tokens // (4 * experts_all))
    slots = experts_all * slot_count

    flat_route = expert_route.reshape(tokens)
    choose = (flat_route[:, None] == jnp.arange(experts_all, dtype=jnp.int32)[None, :]).astype(f32)
    earlier = (
        jnp.arange(tokens, dtype=jnp.int32)[:, None] > jnp.arange(tokens, dtype=jnp.int32)[None, :]
    ).astype(bf16)
    slot_rank = jnp.sum(plain_dot(earlier, choose.astype(bf16)) * choose, axis=1)
    slot_limit = jnp.sum(choose * capacity.astype(f32)[None, :], axis=1)
    kept_mask = slot_rank < slot_limit
    kept_float = kept_mask.astype(f32)
    target = jnp.where(kept_mask, flat_route * slot_count + slot_rank.astype(jnp.int32), slots)
    pick = (target[None, :] == jnp.arange(slots, dtype=jnp.int32)[:, None]).astype(bf16)

    def sent(rows):
        placed = plain_dot(pick, rows).astype(bf16).reshape(experts_all, slot_count, model_width)
        got = lax.all_to_all(placed, "expert", split_axis=0, concat_axis=0, tiled=True)
        return got.reshape(slots, model_width)

    def returned(rows):
        back = rows.astype(bf16).reshape(experts_all, slot_count, model_width)
        got = lax.all_to_all(back, "expert", split_axis=0, concat_axis=0, tiled=True)
        return inner_left(pick, got.reshape(slots, model_width))

    og_own = sent(output_grad.reshape(tokens, model_width))
    og_other = swapped(og_own, "dp", 1)
    w_masks = range(2, groups, 2)
    up_mats = [w_up[0]] + [swapped(w_up[0], "dp", mask) for mask in w_masks]
    down_mats = [w_down[0]] + [swapped(w_down[0], "dp", mask) for mask in w_masks]
    up_full = jnp.concatenate(up_mats, axis=1)
    down_full = jnp.concatenate(down_mats, axis=0)

    stream = layer_input.astype(f32)
    normed_one, inv_one = rms_forward(stream, norm1_gain)
    normed_low = normed_one.astype(bf16)
    projected = plain_dot(normed_low, w_in)
    conv_in = projected[..., :inner_width].astype(bf16)
    gate_z = projected[..., inner_width:]
    rim_rows = shifted(conv_in[:, span_len - conv_taps + 1 :, :], "expert", 1)
    padded = jnp.concatenate([rim_rows, conv_in], axis=1).astype(f32)
    pre_conv = conv_bias + sum(
        (conv_weight[offset] * padded[:, offset : offset + span_len] for offset in range(conv_taps))
    )
    activation_low = jax.nn.silu(pre_conv).astype(bf16)
    activation = activation_low.astype(f32)
    selection = plain_dot(activation_low, w_xproj)
    dt_low = selection[..., :rank_dt].astype(bf16)
    in_mat = selection[..., rank_dt : rank_dt + state_width]
    out_mat = selection[..., rank_dt + state_width :]
    in_t = in_mat.transpose(0, 2, 1)
    out_t = out_mat.transpose(0, 2, 1)
    dt_pre = plain_dot(dt_low, w_dt) + dt_bias
    step_size = jax.nn.softplus(dt_pre)
    drive_x = step_size * activation
    rate = -jnp.exp(a_log).T
    rate2 = rate * LOG2E
    end_state, cum_step = fwd_end(step_size, drive_x, in_t, rate2)
    states, cums = gather_states(end_state, cum_step)
    start_state = carried(states, cums, rate2, False)
    saved, scanned = fwd_out(step_size, drive_x, in_t, rate2, start_state, block_diag(out_mat))
    y_full = scanned + d_skip * activation
    gate_silu = jax.nn.silu(gate_z)
    gated = (y_full * gate_silu).astype(bf16)
    stream_two = stream + plain_dot(gated, w_out)
    normed_two, inv_two = rms_forward(stream_two, norm2_gain)
    flat_in = normed_two.astype(bf16).reshape(tokens, model_width)
    router_prob = jax.nn.softmax(plain_dot(flat_in, router_weight), axis=-1)
    gate_prob = jnp.sum(router_prob * choose, axis=1)

    row_own = sent(flat_in)
    row_other = swapped(row_own, "dp", 1)
    fwd_a, bwd_a, hid_a, grd_a, pre_a, log_a = expert_math(
        row_own, og_own, up_full, down_full, router_weight
    )
    fwd_b, bwd_b, hid_b, grd_b, pre_b, log_b = expert_math(
        row_other, og_other, up_full, down_full, router_weight
    )
    moe_in_grad = returned(bwd_a + swapped(bwd_b.astype(bf16), "dp", 1).astype(f32))
    expert_tok = returned(fwd_a + swapped(fwd_b.astype(bf16), "dp", 1).astype(f32))
    result = stream_two + (gate_prob[:, None] * expert_tok).reshape(layer_input.shape)
    rows_ab = jnp.concatenate([row_own, row_other], axis=0)
    up_grad = inner_left(rows_ab, jnp.concatenate([pre_a, pre_b], axis=0))
    down_grad = inner_left(
        jnp.concatenate([hid_a, hid_b], axis=0), jnp.concatenate([grd_a, grd_b], axis=0)
    )
    grad_w_router = lax.dot_general(
        rows_ab.astype(f32),
        jnp.concatenate([log_a, log_b], axis=0),
        (((0,), (0,)), ((), ())),
        precision=EXACT_PRECISION,
    )
    part = w_up.shape[2]
    grad_w_up = up_grad[:, :part]
    grad_w_down = down_grad[:part]
    for place, mask in enumerate(w_masks, 1):
        cut = slice(place * part, (place + 1) * part)
        grad_w_up += swapped(up_grad[:, cut].astype(bf16), "dp", mask).astype(f32)
        grad_w_down += swapped(down_grad[cut].astype(bf16), "dp", mask).astype(f32)

    norm_two_grad, grad_gain_two = rms_backward(
        stream_two, norm2_gain, inv_two, moe_in_grad.reshape(layer_input.shape)
    )
    stream_two_grad = output_grad.astype(f32) + norm_two_grad
    mix_grad_low = stream_two_grad.astype(bf16).reshape(tokens, model_width)
    grad_w_out = inner_left(gated.reshape(tokens, inner_width), mix_grad_low)
    gated_grad = inner_right(mix_grad_low, w_out).reshape(seq_count, span_len, inner_width)
    y_grad = gated_grad * gate_silu
    z_grad = gated_grad * y_full * silu_slope(gate_z)
    z_grad_low = z_grad.astype(bf16).reshape(tokens, inner_width)
    normed_flat = normed_low.reshape(tokens, model_width)
    grad_w_in_z = inner_left(normed_flat, z_grad_low)
    total_w_out = summed_rows(grad_w_out)
    total_w_in_z = summed_rows(grad_w_in_z)
    grad_d_skip = jnp.sum(y_grad * activation, axis=(0, 1))
    head = bwd_head(step_size, y_grad, out_t, rate2)
    heads, _ = gather_states(head, cum_step)
    tail_adj = carried(heads, cums, rate2, True)
    step_rate, adj_in, in_parts, out_parts, rate_parts = bwd_seq(
        step_size,
        drive_x,
        y_grad,
        out_t,
        rate2,
        rate,
        tail_adj,
        block_diag(in_mat),
        ones_diag(state_width),
        saved,
    )
    in_grad = in_parts.transpose(0, 1, 3, 2).reshape(tokens, state_width)
    out_grad_mat = out_parts.transpose(0, 1, 3, 2).reshape(tokens, state_width)
    grad_a_log = rate * jnp.sum(rate_parts, axis=0)
    step_grad = step_rate + adj_in * activation
    dt_pre_grad = step_grad * jax.nn.sigmoid(dt_pre)
    grad_dt_bias = jnp.sum(dt_pre_grad, axis=(0, 1))
    dt_pre_low = dt_pre_grad.astype(bf16).reshape(tokens, inner_width)
    grad_w_dt = inner_left(dt_low.reshape(tokens, rank_dt), dt_pre_low)
    dt_low_grad = inner_right(dt_pre_low, w_dt)
    selection_grad = jnp.concatenate([dt_low_grad, in_grad, out_grad_mat], axis=1).astype(bf16)
    grad_w_xproj = inner_left(selection_grad, activation_low.reshape(tokens, inner_width))
    act_grad = (
        y_grad * d_skip
        + adj_in * step_size
        + inner_right(selection_grad, w_xproj).reshape(seq_count, span_len, inner_width)
    )
    pre_grad = act_grad * silu_slope(pre_conv)
    grad_conv_bias = jnp.sum(pre_grad, axis=(0, 1))
    grad_conv_weight = jnp.stack(
        [
            jnp.sum(pre_grad * padded[:, offset : offset + span_len], axis=(0, 1))
            for offset in range(conv_taps)
        ]
    )
    padded_grad = jnp.zeros(padded.shape, f32)
    for offset in range(conv_taps):
        padded_grad = padded_grad.at[:, offset : offset + span_len].add(
            conv_weight[offset] * pre_grad
        )
    rim_back = shifted(padded_grad[:, : conv_taps - 1].astype(bf16), "expert", -1).astype(f32)
    filler = jnp.zeros((seq_count, span_len - conv_taps + 1, inner_width), f32)
    conv_in_grad = padded_grad[:, conv_taps - 1 :] + jnp.concatenate([filler, rim_back], axis=1)
    conv_grad_low = conv_in_grad.astype(bf16).reshape(tokens, inner_width)
    grad_w_in_c = inner_left(normed_flat, conv_grad_low)
    normed_grad = inner_right(jnp.concatenate([conv_grad_low, z_grad_low], axis=1), w_in)
    norm_one_grad, grad_gain_one = rms_backward(
        stream, norm1_gain, inv_one, normed_grad.reshape(layer_input.shape)
    )
    grad_input = stream_two_grad + norm_one_grad

    small = [
        grad_w_xproj,
        grad_w_dt,
        grad_a_log,
        grad_conv_weight,
        grad_conv_bias[None],
        grad_dt_bias[None],
        grad_d_skip[None],
        jnp.concatenate([grad_gain_one, grad_gain_two]).reshape(-1, inner_width),
        grad_w_router.reshape(-1, inner_width),
    ]
    heights = [piece.shape[0] for piece in small]
    lift = groups * holders
    extra = -sum(heights) % lift
    total_w_in_c = summed_rows(grad_w_in_c)
    pack = summed_rows(jnp.concatenate(small + [jnp.zeros((extra, inner_width), f32)], axis=0))
    pieces, place = ([], 0)
    for height in heights:
        pieces.append(pack[place : place + height].astype(f32))
        place += height

    kept_count = jnp.sum(choose * kept_float[:, None], axis=0)
    total_count = jnp.sum(choose, axis=0)
    loads = lax.psum(jnp.stack([kept_count, total_count - kept_count]), ("dp", "expert"))
    expert_loads = loads * (experts_all / (tokens * groups * holders))
    return (
        result,
        grad_input,
        pieces[7].reshape(-1)[:model_width],
        jnp.concatenate([total_w_in_c, total_w_in_z], axis=1).astype(f32),
        pieces[3],
        pieces[4][0],
        pieces[0].T,
        pieces[1],
        pieces[5][0],
        pieces[2].T,
        pieces[6][0],
        total_w_out.astype(f32),
        pieces[7].reshape(-1)[model_width:],
        pieces[8].reshape(model_width, experts_all),
        grad_w_up[None],
        grad_w_down[None],
        expert_loads,
    )


def solution(mesh):
    in_specs = (
        P("dp", "expert", None),
        P(),
        P(),
        P(),
        P(),
        P(),
        P(),
        P(),
        P(),
        P(),
        P(),
        P(),
        P(),
        P("expert", None, "dp"),
        P("expert", "dp", None),
        P("dp", "expert"),
        P(),
        P("dp", "expert", None),
    )
    out_specs = (
        P("dp", "expert", None),
        P("dp", "expert", None),
        P(),
        P(),
        P(),
        P(),
        P(),
        P(),
        P(),
        P(),
        P(),
        P(),
        P(),
        P(),
        P("expert", None, "dp"),
        P("expert", "dp", None),
        P(),
    )
    return jax.shard_map(body, mesh=mesh, in_specs=in_specs, out_specs=out_specs, check_vma=False)
```

```python
import jax
import jax.numpy as jnp
from jax import lax
from jax.experimental import pallas as pl
from jax.experimental.pallas import tpu as pltpu
from jax.sharding import PartitionSpec as P

f32 = jnp.float32
bf16 = jnp.bfloat16
LN = 128
SUB = 16
GROUP = 4
BG = 2
EPSILON = 1e-05
LOG2E = 1.4426950408889634
NT = (((1,), (1,)), ((), ()))
TN = (((0,), (0,)), ((), ()))
VM = pl.BlockSpec(memory_space=pltpu.VMEM)
SM = pl.BlockSpec(memory_space=pltpu.SMEM)


def params(mib=56):
    return pltpu.CompilerParams(vmem_limit_bytes=mib << 20)


def shape_of(shape, dtype):
    return jax.ShapeDtypeStruct(shape, dtype)


def dot(left, right):
    return jnp.dot(left, right, preferred_element_type=f32)


def dot_nt(left, right):
    return lax.dot_general(left, right, NT, preferred_element_type=f32)


def dot_tn(left, right):
    return lax.dot_general(left, right, TN, preferred_element_type=f32)


def spread_lanes(table, out_ref):
    ns, span = table.shape
    for t in range(span):
        out_ref[t] = jnp.broadcast_to(table[:, t : t + 1], (ns, LN))


def row_of(block, i, ns):
    return jnp.broadcast_to(block[i : i + 1], (ns, LN))


def tile_of(ref, seq, t0, j):
    return ref[seq, pl.ds(pl.multiple_of(t0, SUB), SUB), j * LN : (j + 1) * LN].astype(f32)


def tile_groups(tiles, size):
    return [range(g, min(g + size, tiles)) for g in range(0, tiles, size)]


def block_diagonal(part):
    ns = part.shape[1]
    lane = lax.broadcasted_iota(jnp.int32, (ns, SUB * ns), 1)
    copy = ((lane & (ns - 1)) == lax.broadcasted_iota(jnp.int32, (ns, SUB * ns), 0)).astype(bf16)
    high = part.astype(bf16)
    low = (part - high.astype(f32)).astype(bf16)
    block = lax.broadcasted_iota(jnp.int32, (SUB, SUB * ns), 1) // ns
    own = block == lax.broadcasted_iota(jnp.int32, (SUB, SUB * ns), 0)
    pieces = [jnp.where(own, dot(half, copy), 0.0) for half in (high, low)]
    return jnp.concatenate(pieces, axis=0).astype(bf16)


def silu_slope(values):
    logistic = jax.nn.sigmoid(values)
    return logistic * (1.0 + values * (1.0 - logistic))


def inverse_rms(values):
    return lax.rsqrt(jnp.mean(values * values, axis=-1, keepdims=True) + EPSILON)


def norm_backward(values, gain_vec, inv_rms, upstream):
    normal = values * inv_rms
    weighted = upstream * gain_vec
    mean = jnp.mean(weighted * normal, axis=-1, keepdims=True)
    return (
        inv_rms * (weighted - normal * mean),
        jnp.sum(upstream * normal, axis=0, keepdims=True),
    )


def route(expert_route, capacity, og, slot_count):
    s, t = expert_route.shape
    experts = capacity.shape[0]
    d = og.shape[2]
    tokens = s * t
    slots = experts * slot_count
    wide = -(-2 * experts // LN) * LN

    def kernel(cap_ref, route_ref, og_ref, pick_ref, placed_ref, choose_ref, count_ref):
        flat = jnp.concatenate([route_ref[k : k + 1] for k in range(s)], axis=1)
        rows = lax.broadcasted_iota(jnp.int32, (LN, tokens), 0)
        choose = (rows == flat).astype(f32)
        earlier = lax.broadcasted_iota(jnp.int32, (tokens, tokens), 0)
        earlier = earlier < lax.broadcasted_iota(jnp.int32, (tokens, tokens), 1)
        rank = dot(choose.astype(bf16), earlier.astype(bf16))
        rank = jnp.sum(rank * choose, axis=0, keepdims=True).astype(jnp.int32)
        limit = jnp.zeros((1, tokens), jnp.int32)
        for e in range(experts):
            limit = jnp.where(flat == e, cap_ref[e], limit)
        kept = rank < limit
        target = jnp.where(kept, flat * slot_count + rank, slots)
        pick = lax.broadcasted_iota(jnp.int32, (slots, tokens), 0) == target
        pick = pick.astype(f32).astype(bf16)
        pick_ref[...] = pick
        every = jnp.concatenate([og_ref[k] for k in range(s)], axis=0)
        placed_ref[...] = dot(pick, every).astype(bf16)
        choose_ref[...] = choose.T[:, :experts]
        kept = kept.astype(f32)
        low = choose[:experts].astype(bf16)
        lines = [dot_nt(v.astype(bf16), low) for v in (kept, 1.0 - kept)]
        lines.append(jnp.zeros((1, wide - 2 * experts), f32))
        count_ref[...] = jnp.concatenate(lines, axis=1)

    return pl.pallas_call(
        kernel,
        out_shape=(
            shape_of((slots, tokens), bf16),
            shape_of((slots, d), bf16),
            shape_of((tokens, experts), f32),
            shape_of((1, wide), f32),
        ),
        in_specs=[SM, VM, VM],
        out_specs=(VM,) * 4,
        compiler_params=params(),
    )(capacity, expert_route, og)


def front_kernel(
    x_ref, rim_ref, gain_ref, win_ref, cw_ref, cb_ref, wxt_ref, wdt_ref, dtb_ref, alog_ref, count_ref,
    normed_ref, conv_ref, gate_ref, pre_ref, act_ref, sel_ref, selt_ref, dtp_ref, step_ref,
    rate_ref, send_ref, bb_ref, cum_ref,
):
    seqs, span, model = x_ref.shape
    width = cw_ref.shape[1]
    taps = cw_ref.shape[0]
    rim = rim_ref.shape[1]
    ns = rate_ref.shape[0]
    rank = wdt_ref.shape[0]
    cols = 512
    gain = gain_ref[...].reshape(1, -1)
    conv_b = cb_ref[...].reshape(1, -1)
    dt_b = dtb_ref[...].reshape(1, -1)
    rate_ref[...] = jnp.exp(alog_ref[...]) * (-LOG2E)
    rows = []
    for ref in (x_ref, rim_ref):
        for seq in range(seqs):
            v = ref[seq].astype(f32)
            rows.append((v * inverse_rms(v) * gain).astype(bf16))
    for seq in range(seqs):
        normed_ref[seq * span : (seq + 1) * span] = rows[seq]
    every = jnp.concatenate(rows, axis=0)
    for c in range(0, width, cols):
        cut = slice(c, c + cols)
        r = dot(every, win_ref[:, cut]).astype(bf16)
        for seq in range(seqs):
            main = r[seq * span : (seq + 1) * span]
            edge = r[seqs * span + seq * rim : seqs * span + (seq + 1) * rim]
            conv_ref[seq, :rim, cut] = edge
            conv_ref[seq, rim:, cut] = main
            v = jnp.concatenate([edge, main], axis=0).astype(f32)
            pre = conv_b[:, cut]
            for k in range(taps):
                first = rim - taps + 1 + k
                pre = pre + cw_ref[k : k + 1, cut] * v[first : first + span]
            pre_ref[seq, :, cut] = pre
            act_ref[seq, :, cut] = (pre * jax.nn.sigmoid(pre)).astype(bf16)
    own = every[: seqs * span]
    for seq in range(seqs):
        sel = dot_nt(act_ref[seq], wxt_ref[...])
        sel_ref[seq] = sel
        lanes = sel.shape[1]
        wide = jnp.concatenate([sel, jnp.zeros((span, -lanes % LN), f32)], axis=1)
        selt = wide.T[:lanes]
        selt_ref[seq] = selt
        low = sel[:, :rank].astype(bf16)
        for c in range(0, width, cols):
            cut = slice(c, c + cols)
            pre = dot(low, wdt_ref[:, cut]) + dt_b[:, cut]
            dtp_ref[seq, :, cut] = pre
            step = jnp.maximum(pre, 0.0) + jnp.log1p(jnp.exp(-jnp.abs(pre)))
            step_ref[seq, :, cut] = step
            cum_ref[seq : seq + 1, cut] = jnp.sum(step, axis=0, keepdims=True)
        spread_lanes(selt[rank : rank + ns], bb_ref)
        tiles = width // LN

        def chunk(k, state):
            t0 = k * SUB
            state = list(state)
            for group in tile_groups(tiles, GROUP):
                dt = {j: tile_of(step_ref, seq, t0, j) for j in group}
                dx = {j: dt[j] * tile_of(act_ref, seq, t0, j) for j in group}
                for i in range(SUB):
                    b = bb_ref[t0 + i]
                    for j in group:
                        rate = rate_ref[:, j * LN : (j + 1) * LN]
                        decay = jnp.exp2(row_of(dt[j], i, ns) * rate)
                        state[j] = decay * state[j] + row_of(dx[j], i, ns) * b
            return tuple(state)

        state = lax.fori_loop(
            0, span // SUB, chunk, tuple(jnp.zeros((ns, LN), f32) for _ in range(tiles))
        )
        for j in range(tiles):
            cut = slice(j * LN, (j + 1) * LN)
            send_ref[seq * ns : (seq + 1) * ns, cut] = state[j].astype(bf16)
    cum = cum_ref[...]
    high = cum.astype(bf16).astype(f32)
    line = jnp.concatenate(
        [count_ref[...], jnp.zeros((1, width - count_ref.shape[1]), f32)], axis=1
    )
    tail = [high, cum - high, line, jnp.zeros((8 - 2 * seqs - 1, width), f32)]
    send_ref[seqs * ns :, :] = jnp.concatenate(tail, axis=0).astype(bf16)
    for c in range(width, 2 * width, cols):
        r = dot(own, win_ref[:, c : c + cols])
        for seq in range(seqs):
            gate_ref[seq, :, c - width : c - width + cols] = r[seq * span : (seq + 1) * span]


def front(x, rim, gain, w_in, conv_w, conv_b, wx_t, w_dt, dt_b, alog_t, counts):
    s, t, d = x.shape
    w = conv_w.shape[1]
    n = alog_t.shape[0]
    k = wx_t.shape[0]
    return pl.pallas_call(
        front_kernel,
        out_shape=(
            shape_of((s * t, d), bf16),
            shape_of((s, rim.shape[1] + t, w), bf16),
            shape_of((s, t, w), f32),
            shape_of((s, t, w), f32),
            shape_of((s, t, w), bf16),
            shape_of((s, t, k), f32),
            shape_of((s, k, t), f32),
            shape_of((s, t, w), f32),
            shape_of((s, t, w), f32),
            shape_of((n, w), f32),
            shape_of((s * n + 8, w), bf16),
        ),
        in_specs=[VM] * 11,
        out_specs=(VM,) * 11,
        scratch_shapes=[pltpu.VMEM((t, n, LN), f32), pltpu.VMEM((s, w), f32)],
        compiler_params=params(),
    )(x, rim, gain, w_in, conv_w, conv_b, wx_t, w_dt, dt_b, alog_t, counts)


def carry_of(every_ref, rate_ref, seq, seqs, place, stop, step):
    ns, width = rate_ref.shape
    count = jnp.maximum((stop - place) * step, 0)

    def join(u, total):
        block = every_ref[place + u * step].astype(f32)
        row = seqs * ns + seq
        cum = block[row : row + 1] + block[row + seqs : row + seqs + 1]
        return jnp.exp2(rate_ref[...] * cum) * total + block[seq * ns : (seq + 1) * ns]

    return lax.fori_loop(0, count, join, jnp.zeros((ns, width), f32))


def middle_kernel(
    mine_ref, every_ref, step_ref, act_ref, sel_ref, selt_ref, rate_ref, skip_ref, gate_ref,
    x_ref, wout_ref, gain_ref, pick_ref, choose_ref, router_ref,
    h_ref, y_ref, gated_ref, two_ref, prob_ref, placed_ref, bb_ref, st_ref, acc_ref,
):
    _, span, width = step_ref.shape
    ns = rate_ref.shape[0]
    rank = sel_ref.shape[2] - 2 * ns
    tiles = width // LN
    seqs = pick_ref.shape[1] // span
    mine = mine_ref[0]
    skip = skip_ref[...].reshape(1, -1)
    for seq in range(seqs):

        @pl.when(pl.program_id(0) == seq)
        def _():
            st_ref[...] = carry_of(every_ref, rate_ref, seq, seqs, 0, mine, 1)

    spread_lanes(selt_ref[0, rank : rank + ns], bb_ref)
    h_ref[0, 0:ns, :] = st_ref[...].astype(bf16)

    def chunk(k, carry):
        t0 = k * SUB
        rows = pl.ds(pl.multiple_of(t0, SUB), SUB)
        for group in tile_groups(tiles, GROUP):
            state = {j: st_ref[:, j * LN : (j + 1) * LN] for j in group}
            dt = {j: tile_of(step_ref, 0, t0, j) for j in group}
            dx = {j: dt[j] * tile_of(act_ref, 0, t0, j) for j in group}
            for i in range(SUB):
                b = bb_ref[t0 + i]
                to = pl.ds(pl.multiple_of((t0 + i + 1) * ns, ns), ns)
                for j in group:
                    cut = slice(j * LN, (j + 1) * LN)
                    decay = jnp.exp2(row_of(dt[j], i, ns) * rate_ref[:, cut])
                    state[j] = decay * state[j] + row_of(dx[j], i, ns) * b
                    h_ref[0, to, cut] = state[j].astype(bf16)
            for j in group:
                st_ref[:, j * LN : (j + 1) * LN] = state[j]
        diag = block_diagonal(sel_ref[0, rows, rank + ns :])
        r = dot(diag, h_ref[0, pl.ds(pl.multiple_of((t0 + 1) * ns, ns), SUB * ns), :])
        y_ref[0, rows, :] = r[:SUB] + r[SUB:] + skip * act_ref[0, rows, :].astype(f32)
        return carry

    lax.fori_loop(0, span // SUB, chunk, 0)
    gate = gate_ref[0]
    gated = (y_ref[0] * (gate * jax.nn.sigmoid(gate))).astype(bf16)
    gated_ref[0] = gated
    two = x_ref[0].astype(f32) + dot(gated, wout_ref[...])
    two_ref[0] = two
    moe = (two * inverse_rms(two) * gain_ref[...].reshape(1, -1)).astype(bf16)
    logits = dot_nt(moe, router_ref[...])
    raised = jnp.exp(logits - jnp.max(logits, axis=1, keepdims=True))
    chosen = jnp.sum(raised * choose_ref[...], axis=1, keepdims=True)
    prob_ref[0] = chosen / jnp.sum(raised, axis=1, keepdims=True)
    for seq in range(seqs):

        @pl.when(pl.program_id(0) == seq)
        def _():
            part = dot(pick_ref[:, seq * span : (seq + 1) * span], moe)
            if seq:
                part = part + acc_ref[...]
            if seq < seqs - 1:
                acc_ref[...] = part
            else:
                placed_ref[...] = part.astype(bf16)


def by_sequence(*shape):
    return pl.BlockSpec((1,) + shape, lambda i: (i,) + (0,) * len(shape))


def whole(*shape):
    return pl.BlockSpec(shape, lambda i: (0,) * len(shape))


def middle(
    mine, every, step, act, sel, selt, rate2, skip, gate, x, w_out, gain, pick, choose, router_t
):
    s, t, w = step.shape
    n = rate2.shape[0]
    d = x.shape[2]
    k = sel.shape[2]
    return pl.pallas_call(
        middle_kernel,
        grid=(s,),
        out_shape=(
            shape_of((s, (t + 1) * n, w), bf16),
            shape_of((s, t, w), f32),
            shape_of((s, t, w), bf16),
            shape_of((s, t, d), f32),
            shape_of((s, t, 1), f32),
            shape_of((pick.shape[0], d), bf16),
        ),
        in_specs=[
            SM,
            whole(*every.shape),
            by_sequence(t, w),
            by_sequence(t, w),
            by_sequence(t, k),
            by_sequence(k, t),
            whole(n, w),
            whole(w),
            by_sequence(t, w),
            by_sequence(t, d),
            whole(w, d),
            whole(d),
            whole(*pick.shape),
            pl.BlockSpec((t, choose.shape[1]), lambda i: (i, 0)),
            whole(*router_t.shape),
        ],
        out_specs=(
            by_sequence((t + 1) * n, w),
            by_sequence(t, w),
            by_sequence(t, w),
            by_sequence(t, d),
            by_sequence(t, 1),
            whole(pick.shape[0], d),
        ),
        scratch_shapes=[
            pltpu.VMEM((t, n, LN), f32),
            pltpu.VMEM((n, w), f32),
            pltpu.VMEM((pick.shape[0], d), f32),
        ],
        compiler_params=params(),
    )(mine, every, step, act, sel, selt, rate2, skip, gate, x, w_out, gain, pick, choose, router_t)


def gelu_pair(v):
    root = 0.7978845608028654
    square = v * v
    bend = jnp.tanh(root * (v + 0.044715 * v * square))
    half = 0.5 * (1.0 + bend)
    slope = half + 0.5 * v * (1.0 - bend * bend) * (root * (1.0 + 3.0 * 0.044715 * square))
    return v * half, slope


def expert_kernel(shares, own_ref, rows_ref, og_ref, router_ref, *refs):
    ups, downs, refs = (refs[:shares], refs[shares : 2 * shares], refs[2 * shares :])
    fwd_ref, bwd_ref, grd_ref, log_ref = refs[:4]
    hids, pres = (refs[4 : 4 + shares], refs[4 + shares :])
    rows = rows_ref[...]
    logits = dot_nt(rows, router_ref[...])
    top = jnp.max(logits, axis=1, keepdims=True)
    raised = jnp.exp(logits - top)
    probs = raised / jnp.sum(raised, axis=1, keepdims=True)
    own = (lax.broadcasted_iota(jnp.int32, (1, probs.shape[1]), 1) == own_ref[0]).astype(f32)
    gate = jnp.sum(probs * own, axis=1, keepdims=True)
    og = og_ref[...].astype(f32)
    grads = (og * gate).astype(bf16)
    grd_ref[...] = grads
    fwd, bwd = (0.0, 0.0)
    for up_ref, down_ref, hid_ref, pre_ref in zip(ups, downs, hids, pres):
        hidden, slope = gelu_pair(dot(rows, up_ref[...]))
        hidden = hidden.astype(bf16)
        hid_ref[...] = hidden
        fwd = fwd + dot(hidden, down_ref[...])
        pre = (dot_nt(grads, down_ref[...]) * slope).astype(bf16)
        pre_ref[...] = pre
        bwd = bwd + dot_nt(pre, up_ref[...])
    logit = jnp.sum(og * fwd, axis=1, keepdims=True) * gate * (own - probs)
    log_ref[...] = logit
    high = logit.astype(bf16)
    low = (logit - high.astype(f32)).astype(bf16)
    bwd = bwd + dot(high, router_ref[...]) + dot(low, router_ref[...])
    fwd_ref[...] = fwd.astype(fwd_ref.dtype)
    bwd_ref[...] = bwd.astype(bwd_ref.dtype)


def expert_rows(own, rows, og, router, ups, downs, dtype):
    m, d = rows.shape
    f = ups[0].shape[1]
    shares = len(ups)

    def kernel(*refs):
        expert_kernel(shares, *refs)

    outs = pl.pallas_call(
        kernel,
        out_shape=(
            shape_of((m, d), dtype),
            shape_of((m, d), dtype),
            shape_of((m, d), bf16),
            shape_of((m, router.shape[0]), f32),
        )
        + (shape_of((m, f), bf16),) * (2 * shares),
        in_specs=[SM] + [VM] * (3 + 2 * shares),
        out_specs=(VM,) * (4 + 2 * shares),
        compiler_params=params(),
    )(own, rows, og, router, *ups, *downs)
    return (*outs[:4], outs[4 : 4 + shares], outs[4 + shares :])


def back(got, pick, two, gain, og, w_out, gate, y, act):
    s, t, w = y.shape
    d = two.shape[2]

    def kernel(
        got_ref, pick_ref, two_ref, gain_ref, og_ref, wout_ref, gate_ref, y_ref, act_ref,
        twog_ref, mix_ref, gain2_ref, yg_ref, zg_ref, skipg_ref,
    ):
        cols = 512
        moe_grad = dot_tn(pick_ref[...], got_ref[...])
        gain = gain_ref[...].reshape(1, -1)
        total = 0.0
        for seq in range(s):
            v = two_ref[seq]
            grad, gained = norm_backward(
                v, gain, inverse_rms(v), moe_grad[seq * t : (seq + 1) * t]
            )
            total = total + gained
            grad = grad + og_ref[seq].astype(f32)
            twog_ref[seq] = grad
            mix_ref[seq * t : (seq + 1) * t] = grad.astype(bf16)
        gain2_ref[...] = total
        for c in range(0, w, cols):
            cut = slice(c, c + cols)
            r = dot_nt(mix_ref[...], wout_ref[cut, :])
            total = 0.0
            for seq in range(s):
                part = r[seq * t : (seq + 1) * t]
                gate = gate_ref[seq, :, cut]
                logistic = jax.nn.sigmoid(gate)
                yg = part * (gate * logistic)
                yg_ref[seq, :, cut] = yg
                slope = logistic * (1.0 + gate * (1.0 - logistic))
                zg_ref[seq, :, cut] = (part * y_ref[seq, :, cut] * slope).astype(bf16)
                total = total + jnp.sum(yg * act_ref[seq, :, cut].astype(f32), axis=0, keepdims=True)
            skipg_ref[:, cut] = total

    return pl.pallas_call(
        kernel,
        out_shape=(
            shape_of((s, t, d), f32),
            shape_of((s * t, d), bf16),
            shape_of((1, d), f32),
            shape_of((s, t, w), f32),
            shape_of((s, t, w), bf16),
            shape_of((1, w), f32),
        ),
        in_specs=[VM] * 9,
        out_specs=(VM,) * 6,
        compiler_params=params(),
    )(got, pick, two, gain, og, w_out, gate, y, act)


def head_of(yg, step, selt, rate2):
    s, t, w = step.shape
    n = rate2.shape[0]
    tiles = w // LN

    def kernel(yg_ref, step_ref, selt_ref, rate_ref, head_ref, cb_ref):
        for seq in range(s):
            spread_lanes(selt_ref[seq, selt.shape[1] - n :], cb_ref)

            def chunk(u, mu):
                t0 = t - SUB - u * SUB
                mu = list(mu)
                for group in tile_groups(tiles, GROUP):
                    dt = {j: tile_of(step_ref, seq, t0, j) for j in group}
                    yg = {j: tile_of(yg_ref, seq, t0, j) for j in group}
                    for i in reversed(range(SUB)):
                        c = cb_ref[t0 + i]
                        for j in group:
                            rate = rate_ref[:, j * LN : (j + 1) * LN]
                            decay = jnp.exp2(row_of(dt[j], i, n) * rate)
                            mu[j] = decay * (mu[j] + row_of(yg[j], i, n) * c)
                return tuple(mu)

            mu = lax.fori_loop(
                0, t // SUB, chunk, tuple(jnp.zeros((n, LN), f32) for _ in range(tiles))
            )
            for j in range(tiles):
                cut = slice(j * LN, (j + 1) * LN)
                head_ref[seq * n : (seq + 1) * n, cut] = mu[j].astype(bf16)

    return pl.pallas_call(
        kernel,
        out_shape=shape_of((s * n, w), bf16),
        in_specs=[VM] * 4,
        out_specs=VM,
        scratch_shapes=[pltpu.VMEM((t, n, LN), f32)],
        compiler_params=params(),
    )(yg, step, selt, rate2)


def scan_back_kernel(
    taps, mine_ref, heads_ref, every_ref, step_ref, act_ref, yg_ref, sel_ref, selt_ref, rate_ref, h_ref,
    dtp_ref, wdt_ref, wxt_ref, skip_ref, pre_ref, conv_ref,
    preg_ref, small_ref, cb_ref, mu_ref, al_ref, lam_ref, rdg_ref, s1_ref, adj_ref, ig_ref, og_ref,
):
    _, span, width = step_ref.shape
    ns = rate_ref.shape[0]
    lanes = sel_ref.shape[2]
    rank = lanes - 2 * ns
    tiles = width // LN
    chunks = span // SUB
    holders = heads_ref.shape[0]
    seqs = heads_ref.shape[1] // ns
    rim = conv_ref.shape[1] - span
    mine = mine_ref[0]
    for seq in range(seqs):

        @pl.when(pl.program_id(0) == seq)
        def _():
            count = holders - 1 - mine

            def join(u, total):
                place = holders - 1 - u
                row = seqs * ns + seq
                tail = every_ref[place, seqs * ns :, :].astype(f32)
                cum = tail[seq : seq + 1] + tail[seqs + seq : seqs + seq + 1]
                head = heads_ref[place, seq * ns : (seq + 1) * ns, :].astype(f32)
                return jnp.exp2(rate_ref[...] * cum) * total + head

            mu_ref[...] = lax.fori_loop(0, count, join, jnp.zeros((ns, width), f32))

    @pl.when(pl.program_id(0) == 0)
    def _():
        small_ref[...] = jnp.zeros(small_ref.shape, f32)

    spread_lanes(selt_ref[0, rank + ns :], cb_ref)
    al_ref[...] = jnp.zeros((ns, width), f32)
    block = lax.broadcasted_iota(jnp.int32, (SUB, SUB * ns), 1) // ns
    ones = (block == lax.broadcasted_iota(jnp.int32, (SUB, SUB * ns), 0)).astype(bf16)

    def chunk(v, carry):
        k = chunks - 1 - v
        t0 = k * SUB
        rows = pl.ds(pl.multiple_of(t0, SUB), SUB)
        for group in tile_groups(tiles, BG):
            cuts = {j: slice(j * LN, (j + 1) * LN) for j in group}
            mu = {j: mu_ref[:, cuts[j]] for j in group}
            al = {j: al_ref[:, cuts[j]] for j in group}
            dts = {j: tile_of(step_ref, 0, t0, j) for j in group}
            ygs = {j: tile_of(yg_ref, 0, t0, j) for j in group}
            for i in reversed(range(SUB)):
                t = t0 + i
                c = cb_ref[t]
                at = pl.ds(pl.multiple_of(t * ns, ns), ns)
                for j in group:
                    rate = rate_ref[:, cuts[j]]
                    dt = row_of(dts[j], i, ns)
                    decay = jnp.exp2(dt * rate)
                    lam = mu[j] + row_of(ygs[j], i, ns) * c
                    mu[j] = decay * lam
                    dg = mu[j] * h_ref[0, at, cuts[j]].astype(f32)
                    al[j] = al[j] + dt * dg
                    lam_ref[i * ns : (i + 1) * ns, cuts[j]] = lam.astype(bf16)
                    rdg_ref[i * ns : (i + 1) * ns, cuts[j]] = (rate * dg).astype(bf16)
            for j in group:
                mu_ref[:, cuts[j]] = mu[j]
                al_ref[:, cuts[j]] = al[j]
        lam = lam_ref[...]
        r = dot(block_diagonal(sel_ref[0, rows, rank : rank + ns]), lam)
        adj_ref[rows, :] = r[:SUB] + r[SUB:]
        s1_ref[rows, :] = dot(ones, rdg_ref[...]) * (1.0 / LOG2E)
        up = lax.broadcasted_iota(jnp.int32, (SUB * ns, SUB), 0) // ns
        own = up == lax.broadcasted_iota(jnp.int32, (SUB * ns, SUB), 1)
        dx = (step_ref[0, rows, :] * act_ref[0, rows, :].astype(f32)).astype(bf16)
        d = dot_nt(lam, dx)
        ig_ref[k] = jnp.sum(jnp.where(own, d, 0.0).reshape(SUB, ns, SUB), axis=0)
        states = h_ref[0, pl.ds(pl.multiple_of((t0 + 1) * ns, ns), SUB * ns), :]
        d = dot_nt(states, yg_ref[0, rows, :].astype(bf16))
        og_ref[k] = jnp.sum(jnp.where(own, d, 0.0).reshape(SUB, ns, SUB), axis=0)
        return carry

    lax.fori_loop(0, chunks, chunk, 0)
    act = act_ref[0].astype(f32)
    adj = adj_ref[...]
    step = step_ref[0]
    dtg = (s1_ref[...] + adj * act) * jax.nn.sigmoid(dtp_ref[0])
    low = dtg.astype(bf16)
    grads = [dot_nt(wdt_ref[...], low)] + [
        jnp.concatenate([ref[k] for k in range(chunks)], axis=1) for ref in (ig_ref, og_ref)
    ]
    grads = jnp.concatenate(grads, axis=0).astype(bf16)
    at = 0

    def put(rows):
        nonlocal at
        cut = slice(at, at + rows.shape[0])
        small_ref[cut, :] = small_ref[cut, :] + rows
        at += rows.shape[0]

    put(dot(grads, act_ref[0]))
    put(dot(selt_ref[0, :rank].astype(bf16), low))
    put(rate_ref[...] * al_ref[...] * (1.0 / LOG2E))
    act_grad = yg_ref[0] * skip_ref[...].reshape(1, -1) + adj * step + dot_tn(grads, wxt_ref[...])
    pre_grad = act_grad * silu_slope(pre_ref[0])
    preg_ref[0] = pre_grad
    inputs = conv_ref[0].astype(f32)
    tail = []
    for k in range(taps):
        first = rim - taps + 1 + k
        tail.append(jnp.sum(pre_grad * inputs[first : first + span], axis=0, keepdims=True))
    tail.append(jnp.sum(pre_grad, axis=0, keepdims=True))
    tail.append(jnp.sum(dtg, axis=0, keepdims=True))
    tail.append(jnp.zeros((8 - len(tail), width), f32))
    put(jnp.concatenate(tail, axis=0))


def scan_back(
    taps, mine, heads, every, step, act, yg, sel, selt, rate2, h, dtp, w_dt, wx_t, skip, pre, conv
):
    s, t, w = step.shape
    n = rate2.shape[0]
    k = sel.shape[2]
    chunks = t // SUB
    small = k + w_dt.shape[0] + n + 8

    def kernel(*refs):
        scan_back_kernel(taps, *refs)

    return pl.pallas_call(
        kernel,
        grid=(s,),
        out_shape=(shape_of((s, t, w), f32), shape_of((small, w), f32)),
        in_specs=[
            SM,
            whole(*heads.shape),
            whole(*every.shape),
            by_sequence(t, w),
            by_sequence(t, w),
            by_sequence(t, w),
            by_sequence(t, k),
            by_sequence(k, t),
            whole(n, w),
            by_sequence((t + 1) * n, w),
            by_sequence(t, w),
            whole(*w_dt.shape),
            whole(*wx_t.shape),
            whole(w),
            by_sequence(t, w),
            by_sequence(conv.shape[1], w),
        ],
        out_specs=(by_sequence(t, w), whole(small, w)),
        scratch_shapes=[
            pltpu.VMEM((t, n, LN), f32),
            pltpu.VMEM((n, w), f32),
            pltpu.VMEM((n, w), f32),
            pltpu.VMEM((SUB * n, w), bf16),
            pltpu.VMEM((SUB * n, w), bf16),
            pltpu.VMEM((t, w), f32),
            pltpu.VMEM((t, w), f32),
            pltpu.VMEM((chunks, n, SUB), f32),
            pltpu.VMEM((chunks, n, SUB), f32),
        ],
        compiler_params=params(60),
    )(mine, heads, every, step, act, yg, sel, selt, rate2, h, dtp, w_dt, wx_t, skip, pre, conv)


def expert_grads(rows, grds, logs, hids, pres):
    blocks = len(rows)
    shares = len(hids[0])
    d = rows[0].shape[1]
    f = hids[0][0].shape[1]
    flat = [*rows, *grds, *logs] + [v for group in (hids, pres) for block in group for v in block]

    def kernel(*refs):
        ins, outs = (refs[: len(flat)], refs[len(flat) :])
        row, grd, log = (ins[k * blocks : (k + 1) * blocks] for k in range(3))
        hid = ins[3 * blocks : (3 + shares) * blocks]
        pre = ins[(3 + shares) * blocks :]

        def total(lefts, rights):
            parts = [dot_tn(left[...], right[...]) for left, right in zip(lefts, rights)]
            return sum(parts[1:], parts[0])

        for k in range(shares):
            up_ref, down_ref = outs[2 * k : 2 * k + 2]
            up_ref[...] = total(row, pre[k::shares]).astype(up_ref.dtype)
            down_ref[...] = total(hid[k::shares], grd).astype(down_ref.dtype)
        router = 0.0
        for log_ref, row_ref in zip(log, row):
            high = log_ref[...].astype(bf16)
            low = (log_ref[...] - high.astype(f32)).astype(bf16)
            router = router + dot_tn(high, row_ref[...]) + dot_tn(low, row_ref[...])
        outs[-1][...] = router

    kinds = [f32] + [bf16] * (shares - 1)
    outs = []
    for kind in kinds:
        outs += [shape_of((d, f), kind), shape_of((f, d), kind)]
    outs.append(shape_of((logs[0].shape[1], d), f32))
    got = pl.pallas_call(
        kernel,
        out_shape=tuple(outs),
        in_specs=[VM] * len(flat),
        out_specs=(VM,) * len(outs),
        compiler_params=params(),
    )(*flat)
    return got[0:-1:2], got[1:-1:2], got[-1]


def deal(block_ref, keep_ref, send_ref, core, first, rows):
    for pair in range(keep_ref.shape[0]):
        for ref, side in ((keep_ref, core), (send_ref, 1 - core)):
            at = pl.ds(pl.multiple_of((2 * pair + side) * rows, rows), rows)
            ref[pair, first : first + rows, :] = block_ref[at, :]


def early_pack(core, mix, gated, normed, zg, holders):
    d = mix.shape[1]
    w = gated.shape[1]
    out_rows, in_rows, pieces = (w // holders, d // holders, w // d)

    def kernel(core_ref, mix_ref, gated_ref, normed_ref, zg_ref, keep_ref, send_ref, block_ref):
        block_ref[...] = dot_tn(gated_ref[...], mix_ref[...]).astype(bf16)
        deal(block_ref, keep_ref, send_ref, core_ref[0], 0, out_rows)
        for p in range(pieces):
            r = dot_tn(normed_ref[...], zg_ref[:, p * d : (p + 1) * d])
            block_ref[p * d : (p + 1) * d] = r.astype(bf16)
            side = block_ref.at[p * d : (p + 1) * d]
            deal(side, keep_ref, send_ref, core_ref[0], out_rows + p * in_rows, in_rows)

    shape = shape_of((holders // 2, out_rows + pieces * in_rows, d), bf16)
    return pl.pallas_call(
        kernel,
        out_shape=(shape, shape),
        in_specs=[SM] + [VM] * 4,
        out_specs=(VM, VM),
        scratch_shapes=[pltpu.VMEM((w, d), bf16)],
        compiler_params=params(),
    )(core, mix, gated, normed, zg)


def finish(
    core, preg, rim, conv_w, zg, w_in, x, gain, normed, twog, small, skipg, gain2, router, plan
):
    s, t, w = preg.shape
    d = x.shape[2]
    holders, srows = plan
    taps = conv_w.shape[0]
    pieces, in_rows = (w // d, d // holders)
    reach = rim.shape[1]

    def kernel(
        core_ref, preg_ref, rim_ref, cw_ref, zg_ref, win_ref, x_ref, gain_ref, normed_ref, twog_ref,
        small_ref, skip_ref, gain2_ref, router_ref,
        keep_ref, send_ref, input_ref, cg_ref, pack_ref, block_ref,
    ):
        cols = 512
        gain = gain_ref[...].reshape(1, -1)
        for seq in range(s):
            for c in range(0, w, cols):
                cut = slice(c, c + cols)
                v = jnp.concatenate(
                    [preg_ref[seq, :, cut], rim_ref[seq, :, cut].astype(f32)], axis=0
                )
                total = cw_ref[taps - 1 : taps, cut] * v[:t]
                for k in range(1, taps):
                    total = total + cw_ref[taps - 1 - k : taps - k, cut] * v[k : k + t]
                cg_ref[seq * t : (seq + 1) * t, cut] = total.astype(bf16)
        for p in range(pieces):
            block_ref[:d] = dot_tn(normed_ref[...], cg_ref[:, p * d : (p + 1) * d]).astype(bf16)
            deal(block_ref, keep_ref, send_ref, core_ref[0], p * in_rows, in_rows)
        gain1 = 0.0
        for seq in range(s):
            grad = dot_nt(cg_ref[seq * t : (seq + 1) * t], win_ref[:, :w])
            grad = grad + dot_nt(zg_ref[seq], win_ref[:, w:])
            v = x_ref[seq].astype(f32)
            grad, gained = norm_backward(v, gain, inverse_rms(v), grad)
            gain1 = gain1 + gained
            input_ref[seq] = twog_ref[seq] + grad
        pack_ref[...] = jnp.zeros(pack_ref.shape, f32)
        at = 0
        for p in range(pieces):
            pack_ref[at : at + small_ref.shape[0]] = small_ref[:, p * d : (p + 1) * d]
            at += small_ref.shape[0]
        lines = [skip_ref[:, p * d : (p + 1) * d] for p in range(pieces)] + [gain1, gain2_ref[...]]
        for line in lines:
            pack_ref[at : at + 1] = line
            at += 1
        at += -at % 8
        pack_ref[at : at + router_ref.shape[0]] = router_ref[...]
        block_ref[: holders * srows] = pack_ref[...].astype(bf16)
        deal(block_ref, keep_ref, send_ref, core_ref[0], pieces * in_rows, srows)

    return pl.pallas_call(
        kernel,
        out_shape=(
            shape_of((holders // 2, pieces * in_rows + srows, d), bf16),
            shape_of((holders // 2, pieces * in_rows + srows, d), bf16),
            shape_of((s, t, d), f32),
        ),
        in_specs=[SM] + [VM] * 13,
        out_specs=(VM,) * 3,
        scratch_shapes=[
            pltpu.VMEM((s * t, w), bf16),
            pltpu.VMEM((holders * srows, d), f32),
            pltpu.VMEM((max(d, holders * srows), d), bf16),
        ],
        compiler_params=params(),
    )(core, preg, rim, conv_w, zg, w_in, x, gain, normed, twog, small, skipg, gain2, router)


def unpack_early(core, mine, other, width_in):
    pairs, rows, d = mine.shape
    holders = 2 * pairs
    w = width_in // 2
    out_rows, in_rows, pieces = (w // holders, d // holders, w // d)

    def kernel(core_ref, mine_ref, other_ref, win_ref, wout_ref):
        def write(ref):
            wout_ref[...] = ref[0, :out_rows].astype(f32)
            for p in range(pieces):
                first = out_rows + p * in_rows
                win_ref[:, p * d : (p + 1) * d] = ref[0, first : first + in_rows].astype(f32)

        for side, ref in enumerate((mine_ref, other_ref)):

            @pl.when(pl.program_id(1) == side)
            def _():
                write(ref)

    def here(i, j, c):
        return (i, 0, 0)

    def there(i, j, c):
        return 2 * i + jnp.bitwise_xor(c[0], j)

    return pl.pallas_call(
        kernel,
        out_shape=(shape_of((d, width_in), f32), shape_of((w, d), f32)),
        grid_spec=pltpu.PrefetchScalarGridSpec(
            num_scalar_prefetch=1,
            grid=(pairs, 2),
            in_specs=[pl.BlockSpec((1, rows, d), here)] * 2,
            out_specs=(
                pl.BlockSpec((in_rows, w), lambda i, j, c: (there(i, j, c), 1)),
                pl.BlockSpec((out_rows, d), lambda i, j, c: (there(i, j, c), 0)),
            ),
        ),
        compiler_params=params(),
    )(core, mine, other)


def unpack_late(core, mine, other, wide):
    pairs, rows, d = mine.shape
    holders = 2 * pairs
    w = wide.shape[1] // 2
    in_rows, pieces = (d // holders, w // d)
    srows = rows - pieces * in_rows

    def kernel(core_ref, mine_ref, other_ref, wide_ref, win_ref, small_ref):
        def write(ref):
            for p in range(pieces):
                part = ref[0, p * in_rows : (p + 1) * in_rows]
                win_ref[:, p * d : (p + 1) * d] = part.astype(f32)
            small_ref[...] = ref[0, pieces * in_rows :].astype(f32)

        for side, ref in enumerate((mine_ref, other_ref)):

            @pl.when(pl.program_id(1) == side)
            def _():
                write(ref)

    def here(i, j, c):
        return (i, 0, 0)

    def there(i, j, c):
        return (2 * i + jnp.bitwise_xor(c[0], j), 0)

    return pl.pallas_call(
        kernel,
        out_shape=(shape_of(wide.shape, f32), shape_of((holders * srows, d), f32)),
        grid_spec=pltpu.PrefetchScalarGridSpec(
            num_scalar_prefetch=1,
            grid=(pairs, 2),
            in_specs=[pl.BlockSpec((1, rows, d), here)] * 2 + [pl.BlockSpec(memory_space=pl.ANY)],
            out_specs=(pl.BlockSpec((in_rows, w), there), pl.BlockSpec((srows, d), there)),
        ),
        input_output_aliases={3: 0},
        compiler_params=params(),
    )(core, mine, other, wide)


def unpack_small(pack, heights, w, experts):
    d = pack.shape[1]
    pieces = w // d
    k, rank, n, taps = heights
    tall = k + rank + n + 8

    def kernel(pack_ref, wx_ref, wdt_ref, alog_ref, cw_ref, *refs):
        vectors, (gain1_ref, gain2_ref, router_ref) = (refs[:3], refs[3:])
        wide = [pack_ref[p * tall : (p + 1) * tall] for p in range(pieces)]
        wide = jnp.concatenate(wide, axis=1)
        at = 0
        for ref in (wx_ref, wdt_ref, alog_ref):
            ref[...] = wide[at : at + ref.shape[0]]
            at += ref.shape[0]
        tail = wide[at:]
        cw_ref[...] = tail[:taps]
        at = pieces * tall
        vectors[0][...] = tail[taps]
        vectors[1][...] = tail[taps + 1]
        skips = pack_ref[at : at + 8]
        vectors[2][...] = jnp.concatenate([skips[p : p + 1] for p in range(pieces)], axis=1)[0]
        gain1_ref[...] = skips[pieces]
        gain2_ref[...] = skips[pieces + 1]
        router_ref[...] = pack_ref[at + 8 : at + 8 + experts]

    return pl.pallas_call(
        kernel,
        out_shape=(
            shape_of((k, w), f32),
            shape_of((rank, w), f32),
            shape_of((n, w), f32),
            shape_of((taps, w), f32),
            shape_of((w,), f32),
            shape_of((w,), f32),
            shape_of((w,), f32),
            shape_of((d,), f32),
            shape_of((d,), f32),
            shape_of((experts, d), f32),
        ),
        in_specs=[VM],
        out_specs=(VM,) * 10,
        compiler_params=params(),
    )(pack)


def blend(pick, got, prob, two):
    s, t, d = two.shape

    def kernel(pick_ref, got_ref, prob_ref, two_ref, out_ref):
        rows = dot_tn(pick_ref[...], got_ref[...])
        for seq in range(s):
            out_ref[seq] = two_ref[seq] + prob_ref[seq] * rows[seq * t : (seq + 1) * t]

    return pl.pallas_call(
        kernel,
        out_shape=shape_of((s, t, d), f32),
        in_specs=[VM] * 4,
        out_specs=VM,
        compiler_params=params(),
    )(pick, got, prob, two)


def shifted(value, axis, steps):
    count = lax.axis_size(axis)
    leading, last = (max(0, -steps), min(count, count - steps))
    return lax.ppermute(value, axis, [(source, source + steps) for source in range(leading, last)])


def swapped(value, axis, mask):
    return lax.ppermute(value, axis, [(i, i ^ mask) for i in range(lax.axis_size(axis))])


def after(value, *others):
    return lax.optimization_barrier((value, others))[0]


def together(*values):
    return lax.optimization_barrier(values)


def exchanged(parts, axis):
    return lax.all_to_all(parts, axis, split_axis=0, concat_axis=0, tiled=True)


def added(first, *others):
    total = first.astype(f32)
    for other in others:
        total = total + other.astype(f32)
    return total.astype(bf16)


def bits_of(axis):
    return range(lax.axis_size(axis).bit_length() - 1)


def doubled(block, axis, bit, dim):
    other = swapped(block, axis, 1 << bit)
    low = (lax.axis_index(axis) >> bit) & 1 == 0
    return jnp.where(
        low,
        jnp.concatenate([block, other], axis=dim),
        jnp.concatenate([other, block], axis=dim),
    )


class Gather:
    def __init__(self, block):
        many = len(bits_of("expert")) - 1
        cut = block.shape[1] // 2
        self.many = many
        self.routes = [[*range(1, many + 1)], [*range(many, 0, -1)]]
        self.halves = [
            piece.reshape((2,) * many + piece.shape[1:]) for piece in (block[:, :cut], block[:, cut:])
        ]

    def step(self, place):
        self.pairs = []
        for half, route in zip(self.halves, self.routes):
            bit = route[place]
            side = (lax.axis_index("expert") >> bit) & 1
            dim = self.many - bit
            stays = lax.dynamic_slice_in_dim(half, side, 1, dim)
            goes = lax.dynamic_slice_in_dim(half, 1 - side, 1, dim)
            self.pairs.append((stays, swapped(goes, "expert", 1 << bit)))
        return self.pairs

    def add(self):
        self.halves = [added(*pair) for pair in self.pairs]

    def whole(self):
        return jnp.concatenate([half.reshape(half.shape[self.many :]) for half in self.halves], axis=0)


def group_parts(block):
    count = lax.axis_size("dp")
    mine = lax.axis_index("dp")
    parts = block.reshape(count, -1, block.shape[-1])

    def part(place):
        return lax.dynamic_index_in_dim(parts, place, 0, keepdims=False)

    return [part(mine)] + [swapped(part(mine ^ mask), "dp", mask) for mask in range(1, count)]


def group_blocks(share):
    return [share] + [swapped(share, "dp", mask) for mask in range(1, lax.axis_size("dp"))]


def joined_groups(seen):
    mine = lax.axis_index("dp")
    blocks = []
    for place in range(len(seen)):
        block = seen[0]
        for mask in range(1, len(seen)):
            block = jnp.where(mine ^ mask == place, seen[mask], block)
        blocks.append(block)
    return jnp.concatenate(blocks, axis=0)


class Spread:
    def __init__(self, block):
        many = len(bits_of("expert")) - 1
        cut = block.shape[0] // 2
        self.many = many
        self.routes = [[*range(many, 0, -1)], [*range(1, many + 1)]]
        self.halves = [
            piece.reshape((1,) * many + piece.shape) for piece in (block[:cut], block[cut:])
        ]

    def step(self, place):
        self.halves = [
            doubled(half, "expert", route[place], self.many - route[place])
            for half, route in zip(self.halves, self.routes)
        ]
        return self.halves

    def whole(self):
        blocks = [half.reshape((-1,) + half.shape[self.many :]) for half in self.halves]
        return jnp.concatenate(blocks, axis=1)


def body(
    layer_input,
    norm1_gain,
    w_in,
    conv_weight,
    conv_bias,
    w_xproj,
    w_dt,
    dt_bias,
    a_log,
    d_skip,
    w_out,
    norm2_gain,
    router_weight,
    w_up,
    w_down,
    expert_route,
    capacity,
    output_grad,
):
    seq_count, span_len, model_width = layer_input.shape
    inner_width = w_in.shape[1] // 2
    conv_taps = conv_weight.shape[0]
    rank_dt = w_dt.shape[0]
    state_width = a_log.shape[1]
    experts_all = router_weight.shape[1]
    tokens = seq_count * span_len
    groups, holders = (lax.axis_size("dp"), lax.axis_size("expert"))
    slot_count = max(2, 5 * tokens // (4 * experts_all))
    slots = experts_all * slot_count
    far = max(1, groups // 2)
    w_masks = range(1, far)
    mine = lax.axis_index("expert").astype(jnp.int32).reshape(1)
    reach = 8

    core = mine & 1

    def traded(placed):
        blocks = placed.reshape(experts_all, slot_count, model_width)
        return exchanged(blocks, "expert").reshape(slots, model_width)

    rim = shifted(layer_input[:, span_len - reach :], "expert", 1)
    pick, placed, choose, counts = route(expert_route, capacity, output_grad, slot_count)
    og_own = traded(placed)
    up_mats = [w_up[0]] + [swapped(w_up[0], "dp", mask) for mask in w_masks]
    down_mats = [w_down[0]] + [swapped(w_down[0], "dp", mask) for mask in w_masks]
    router_t = router_weight.T

    normed, conv_in, gate_z, pre_conv, act, sel, selt, dt_pre, step, rate2, ends = front(
        layer_input, rim, norm1_gain, w_in, conv_weight, conv_bias, w_xproj.T, w_dt, dt_bias, a_log.T, counts
    )
    og_own, ends = together(og_own, ends)
    og_other = swapped(og_own, "dp", far)
    every = lax.all_gather(ends, "expert")
    saved, y_full, gated, stream_two, gate_prob, placed = middle(
        mine, every, step, act, sel, selt, rate2, d_skip, gate_z, layer_input, w_out, norm2_gain, pick, choose,
        router_t,
    )
    placed, og_other, up_mats, down_mats = together(placed, og_other, up_mats, down_mats)

    row_own = traded(placed)
    row_other = swapped(row_own, "dp", far)
    fwd_a, bwd_a, grd_a, log_a, hid_a, pre_a = expert_rows(
        mine, row_own, og_own, router_t, up_mats, down_mats, f32
    )
    counts = jnp.sum(
        after(every, row_own)[:, -8 + 2 * seq_count, : 2 * experts_all].astype(f32), axis=0
    ).reshape(2, experts_all)
    for bit in bits_of("dp"):
        counts = counts + swapped(counts, "dp", 1 << bit)
    row_other, bwd_a, counts = together(row_other, bwd_a, counts)
    fwd_b, bwd_b, grd_b, log_b, hid_b, pre_b = expert_rows(
        mine, row_other, og_other, router_t, up_mats, down_mats, bf16
    )
    bwd_back = swapped(bwd_b, "dp", far)
    up_grads, down_grads, router_grad = expert_grads(
        (row_own, row_other), (grd_a, grd_b), (log_a, log_b), (hid_a, hid_b), (pre_a, pre_b)
    )
    bwd_back, router_grad = together(bwd_back, router_grad)
    got = traded((bwd_a + bwd_back.astype(f32)).astype(bf16))

    stream_two_grad, mix_grad, gain_two_grad, y_grad, z_grad, skip_grad = back(
        got, pick, stream_two, norm2_gain, output_grad, w_out, gate_z, y_full, act
    )
    up_back = [swapped(after(low, got), "dp", mask) for low, mask in zip(up_grads[1:], w_masks)]
    fwd_back = swapped(after(fwd_b, got), "dp", far)
    early, sent = early_pack(
        core, mix_grad, gated.reshape(tokens, inner_width), normed, z_grad.reshape(tokens, inner_width), holders
    )
    y_grad, sent = together(y_grad, sent)
    came = swapped(sent, "expert", 1)
    head = head_of(y_grad, step, selt, rate2)
    head, came = together(head, came)
    first = Gather(added(early, came))
    first.step(0)
    heads = lax.all_gather(head, "expert")
    heads, first.pairs = together(heads, first.pairs)
    first.add()
    for place in range(1, first.many):
        first.step(place)
        if place < first.many - 1:
            first.add()
    down_back = [swapped(after(low, heads), "dp", mask) for low, mask in zip(down_grads[1:], w_masks)]
    pre_grad, small = scan_back(
        conv_taps, mine, heads, every, step, act, y_grad, sel, selt, rate2, saved, dt_pre, w_dt,
        w_xproj.T, d_skip, pre_conv, conv_in,
    )
    up_back, down_back, fwd_back, first.pairs, pre_grad = together(
        up_back, down_back, fwd_back, first.pairs, pre_grad
    )
    first.add()
    parts = group_parts(first.whole())
    rim_back = shifted(pre_grad[:, :reach].astype(bf16), "expert", -1)
    in_rows = model_width // holders * (inner_width // model_width)
    lines = inner_width // model_width * small.shape[0] + 8 + experts_all
    srows = -(-lines // (16 * holders)) * 16
    srows += -(in_rows + srows) % (8 * groups)
    late, sent, grad_input = finish(
        core, pre_grad, rim_back, conv_weight, z_grad, w_in, layer_input, norm1_gain, normed,
        stream_two_grad, small, skip_grad, gain_two_grad, router_grad, (holders, srows),
    )
    parts, late, sent = together(parts, late, sent)

    came = swapped(sent, "expert", 1)
    share = added(*parts)
    seen = group_blocks(share)
    last = Gather(added(late, came))
    for place in range(last.many):
        last.step(place)
        if place < last.many - 1:
            last.add()
    last.pairs, seen = together(last.pairs, seen)
    last.add()
    parts = group_parts(last.whole())
    spread = Spread(joined_groups(seen))
    spread.step(0)
    fwd_sum = added(fwd_a, fwd_back)
    fwd_sum, *spread.halves = together(fwd_sum, *spread.halves)
    fwd_got = traded(fwd_sum)
    parts, fwd_got = together(parts, fwd_got)
    share = added(*parts)
    seen = group_blocks(share)
    for place in range(1, spread.many):
        spread.step(place)
    result = blend(pick, fwd_got, gate_prob, stream_two)
    seen, result, *spread.halves = together(seen, result, *spread.halves)
    early = spread.whole()
    early_far = swapped(early, "expert", 1)
    spread = Spread(joined_groups(seen))
    grad_w_up = up_grads[0] + sum(back_part.astype(f32) for back_part in up_back)
    halves = spread.step(0)
    early, early_far, grad_w_up, *spread.halves = together(early, early_far, grad_w_up, *halves)
    for place in range(1, spread.many):
        spread.step(place)
    grad_w_in, grad_w_out = unpack_early(core, early, early_far, 2 * inner_width)
    grad_w_in, *spread.halves = together(grad_w_in, *spread.halves)
    late = spread.whole()
    late_far = swapped(late, "expert", 1)
    grad_w_down = down_grads[0] + sum(back_part.astype(f32) for back_part in down_back)
    late_far, grad_w_down = together(late_far, grad_w_down)
    grad_w_in, pack = unpack_late(core, late, late_far, grad_w_in)
    wx_grad, wdt_grad, alog_grad, conv_grad, conv_b_grad, dt_b_grad, skip_grad, gain_one, gain_two, router_grad = (
        unpack_small(pack, (sel.shape[2], rank_dt, state_width, conv_taps), inner_width, experts_all)
    )
    expert_loads = counts * (experts_all / (tokens * groups * holders))
    return (
        result,
        grad_input,
        gain_one,
        grad_w_in,
        conv_grad,
        conv_b_grad,
        wx_grad.T,
        wdt_grad,
        dt_b_grad,
        alog_grad.T,
        skip_grad,
        grad_w_out,
        gain_two,
        router_grad.T,
        grad_w_up[None],
        grad_w_down[None],
        expert_loads,
    )


def solution(mesh):
    in_specs = (
        P("dp", "expert", None),
        P(),
        P(),
        P(),
        P(),
        P(),
        P(),
        P(),
        P(),
        P(),
        P(),
        P(),
        P(),
        P("expert", None, "dp"),
        P("expert", "dp", None),
        P("dp", "expert"),
        P(),
        P("dp", "expert", None),
    )
    out_specs = (
        P("dp", "expert", None),
        P("dp", "expert", None),
        P(),
        P(),
        P(),
        P(),
        P(),
        P(),
        P(),
        P(),
        P(),
        P(),
        P(),
        P(),
        P("expert", None, "dp"),
        P("expert", "dp", None),
        P(),
    )
    return jax.shard_map(body, mesh=mesh, in_specs=in_specs, out_specs=out_specs, check_vma=False)
```

```python
import jax
import jax.numpy as jnp
from jax import lax
from jax.experimental import pallas as pl
from jax.experimental.pallas import tpu as pltpu
from jax.sharding import PartitionSpec as P

f32 = jnp.float32
bf16 = jnp.bfloat16
LN = 128
SUB = 16
GROUP = 4
BG = 2
EPSILON = 1e-05
LOG2E = 1.4426950408889634
NT = (((1,), (1,)), ((), ()))
TN = (((0,), (0,)), ((), ()))
VM = pl.BlockSpec(memory_space=pltpu.VMEM)
SM = pl.BlockSpec(memory_space=pltpu.SMEM)
HB = pl.BlockSpec(memory_space=pltpu.HBM)


class Copies:
    def __init__(self, sems):
        self.sems = sems
        self.count = 0
        self.under_way = []

    def start(self, source, target):
        copy = pltpu.make_async_copy(source, target, self.sems.at[self.count])
        self.count += 1
        copy.start()
        self.under_way.append(copy)
        return copy

    def arrived(self, copy):
        copy.wait()
        self.under_way.remove(copy)

    def wait(self):
        while self.under_way:
            self.under_way.pop().wait()


FRONT, MIDDLE, BACK, SCAN, FINISH = (28, 30, 28, 32, 28)


def params(mib=24):
    return pltpu.CompilerParams(vmem_limit_bytes=mib << 20)


def shape_of(shape, dtype):
    return jax.ShapeDtypeStruct(shape, dtype)


def in_hbm(shape, dtype):
    return pltpu.HBM(shape, dtype)


def pinned(*values):
    return [pltpu.with_memory_space_constraint(value, pltpu.HBM) for value in values]


def dot(left, right):
    return jnp.dot(left, right, preferred_element_type=f32)


def dot_nt(left, right):
    return lax.dot_general(left, right, NT, preferred_element_type=f32)


def dot_tn(left, right):
    return lax.dot_general(left, right, TN, preferred_element_type=f32)


def spread_lanes(table, out_ref):
    ns, span = table.shape
    for t in range(span):
        out_ref[t] = jnp.broadcast_to(table[:, t : t + 1], (ns, LN))


def row_of(block, i, ns):
    return jnp.broadcast_to(block[i : i + 1], (ns, LN))


def tile_of(ref, seq, t0, j):
    return ref[seq, pl.ds(pl.multiple_of(t0, SUB), SUB), j * LN : (j + 1) * LN].astype(f32)


def tile_groups(tiles, size):
    return [range(g, min(g + size, tiles)) for g in range(0, tiles, size)]


def block_diagonal(part):
    ns = part.shape[1]
    lane = lax.broadcasted_iota(jnp.int32, (ns, SUB * ns), 1)
    copy = ((lane & (ns - 1)) == lax.broadcasted_iota(jnp.int32, (ns, SUB * ns), 0)).astype(bf16)
    high = part.astype(bf16)
    low = (part - high.astype(f32)).astype(bf16)
    block = lax.broadcasted_iota(jnp.int32, (SUB, SUB * ns), 1) // ns
    own = block == lax.broadcasted_iota(jnp.int32, (SUB, SUB * ns), 0)
    pieces = [jnp.where(own, dot(half, copy), 0.0) for half in (high, low)]
    return jnp.concatenate(pieces, axis=0).astype(bf16)


def silu_slope(values):
    logistic = jax.nn.sigmoid(values)
    return logistic * (1.0 + values * (1.0 - logistic))


def inverse_rms(values):
    return lax.rsqrt(jnp.mean(values * values, axis=-1, keepdims=True) + EPSILON)


def norm_backward(values, gain_vec, inv_rms, upstream):
    normal = values * inv_rms
    weighted = upstream * gain_vec
    mean = jnp.mean(weighted * normal, axis=-1, keepdims=True)
    return (
        inv_rms * (weighted - normal * mean),
        jnp.sum(upstream * normal, axis=0, keepdims=True),
    )


def route(expert_route, capacity, og, slot_count):
    s, t = expert_route.shape
    experts = capacity.shape[0]
    d = og.shape[2]
    tokens = s * t
    slots = experts * slot_count
    digits = tokens.bit_length()

    def kernel(
        cap_from, route_from, og_from, pick_to, placed_ref, choose_to, count_to,
        cap_ref, route_ref, og_ref, pick_ref, choose_ref, count_ref, sems,
    ):
        copies = Copies(sems)
        loads = [
            copies.start(source, target)
            for source, target in ((cap_from, cap_ref), (route_from, route_ref), (og_from, og_ref))
        ]
        copies.arrived(loads[0])
        copies.arrived(loads[1])
        flat = jnp.concatenate([route_ref[k : k + 1] for k in range(s)], axis=1)
        rows = lax.broadcasted_iota(jnp.int32, (LN, tokens), 0)
        choose = (rows == flat).astype(f32)
        earlier = lax.broadcasted_iota(jnp.int32, (tokens, tokens), 0)
        earlier = earlier < lax.broadcasted_iota(jnp.int32, (tokens, tokens), 1)
        rank = dot(choose.astype(bf16), earlier.astype(bf16))
        rank = jnp.sum(rank * choose, axis=0, keepdims=True).astype(jnp.int32)
        slot_limit = cap_ref[...].reshape(1, experts).astype(f32).astype(bf16)
        limit = dot(slot_limit, choose[:experts].astype(bf16)).astype(jnp.int32)
        kept = rank < limit
        target = jnp.where(kept, flat * slot_count + rank, slots)
        pick = lax.broadcasted_iota(jnp.int32, (slots, tokens), 0) == target
        pick = pick.astype(f32).astype(bf16)
        pick_ref[...] = pick
        copies.start(pick_ref, pick_to)
        copies.arrived(loads[2])
        every = jnp.concatenate([og_ref[k] for k in range(s)], axis=0)
        placed_ref[...] = dot(pick, every).astype(bf16)
        choose_ref[...] = choose.T[:, :experts]
        copies.start(choose_ref, choose_to)
        kept = kept.astype(f32)
        low = choose[:experts].astype(bf16)
        lines = [dot_nt(v.astype(bf16), low) for v in (kept, 1.0 - kept)]
        count = jnp.concatenate(lines, axis=1).astype(jnp.int32)
        lines = [((count >> k) & 1).astype(f32) for k in range(digits)]
        lines.append(jnp.zeros((1, d - 2 * experts * digits), f32))
        count_ref[...] = jnp.concatenate(lines, axis=1)
        copies.start(count_ref, count_to)
        copies.wait()

    return pl.pallas_call(
        kernel,
        out_shape=(
            in_hbm((slots, tokens), bf16),
            shape_of((slots, d), bf16),
            in_hbm((tokens, experts), f32),
            in_hbm((1, d), f32),
        ),
        in_specs=[HB] * 3,
        out_specs=(HB, VM, HB, HB),
        scratch_shapes=[
            pltpu.VMEM((experts,), jnp.int32),
            pltpu.VMEM((s, t), jnp.int32),
            pltpu.VMEM((s, t, d), bf16),
            pltpu.VMEM((slots, tokens), bf16),
            pltpu.VMEM((tokens, experts), f32),
            pltpu.VMEM((1, d), f32),
            pltpu.SemaphoreType.DMA((6,)),
        ],
        compiler_params=params(),
    )(*pinned(capacity, expert_route, og))


def front_kernel(
    x_from, rim_ref, gain_from, win_from, cw_from, cb_from, wxt_from, wdt_from, dtb_from, alog_from,
    normed_to, conv_to, gate_to, pre_to, act_to, sel_to, selt_to, dtp_to, step_to,
    rate_ref, send_ref, bb_ref, cum_ref,
    win_ref, normed_ref, conv_ref, gate_ref, pre_ref, act_ref, dtp_ref, step_ref, sel_ref, selt_ref,
    x_ref, gain_ref, cw_ref, cb_ref, wxt_ref, wdt_ref, dtb_ref, alog_ref, sems,
):
    copies = Copies(sems)
    loads = [
        copies.start(source, target)
        for source, target in (
            (x_from, x_ref), (gain_from, gain_ref), (cw_from, cw_ref), (cb_from, cb_ref),
            (wxt_from, wxt_ref), (wdt_from, wdt_ref), (dtb_from, dtb_ref), (alog_from, alog_ref),
        )
    ]
    seqs, span, model = x_ref.shape
    width = cw_ref.shape[1]
    taps = cw_ref.shape[0]
    rim = rim_ref.shape[1]
    ns = rate_ref.shape[0]
    rank = wdt_ref.shape[0]
    cols = 512
    halves = [
        copies.start(win_from.at[:, cut], win_ref.at[:, cut])
        for cut in (slice(0, width), slice(width, 2 * width))
    ]
    for load in loads:
        copies.arrived(load)
    gain = gain_ref[...].reshape(1, -1)
    conv_b = cb_ref[...].reshape(1, -1)
    dt_b = dtb_ref[...].reshape(1, -1)
    rate_ref[...] = jnp.exp(alog_ref[...]) * (-LOG2E)
    rows = []
    for ref in (x_ref, rim_ref):
        for seq in range(seqs):
            v = ref[seq].astype(f32)
            rows.append((v * inverse_rms(v) * gain).astype(bf16))
    for seq in range(seqs):
        normed_ref[seq * span : (seq + 1) * span] = rows[seq]
    copies.start(normed_ref, normed_to)
    every = jnp.concatenate(rows, axis=0)
    copies.arrived(halves[0])
    for c in range(0, width, cols):
        cut = slice(c, c + cols)
        r = dot(every, win_ref[:, cut]).astype(bf16)
        for seq in range(seqs):
            main = r[seq * span : (seq + 1) * span]
            edge = r[seqs * span + seq * rim : seqs * span + (seq + 1) * rim]
            conv_ref[seq, :rim, cut] = edge
            conv_ref[seq, rim:, cut] = main
            v = jnp.concatenate([edge, main], axis=0).astype(f32)
            pre = conv_b[:, cut]
            for k in range(taps):
                first = rim - taps + 1 + k
                pre = pre + cw_ref[k : k + 1, cut] * v[first : first + span]
            pre_ref[seq, :, cut] = pre
            act_ref[seq, :, cut] = (pre * jax.nn.sigmoid(pre)).astype(bf16)
    for source, target in ((conv_ref, conv_to), (pre_ref, pre_to), (act_ref, act_to)):
        copies.start(source, target)
    own = every[: seqs * span]
    copies.arrived(halves[1])
    for c in range(width, 2 * width, cols):
        r = dot(own, win_ref[:, c : c + cols])
        for seq in range(seqs):
            gate_ref[seq, :, c - width : c - width + cols] = r[seq * span : (seq + 1) * span]
    copies.start(gate_ref, gate_to)
    for seq in range(seqs):
        sel = dot_nt(act_ref[seq], wxt_ref[...])
        sel_ref[seq] = sel
        lanes = sel.shape[1]
        wide = jnp.concatenate([sel, jnp.zeros((span, -lanes % LN), f32)], axis=1)
        selt = wide.T[:lanes]
        selt_ref[seq] = selt
        low = sel[:, :rank].astype(bf16)
        for c in range(0, width, cols):
            cut = slice(c, c + cols)
            pre = dot(low, wdt_ref[:, cut]) + dt_b[:, cut]
            dtp_ref[seq, :, cut] = pre
            step = jnp.maximum(pre, 0.0) + jnp.log1p(jnp.exp(-jnp.abs(pre)))
            step_ref[seq, :, cut] = step
            cum_ref[seq : seq + 1, cut] = jnp.sum(step, axis=0, keepdims=True)
        if seq == seqs - 1:
            copies.start(sel_ref, sel_to)
            copies.start(selt_ref, selt_to)
        copies.start(dtp_ref.at[seq], dtp_to.at[seq])
        copies.start(step_ref.at[seq], step_to.at[seq])
        spread_lanes(selt[rank : rank + ns], bb_ref)
        tiles = width // LN

        def chunk(k, state):
            t0 = k * SUB
            state = list(state)
            for group in tile_groups(tiles, GROUP):
                dt = {j: tile_of(step_ref, seq, t0, j) for j in group}
                dx = {j: dt[j] * tile_of(act_ref, seq, t0, j) for j in group}
                for i in range(SUB):
                    b = bb_ref[t0 + i]
                    for j in group:
                        rate = rate_ref[:, j * LN : (j + 1) * LN]
                        decay = jnp.exp2(row_of(dt[j], i, ns) * rate)
                        state[j] = decay * state[j] + row_of(dx[j], i, ns) * b
            return tuple(state)

        state = lax.fori_loop(
            0, span // SUB, chunk, tuple(jnp.zeros((ns, LN), f32) for _ in range(tiles))
        )
        for j in range(tiles):
            cut = slice(j * LN, (j + 1) * LN)
            send_ref[seq * ns : (seq + 1) * ns, cut] = state[j].astype(bf16)
    cum = cum_ref[...]
    high = cum.astype(bf16).astype(f32)
    tail = [high, cum - high, jnp.zeros((8 - 2 * seqs, width), f32)]
    send_ref[seqs * ns :, :] = jnp.concatenate(tail, axis=0).astype(bf16)
    copies.wait()


def front(x, rim, gain, w_in, conv_w, conv_b, wx_t, w_dt, dt_b, alog_t):
    s, t, d = x.shape
    w = conv_w.shape[1]
    n = alog_t.shape[0]
    k = wx_t.shape[0]
    return pl.pallas_call(
        front_kernel,
        out_shape=(
            in_hbm((s * t, d), bf16),
            in_hbm((s, rim.shape[1] + t, w), bf16),
            in_hbm((s, t, w), f32),
            in_hbm((s, t, w), f32),
            in_hbm((s, t, w), bf16),
            in_hbm((s, t, k), f32),
            in_hbm((s, k, t), f32),
            in_hbm((s, t, w), f32),
            in_hbm((s, t, w), f32),
            shape_of((n, w), f32),
            shape_of((s * n + 8, w), bf16),
        ),
        in_specs=[HB, VM] + [HB] * 8,
        out_specs=(HB,) * 9 + (VM,) * 2,
        scratch_shapes=[
            pltpu.VMEM((t, n, LN), f32),
            pltpu.VMEM((s, w), f32),
            pltpu.VMEM(w_in.shape, bf16),
            pltpu.VMEM((s * t, d), bf16),
            pltpu.VMEM((s, rim.shape[1] + t, w), bf16),
            pltpu.VMEM((s, t, w), f32),
            pltpu.VMEM((s, t, w), f32),
            pltpu.VMEM((s, t, w), bf16),
            pltpu.VMEM((s, t, w), f32),
            pltpu.VMEM((s, t, w), f32),
            pltpu.VMEM((s, t, k), f32),
            pltpu.VMEM((s, k, t), f32),
        ]
        + [pltpu.VMEM(v.shape, v.dtype) for v in (x, gain, conv_w, conv_b, wx_t, w_dt, dt_b, alog_t)]
        + [
            pltpu.SemaphoreType.DMA((17 + 2 * s,)),
        ],
        compiler_params=params(FRONT),
    )(*pinned(x), rim, *pinned(gain, w_in, conv_w, conv_b, wx_t, w_dt, dt_b, alog_t))


def carry_of(every_ref, rate_ref, seq, seqs, place, stop, step):
    ns, width = rate_ref.shape
    count = jnp.maximum((stop - place) * step, 0)

    def join(u, total):
        block = every_ref[place + u * step].astype(f32)
        row = seqs * ns + seq
        cum = block[row : row + 1] + block[row + seqs : row + seqs + 1]
        return jnp.exp2(rate_ref[...] * cum) * total + block[seq * ns : (seq + 1) * ns]

    return lax.fori_loop(0, count, join, jnp.zeros((ns, width), f32))


def middle_kernel(
    mine_ref, every_ref, step_ref, act_ref, sel_ref, selt_ref, rate_ref, skip_ref, gate_ref,
    x_ref, wout_from, gain_ref, pick_ref, choose_ref, router_ref,
    h_to, y_ref, gated_ref, two_ref, prob_ref, placed_ref, bb_ref, st_ref, acc_ref,
    wout_ref, first_ref, h_ref, sems,
):
    _, span, width = step_ref.shape
    ns = rate_ref.shape[0]
    rank = sel_ref.shape[2] - 2 * ns
    tiles = width // LN
    seqs = pick_ref.shape[1] // span
    mine = mine_ref[0]
    this = pl.program_id(0)
    wout = pltpu.make_async_copy(wout_from, wout_ref, sems.at[0])

    @pl.when(this == 0)
    def _():
        wout.start()

    skip = skip_ref[...].reshape(1, -1)
    for seq in range(seqs):

        @pl.when(pl.program_id(0) == seq)
        def _():
            st_ref[...] = carry_of(every_ref, rate_ref, seq, seqs, 0, mine, 1)

    spread_lanes(selt_ref[0, rank : rank + ns], bb_ref)
    first_ref[...] = st_ref[...].astype(bf16)
    first = pltpu.make_async_copy(first_ref, h_to.at[this, 0:ns, :], sems.at[1])
    first.start()

    def saving(k):
        at = pl.ds(pl.multiple_of((k * SUB + 1) * ns, ns), SUB * ns)
        slot = k & 1
        return pltpu.make_async_copy(h_ref.at[slot], h_to.at[this, at, :], sems.at[2 + slot])

    def chunk(k, carry):
        t0 = k * SUB
        slot = k & 1
        rows = pl.ds(pl.multiple_of(t0, SUB), SUB)

        @pl.when(k >= 2)
        def _():
            saving(k - 2).wait()

        for group in tile_groups(tiles, GROUP):
            state = {j: st_ref[:, j * LN : (j + 1) * LN] for j in group}
            dt = {j: tile_of(step_ref, 0, t0, j) for j in group}
            dx = {j: dt[j] * tile_of(act_ref, 0, t0, j) for j in group}
            for i in range(SUB):
                b = bb_ref[t0 + i]
                for j in group:
                    cut = slice(j * LN, (j + 1) * LN)
                    decay = jnp.exp2(row_of(dt[j], i, ns) * rate_ref[:, cut])
                    state[j] = decay * state[j] + row_of(dx[j], i, ns) * b
                    h_ref[slot, i * ns : (i + 1) * ns, cut] = state[j].astype(bf16)
            for j in group:
                st_ref[:, j * LN : (j + 1) * LN] = state[j]
        diag = block_diagonal(sel_ref[0, rows, rank + ns :])
        saving(k).start()
        r = dot(diag, h_ref[slot])
        y_ref[0, rows, :] = r[:SUB] + r[SUB:] + skip * act_ref[0, rows, :].astype(f32)
        return carry

    chunks = span // SUB
    lax.fori_loop(0, chunks, chunk, 0)
    gate = gate_ref[0]
    gated = (y_ref[0] * (gate * jax.nn.sigmoid(gate))).astype(bf16)
    gated_ref[0] = gated

    @pl.when(this == 0)
    def _():
        wout.wait()

    two = x_ref[0].astype(f32) + dot(gated, wout_ref[...])
    two_ref[0] = two
    moe = (two * inverse_rms(two) * gain_ref[...].reshape(1, -1)).astype(bf16)
    logits = dot_nt(moe, router_ref[...])
    raised = jnp.exp(logits - jnp.max(logits, axis=1, keepdims=True))
    chosen = jnp.sum(raised * choose_ref[...], axis=1, keepdims=True)
    prob_ref[0] = chosen / jnp.sum(raised, axis=1, keepdims=True)
    for seq in range(seqs):

        @pl.when(pl.program_id(0) == seq)
        def _():
            part = dot(pick_ref[:, seq * span : (seq + 1) * span], moe)
            if seq:
                part = part + acc_ref[...]
            if seq < seqs - 1:
                acc_ref[...] = part
            else:
                placed_ref[...] = part.astype(bf16)

    first.wait()
    for k in range(max(0, chunks - 2), chunks):
        saving(k).wait()


def by_sequence(*shape):
    return pl.BlockSpec((1,) + shape, lambda i: (i,) + (0,) * len(shape))


def whole(*shape):
    return pl.BlockSpec(shape, lambda i: (0,) * len(shape))


def middle(
    mine, every, step, act, sel, selt, rate2, skip, gate, x, w_out, gain, pick, choose, router_t
):
    s, t, w = step.shape
    n = rate2.shape[0]
    d = x.shape[2]
    k = sel.shape[2]
    return pl.pallas_call(
        middle_kernel,
        grid=(s,),
        out_shape=(
            in_hbm((s, (t + 1) * n, w), bf16),
            in_hbm((s, t, w), f32),
            in_hbm((s, t, w), bf16),
            in_hbm((s, t, d), f32),
            shape_of((s, t, 1), f32),
            shape_of((pick.shape[0], d), bf16),
        ),
        in_specs=[
            SM,
            whole(*every.shape),
            by_sequence(t, w),
            by_sequence(t, w),
            by_sequence(t, k),
            by_sequence(k, t),
            whole(n, w),
            whole(w),
            by_sequence(t, w),
            by_sequence(t, d),
            HB,
            whole(d),
            whole(*pick.shape),
            pl.BlockSpec((t, choose.shape[1]), lambda i: (i, 0)),
            whole(*router_t.shape),
        ],
        out_specs=(
            HB,
            by_sequence(t, w),
            by_sequence(t, w),
            by_sequence(t, d),
            by_sequence(t, 1),
            whole(pick.shape[0], d),
        ),
        scratch_shapes=[
            pltpu.VMEM((t, n, LN), f32),
            pltpu.VMEM((n, w), f32),
            pltpu.VMEM((pick.shape[0], d), f32),
            pltpu.VMEM((w, d), bf16),
            pltpu.VMEM((n, w), bf16),
            pltpu.VMEM((2, SUB * n, w), bf16),
            pltpu.SemaphoreType.DMA((4,)),
        ],
        compiler_params=params(MIDDLE),
    )(mine, every, *pinned(step, act, sel, selt, rate2, skip, gate, x, w_out, gain, pick, choose), router_t)


def gelu_pair(v):
    root = 0.7978845608028654
    square = v * v
    bend = jnp.tanh(root * (v + 0.044715 * v * square))
    half = 0.5 * (1.0 + bend)
    slope = half + 0.5 * v * (1.0 - bend * bend) * (root * (1.0 + 3.0 * 0.044715 * square))
    return v * half, slope


def expert_kernel(shares, own_ref, rows_ref, og_ref, router_ref, *refs):
    ups, downs, refs = (refs[:shares], refs[shares : 2 * shares], refs[2 * shares :])
    fwd_ref, bwd_ref = refs[:2]
    kept = 2 + 2 * shares
    targets, sources, sems = (refs[2 : 2 + kept], refs[2 + kept : 2 + 2 * kept], refs[-1])
    copies = Copies(sems)
    grd_ref, log_ref = sources[:2]
    hids, pres = (sources[2 : 2 + shares], sources[2 + shares :])
    rows = rows_ref[...]
    logits = dot_nt(rows, router_ref[...])
    top = jnp.max(logits, axis=1, keepdims=True)
    raised = jnp.exp(logits - top)
    probs = raised / jnp.sum(raised, axis=1, keepdims=True)
    own = (lax.broadcasted_iota(jnp.int32, (1, probs.shape[1]), 1) == own_ref[0]).astype(f32)
    gate = jnp.sum(probs * own, axis=1, keepdims=True)
    og = og_ref[...].astype(f32)
    grads = (og * gate).astype(bf16)
    grd_ref[...] = grads
    fwd, bwd = (0.0, 0.0)
    for up_ref, down_ref, hid_ref, pre_ref in zip(ups, downs, hids, pres):
        hidden, slope = gelu_pair(dot(rows, up_ref[...]))
        hidden = hidden.astype(bf16)
        hid_ref[...] = hidden
        fwd = fwd + dot(hidden, down_ref[...])
        pre = (dot_nt(grads, down_ref[...]) * slope).astype(bf16)
        pre_ref[...] = pre
        bwd = bwd + dot_nt(pre, up_ref[...])
    logit = jnp.sum(og * fwd, axis=1, keepdims=True) * gate * (own - probs)
    log_ref[...] = logit
    high = logit.astype(bf16)
    low = (logit - high.astype(f32)).astype(bf16)
    bwd = bwd + dot(high, router_ref[...]) + dot(low, router_ref[...])
    for source, target in zip(sources, targets):
        copies.start(source, target)
    fwd_ref[...] = fwd.astype(fwd_ref.dtype)
    bwd_ref[...] = bwd.astype(bwd_ref.dtype)
    copies.wait()


def expert_rows(own, rows, og, router, ups, downs, dtype):
    m, d = rows.shape
    f = ups[0].shape[1]
    shares = len(ups)

    def kernel(*refs):
        expert_kernel(shares, *refs)

    kept = [((m, d), bf16), ((m, router.shape[0]), f32)] + [((m, f), bf16)] * (2 * shares)
    outs = pl.pallas_call(
        kernel,
        out_shape=(shape_of((m, d), dtype), shape_of((m, d), dtype))
        + tuple(in_hbm(*one) for one in kept),
        in_specs=[SM] + [VM] * (3 + 2 * shares),
        out_specs=(VM, VM) + (HB,) * len(kept),
        scratch_shapes=[pltpu.VMEM(*one) for one in kept] + [pltpu.SemaphoreType.DMA((len(kept),))],
        compiler_params=params(),
    )(own, rows, og, router, *ups, *downs)
    return (*outs[:4], outs[4 : 4 + shares], outs[4 + shares :])


def back(got, pick, two, gain, og, w_out, gate, y, act):
    s, t, w = y.shape
    d = two.shape[2]

    def kernel(
        got_ref, pick_from, two_from, gain_ref, og_from, wout_from, gate_from, y_from, act_from,
        twog_to, mix_ref, gain2_ref, yg_to, zg_to, skipg_ref,
        wout_ref, gate_ref, y_ref, act_ref, twog_ref, yg_ref, zg_ref,
        pick_ref, two_ref, og_ref, sems,
    ):
        cols = 512
        copies = Copies(sems)
        firsts = [
            copies.start(source, target)
            for source, target in ((pick_from, pick_ref), (two_from, two_ref), (og_from, og_ref))
        ]
        loads = [
            copies.start(source, target)
            for source, target in (
                (wout_from, wout_ref), (gate_from, gate_ref), (y_from, y_ref), (act_from, act_ref)
            )
        ]
        for load in firsts:
            copies.arrived(load)
        moe_grad = dot_tn(pick_ref[...], got_ref[...])
        gain = gain_ref[...].reshape(1, -1)
        total = 0.0
        for seq in range(s):
            v = two_ref[seq]
            grad, gained = norm_backward(
                v, gain, inverse_rms(v), moe_grad[seq * t : (seq + 1) * t]
            )
            total = total + gained
            grad = grad + og_ref[seq].astype(f32)
            twog_ref[seq] = grad
            mix_ref[seq * t : (seq + 1) * t] = grad.astype(bf16)
        gain2_ref[...] = total
        copies.start(twog_ref, twog_to)
        for load in loads:
            copies.arrived(load)
        for c in range(0, w, cols):
            cut = slice(c, c + cols)
            r = dot_nt(mix_ref[...], wout_ref[cut, :])
            total = 0.0
            for seq in range(s):
                part = r[seq * t : (seq + 1) * t]
                gate = gate_ref[seq, :, cut]
                logistic = jax.nn.sigmoid(gate)
                yg = part * (gate * logistic)
                yg_ref[seq, :, cut] = yg
                slope = logistic * (1.0 + gate * (1.0 - logistic))
                zg_ref[seq, :, cut] = (part * y_ref[seq, :, cut] * slope).astype(bf16)
                total = total + jnp.sum(yg * act_ref[seq, :, cut].astype(f32), axis=0, keepdims=True)
            skipg_ref[:, cut] = total
            for source, target in ((yg_ref, yg_to), (zg_ref, zg_to)):
                copies.start(source.at[:, :, cut], target.at[:, :, cut])
        copies.wait()

    return pl.pallas_call(
        kernel,
        out_shape=(
            in_hbm((s, t, d), f32),
            shape_of((s * t, d), bf16),
            shape_of((1, d), f32),
            in_hbm((s, t, w), f32),
            in_hbm((s, t, w), bf16),
            shape_of((1, w), f32),
        ),
        in_specs=[VM, HB, HB, VM] + [HB] * 5,
        out_specs=(HB, VM, VM, HB, HB, VM),
        scratch_shapes=[
            pltpu.VMEM((w, d), bf16),
            pltpu.VMEM((s, t, w), f32),
            pltpu.VMEM((s, t, w), f32),
            pltpu.VMEM((s, t, w), bf16),
            pltpu.VMEM((s, t, d), f32),
            pltpu.VMEM((s, t, w), f32),
            pltpu.VMEM((s, t, w), bf16),
            pltpu.VMEM(pick.shape, bf16),
            pltpu.VMEM(two.shape, f32),
            pltpu.VMEM(og.shape, bf16),
            pltpu.SemaphoreType.DMA((8 + 2 * (w // 512),)),
        ],
        compiler_params=params(BACK),
    )(got, *pinned(pick, two), gain, *pinned(og, w_out, gate, y, act))


def head_of(yg, step, selt, rate2):
    s, t, w = step.shape
    n = rate2.shape[0]
    tiles = w // LN

    def kernel(yg_ref, step_ref, selt_ref, rate_ref, head_ref, cb_ref):
        for seq in range(s):
            spread_lanes(selt_ref[seq, selt.shape[1] - n :], cb_ref)

            def chunk(u, mu):
                t0 = t - SUB - u * SUB
                mu = list(mu)
                for group in tile_groups(tiles, GROUP):
                    dt = {j: tile_of(step_ref, seq, t0, j) for j in group}
                    yg = {j: tile_of(yg_ref, seq, t0, j) for j in group}
                    for i in reversed(range(SUB)):
                        c = cb_ref[t0 + i]
                        for j in group:
                            rate = rate_ref[:, j * LN : (j + 1) * LN]
                            decay = jnp.exp2(row_of(dt[j], i, n) * rate)
                            mu[j] = decay * (mu[j] + row_of(yg[j], i, n) * c)
                return tuple(mu)

            mu = lax.fori_loop(
                0, t // SUB, chunk, tuple(jnp.zeros((n, LN), f32) for _ in range(tiles))
            )
            for j in range(tiles):
                cut = slice(j * LN, (j + 1) * LN)
                head_ref[seq * n : (seq + 1) * n, cut] = mu[j].astype(bf16)

    return pl.pallas_call(
        kernel,
        out_shape=shape_of((s * n, w), bf16),
        in_specs=[VM] * 4,
        out_specs=VM,
        scratch_shapes=[pltpu.VMEM((t, n, LN), f32)],
        compiler_params=params(),
    )(yg, step, selt, rate2)


def scan_back_kernel(
    taps, seq, seqs, mine_ref, heads_ref, every_ref, step_ref, act_ref, yg_ref, sel_ref, selt_ref, rate_ref, h_from,
    dtp_from, wdt_from, wxt_from, skip_ref, pre_from, conv_from, *refs
):
    prior, refs = (refs[:2], refs[2:]) if seq else ((), refs)
    scan_back_run(
        taps, seq, seqs, mine_ref, heads_ref, every_ref, step_ref, act_ref, yg_ref, sel_ref, selt_ref, rate_ref,
        h_from, dtp_from, wdt_from, wxt_from, skip_ref, pre_from, conv_from, prior, *refs
    )


def scan_back_run(
    taps, seq, seqs, mine_ref, heads_ref, every_ref, step_ref, act_ref, yg_ref, sel_ref, selt_ref, rate_ref,
    h_from, dtp_from, wdt_from, wxt_from, skip_ref, pre_from, conv_from, prior,
    preg_ref, rim_ref, small_ref, cb_ref, mu_ref, al_ref, lam_ref, rdg_ref, s1_ref, adj_ref, ig_ref, og_ref,
    h_ref, dtp_ref, wdt_ref, wxt_ref, pre_ref, conv_ref, sems,
):
    chunks = step_ref.shape[1] // SUB

    def loading(v):
        at = pl.ds(pl.multiple_of((chunks - 1 - v) * SUB * rate_ref.shape[0], 8), h_ref.shape[1])
        return pltpu.make_async_copy(h_from.at[seq, at, :], h_ref.at[v & 1], sems.at[v & 1])

    loading(0).start()
    copies = Copies(sems.at[2:])
    for source, target in (
        (dtp_from.at[seq], dtp_ref), (wdt_from, wdt_ref), (wxt_from, wxt_ref), (pre_from.at[seq], pre_ref),
        (conv_from.at[seq], conv_ref),
    ):
        copies.start(source, target)
    _, span, width = step_ref.shape
    ns = rate_ref.shape[0]
    lanes = sel_ref.shape[2]
    rank = lanes - 2 * ns
    tiles = width // LN
    holders = heads_ref.shape[0]
    rim = conv_ref.shape[0] - span
    count = holders - 1 - mine_ref[0]

    def join(u, total):
        place = holders - 1 - u
        tail = every_ref[place].astype(f32)
        cum = tail[seq : seq + 1] + tail[seqs + seq : seqs + seq + 1]
        return jnp.exp2(rate_ref[...] * cum) * total + heads_ref[place].astype(f32)

    mu_ref[...] = lax.fori_loop(0, count, join, jnp.zeros((ns, width), f32))
    spread_lanes(selt_ref[0, rank + ns :], cb_ref)
    al_ref[...] = jnp.zeros((ns, width), f32)
    block = lax.broadcasted_iota(jnp.int32, (SUB, SUB * ns), 1) // ns
    ones = (block == lax.broadcasted_iota(jnp.int32, (SUB, SUB * ns), 0)).astype(bf16)

    def chunk(v, carry):
        k = chunks - 1 - v
        t0 = k * SUB
        slot = v & 1
        rows = pl.ds(pl.multiple_of(t0, SUB), SUB)

        @pl.when(v + 1 < chunks)
        def _():
            loading(v + 1).start()

        loading(v).wait()
        for group in tile_groups(tiles, BG):
            cuts = {j: slice(j * LN, (j + 1) * LN) for j in group}
            mu = {j: mu_ref[:, cuts[j]] for j in group}
            al = {j: al_ref[:, cuts[j]] for j in group}
            dts = {j: tile_of(step_ref, 0, t0, j) for j in group}
            ygs = {j: tile_of(yg_ref, 0, t0, j) for j in group}
            for i in reversed(range(SUB)):
                c = cb_ref[t0 + i]
                for j in group:
                    rate = rate_ref[:, cuts[j]]
                    dt = row_of(dts[j], i, ns)
                    decay = jnp.exp2(dt * rate)
                    lam = mu[j] + row_of(ygs[j], i, ns) * c
                    mu[j] = decay * lam
                    dg = mu[j] * h_ref[slot, i * ns : (i + 1) * ns, cuts[j]].astype(f32)
                    al[j] = al[j] + dt * dg
                    lam_ref[i * ns : (i + 1) * ns, cuts[j]] = lam.astype(bf16)
                    rdg_ref[i * ns : (i + 1) * ns, cuts[j]] = (rate * dg).astype(bf16)
            for j in group:
                mu_ref[:, cuts[j]] = mu[j]
                al_ref[:, cuts[j]] = al[j]
        lam = lam_ref[...]
        r = dot(block_diagonal(sel_ref[0, rows, rank : rank + ns]), lam)
        adj_ref[rows, :] = r[:SUB] + r[SUB:]
        s1_ref[rows, :] = dot(ones, rdg_ref[...]) * (1.0 / LOG2E)
        up = lax.broadcasted_iota(jnp.int32, (SUB * ns, SUB), 0) // ns
        own = up == lax.broadcasted_iota(jnp.int32, (SUB * ns, SUB), 1)
        dx = (step_ref[0, rows, :] * act_ref[0, rows, :].astype(f32)).astype(bf16)
        d = dot_nt(lam, dx)
        ig_ref[k] = jnp.sum(jnp.where(own, d, 0.0).reshape(SUB, ns, SUB), axis=0)
        d = dot_nt(h_ref[slot, ns:, :], yg_ref[0, rows, :].astype(bf16))
        og_ref[k] = jnp.sum(jnp.where(own, d, 0.0).reshape(SUB, ns, SUB), axis=0)
        return carry

    lax.fori_loop(0, chunks, chunk, 0)
    copies.wait()
    act = act_ref[0].astype(f32)
    adj = adj_ref[...]
    step = step_ref[0]
    dtg = (s1_ref[...] + adj * act) * jax.nn.sigmoid(dtp_ref[...])
    low = dtg.astype(bf16)
    grads = [dot_nt(wdt_ref[...], low)] + [
        jnp.concatenate([ref[k] for k in range(chunks)], axis=1) for ref in (ig_ref, og_ref)
    ]
    grads = jnp.concatenate(grads, axis=0).astype(bf16)
    at = 0

    def put(rows):
        nonlocal at
        cut = slice(at, at + rows.shape[0])
        small_ref[cut, :] = prior[0][cut, :] + rows if seq else rows
        at += rows.shape[0]

    put(dot(grads, act_ref[0]))
    put(dot(selt_ref[0, :rank].astype(bf16), low))
    put(rate_ref[...] * al_ref[...] * (1.0 / LOG2E))
    act_grad = yg_ref[0] * skip_ref[...].reshape(1, -1) + adj * step + dot_tn(grads, wxt_ref[...])
    pre_grad = act_grad * silu_slope(pre_ref[...])
    preg_ref[0] = pre_grad
    rim_ref[seq] = pre_grad[:rim].astype(bf16)
    for place in range(seq):
        rim_ref[place] = prior[1][place]
    inputs = conv_ref[...].astype(f32)
    tail = []
    for k in range(taps):
        first = rim - taps + 1 + k
        tail.append(jnp.sum(pre_grad * inputs[first : first + span], axis=0, keepdims=True))
    tail.append(jnp.sum(pre_grad, axis=0, keepdims=True))
    tail.append(jnp.sum(dtg, axis=0, keepdims=True))
    tail.append(jnp.zeros((8 - len(tail), width), f32))
    put(jnp.concatenate(tail, axis=0))


def scan_back(
    taps, seq, mine, heads, every, step, act, yg, sel, selt, rate2, h, dtp, w_dt, wx_t, skip, pre, conv,
    prior,
):
    s, t, w = step.shape
    n = rate2.shape[0]
    k = sel.shape[2]
    chunks = t // SUB
    rim = conv.shape[1] - t
    small = k + w_dt.shape[0] + n + 8

    def kernel(*refs):
        scan_back_kernel(taps, seq, s, *refs)

    def own(*shape):
        return pl.BlockSpec((1,) + shape, lambda i: (seq,) + (0,) * len(shape))

    return pl.pallas_call(
        kernel,
        grid=(1,),
        out_shape=(
            shape_of((1, t, w), f32),
            shape_of((s, rim, w), bf16),
            shape_of((small, w), f32),
        ),
        in_specs=[
            SM,
            pl.BlockSpec((heads.shape[0], n, w), lambda i: (0, seq, 0)),
            pl.BlockSpec((every.shape[0], 8, w), lambda i: (0, s * n // 8, 0)),
            own(t, w),
            own(t, w),
            own(t, w),
            own(t, k),
            own(k, t),
            whole(n, w),
            HB,
            HB,
            HB,
            HB,
            whole(w),
            HB,
            HB,
            *(whole(*value.shape) for value in prior),
        ],
        out_specs=(whole(1, t, w), whole(s, rim, w), whole(small, w)),
        scratch_shapes=[
            pltpu.VMEM((t, n, LN), f32),
            pltpu.VMEM((n, w), f32),
            pltpu.VMEM((n, w), f32),
            pltpu.VMEM((SUB * n, w), bf16),
            pltpu.VMEM((SUB * n, w), bf16),
            pltpu.VMEM((t, w), f32),
            pltpu.VMEM((t, w), f32),
            pltpu.VMEM((chunks, n, SUB), f32),
            pltpu.VMEM((chunks, n, SUB), f32),
            pltpu.VMEM((2, (SUB + 1) * n, w), bf16),
            pltpu.VMEM((t, w), f32),
            pltpu.VMEM(w_dt.shape, bf16),
            pltpu.VMEM(wx_t.shape, bf16),
            pltpu.VMEM((t, w), f32),
            pltpu.VMEM(conv.shape[1:], bf16),
            pltpu.SemaphoreType.DMA((7,)),
        ],
        compiler_params=params(SCAN),
    )(
        mine, heads, *pinned(every, step, act, yg, sel, selt, rate2, h, dtp, w_dt, wx_t, skip, pre, conv), *prior
    )


def expert_grads(rows, grds, logs, hids, pres):
    blocks = len(rows)
    shares = len(hids[0])
    d = rows[0].shape[1]
    f = hids[0][0].shape[1]
    flat = [*rows, *grds, *logs] + [v for group in (hids, pres) for block in group for v in block]

    def kernel(*refs):
        count, many = (len(flat), len(outs_shape))
        targets = refs[count : count + many]
        ins = refs[count + many : 2 * count + many]
        outs = refs[2 * count + many : 2 * (count + many)]
        copies = Copies(refs[-1])
        for source, target in zip(refs[:count], ins):
            copies.start(source, target)
        copies.wait()
        row, grd, log = (ins[k * blocks : (k + 1) * blocks] for k in range(3))
        hid = ins[3 * blocks : (3 + shares) * blocks]
        pre = ins[(3 + shares) * blocks :]

        def total(lefts, rights):
            parts = [dot_tn(left[...], right[...]) for left, right in zip(lefts, rights)]
            return sum(parts[1:], parts[0])

        at = 0
        for k in range(shares):
            for value in (total(row, pre[k::shares]), total(hid[k::shares], grd)):
                first = 0
                while first < value.shape[0]:
                    ref = outs[at]
                    ref[...] = value[first : first + ref.shape[0]].astype(ref.dtype)
                    copies.start(ref, targets[at])
                    first += ref.shape[0]
                    at += 1
        router = 0.0
        for log_ref, row_ref in zip(log, row):
            high = log_ref[...].astype(bf16)
            low = (log_ref[...] - high.astype(f32)).astype(bf16)
            router = router + dot_tn(high, row_ref[...]) + dot_tn(low, row_ref[...])
        outs[-1][...] = router
        copies.start(outs[-1], targets[-1])
        copies.wait()

    outs_shape = [((d, f), f32), ((f, d), f32)]
    for _ in range(1, shares):
        outs_shape += [((d // 2, f), bf16)] * 2
        outs_shape += [((f // 4, d), bf16), ((f - f // 4, d), bf16)]
    outs_shape.append(((logs[0].shape[1], d), f32))
    got = pl.pallas_call(
        kernel,
        out_shape=tuple(in_hbm(*one) for one in outs_shape),
        in_specs=[HB] * len(flat),
        out_specs=(HB,) * len(outs_shape),
        scratch_shapes=[pltpu.VMEM(v.shape, v.dtype) for v in flat]
        + [pltpu.VMEM(*one) for one in outs_shape]
        + [pltpu.SemaphoreType.DMA((len(flat) + len(outs_shape),))],
        compiler_params=params(),
    )(*pinned(*flat))
    return got[0], got[1], [got[2 + k : -1 : 4] for k in range(4)], got[-1]


def deal(block_ref, keep_ref, send_ref, core, first, rows):
    for pair in range(keep_ref.shape[0]):
        for ref, side in ((keep_ref, core), (send_ref, 1 - core)):
            at = pl.ds(pl.multiple_of((2 * pair + side) * rows, rows), rows)
            ref[pair, first : first + rows, :] = block_ref[at, :]


def early_pack(core, mix, gated, normed, zg, holders):
    d = mix.shape[1]
    w = gated.shape[1]
    out_rows, in_rows, pieces = (w // holders, d // holders, w // d)

    def kernel(core_ref, mix_ref, gated_ref, normed_ref, zg_ref, keep_ref, send_ref, block_ref):
        block_ref[...] = dot_tn(gated_ref[...], mix_ref[...]).astype(bf16)
        deal(block_ref, keep_ref, send_ref, core_ref[0], 0, out_rows)
        for p in range(pieces):
            r = dot_tn(normed_ref[...], zg_ref[:, p * d : (p + 1) * d])
            block_ref[p * d : (p + 1) * d] = r.astype(bf16)
            side = block_ref.at[p * d : (p + 1) * d]
            deal(side, keep_ref, send_ref, core_ref[0], out_rows + p * in_rows, in_rows)

    shape = shape_of((holders // 2, out_rows + pieces * in_rows, d), bf16)
    return pl.pallas_call(
        kernel,
        out_shape=(shape, shape),
        in_specs=[SM] + [VM] * 4,
        out_specs=(VM, VM),
        scratch_shapes=[pltpu.VMEM((w, d), bf16)],
        compiler_params=params(),
    )(core, mix, gated, normed, zg)


def finish(
    core, preg, rim, conv_w, zg, w_in, x, gain, normed, twog, small, skipg, gain2, counts, router,
    plan,
):
    s = len(preg)
    _, t, w = preg[0].shape
    d = x.shape[2]
    holders, srows = plan
    taps = conv_w.shape[0]
    pieces, in_rows = (w // d, d // holders)

    def kernel(core_ref, *refs):
        preg_refs, refs = (refs[:s], refs[s:])
        run(core_ref, preg_refs, *refs)

    def run(
        core_ref, preg_refs, rim_ref, cw_ref, zg_from, win_from, x_from, gain_ref, normed_from, twog_from,
        small_from, skip_ref, gain2_ref, count_ref, router_ref,
        keep_ref, send_ref, input_to, cg_ref, pack_ref, block_ref,
        zg_ref, win_ref, x_ref, normed_ref, twog_ref, input_ref, sems,
    ):
        copies = Copies(sems)
        pack_ref[...] = jnp.zeros(pack_ref.shape, f32)
        tall = small_from.shape[0]
        first = copies.start(normed_from, normed_ref)
        loads = [copies.start(win_from, win_ref), copies.start(zg_from, zg_ref)]
        loads += [copies.start(x_from, x_ref), copies.start(twog_from, twog_ref)]
        smalls = [
            copies.start(
                small_from.at[:, p * d : (p + 1) * d], pack_ref.at[p * tall : (p + 1) * tall]
            )
            for p in range(pieces)
        ]
        cols = 512
        gain = gain_ref[...].reshape(1, -1)
        for seq in range(s):
            for c in range(0, w, cols):
                cut = slice(c, c + cols)
                v = jnp.concatenate(
                    [preg_refs[seq][0, :, cut], rim_ref[seq, :, cut].astype(f32)], axis=0
                )
                total = cw_ref[taps - 1 : taps, cut] * v[:t]
                for k in range(1, taps):
                    total = total + cw_ref[taps - 1 - k : taps - k, cut] * v[k : k + t]
                cg_ref[seq * t : (seq + 1) * t, cut] = total.astype(bf16)
        copies.arrived(first)
        for p in range(pieces):
            block_ref[:d] = dot_tn(normed_ref[...], cg_ref[:, p * d : (p + 1) * d]).astype(bf16)
            deal(block_ref, keep_ref, send_ref, core_ref[0], p * in_rows, in_rows)
        for load in loads:
            copies.arrived(load)
        gain1 = 0.0
        for seq in range(s):
            grad = dot_nt(cg_ref[seq * t : (seq + 1) * t], win_ref[:, :w])
            grad = grad + dot_nt(zg_ref[seq], win_ref[:, w:])
            v = x_ref[seq].astype(f32)
            grad, gained = norm_backward(v, gain, inverse_rms(v), grad)
            gain1 = gain1 + gained
            input_ref[seq] = twog_ref[seq] + grad
        copies.start(input_ref, input_to)
        for load in smalls:
            copies.arrived(load)
        at = pieces * tall
        lines = [skip_ref[:, p * d : (p + 1) * d] for p in range(pieces)] + [gain1, gain2_ref[...], count_ref[...]]
        for line in lines:
            pack_ref[at : at + 1] = line
            at += 1
        at += -at % 8
        pack_ref[at : at + router_ref.shape[0]] = router_ref[...]
        block_ref[: holders * srows] = pack_ref[...].astype(bf16)
        deal(block_ref, keep_ref, send_ref, core_ref[0], pieces * in_rows, srows)
        copies.wait()

    return pl.pallas_call(
        kernel,
        out_shape=(
            shape_of((holders // 2, pieces * in_rows + srows, d), bf16),
            shape_of((holders // 2, pieces * in_rows + srows, d), bf16),
            shape_of((s, t, d), f32),
        ),
        in_specs=[SM]
        + [VM] * (s + 2)
        + [HB] * 3
        + [VM]
        + [HB] * 3
        + [VM] * 4,
        out_specs=(VM, VM, HB),
        scratch_shapes=[
            pltpu.VMEM((s * t, w), bf16),
            pltpu.VMEM((holders * srows, d), f32),
            pltpu.VMEM((max(d, holders * srows), d), bf16),
            pltpu.VMEM(zg.shape, bf16),
            pltpu.VMEM(w_in.shape, bf16),
            pltpu.VMEM(x.shape, bf16),
            pltpu.VMEM(normed.shape, bf16),
            pltpu.VMEM(twog.shape, f32),
            pltpu.VMEM(twog.shape, f32),
            pltpu.SemaphoreType.DMA((6 + pieces,)),
        ],
        compiler_params=params(FINISH),
    )(
        core, *preg, rim, conv_w, *pinned(zg, w_in, x), gain, *pinned(normed, twog, small), skipg, gain2, counts,
        router,
    )


def unpack_early(core, mine, other, width_in):
    pairs, rows, d = mine.shape
    holders = 2 * pairs
    w = width_in // 2
    out_rows, in_rows, pieces = (w // holders, d // holders, w // d)

    def kernel(core_ref, mine_ref, other_ref, win_ref, wout_ref):
        for ref, side in ((mine_ref, core_ref[0]), (other_ref, 1 - core_ref[0])):
            for i in range(pairs):
                at = pl.ds(pl.multiple_of((2 * i + side) * out_rows, out_rows), out_rows)
                wout_ref[at, :] = ref[i, :out_rows].astype(f32)
                at = pl.ds(pl.multiple_of((2 * i + side) * in_rows, in_rows), in_rows)
                for p in range(pieces):
                    first = out_rows + p * in_rows
                    win_ref[at, p * d : (p + 1) * d] = ref[i, first : first + in_rows].astype(f32)

    return pl.pallas_call(
        kernel,
        grid=(1,),
        out_shape=(shape_of((d, width_in), f32), shape_of((w, d), f32)),
        in_specs=[SM, whole(*mine.shape), whole(*mine.shape)],
        out_specs=(pl.BlockSpec((d, w), lambda i: (0, 1)), whole(w, d)),
        compiler_params=params(),
    )(core, mine, other)


def unpack_late(core, mine, other, wide, heights, experts, digits, scale):
    pairs, rows, d = mine.shape
    holders = 2 * pairs
    w = wide.shape[1] // 2
    in_rows, pieces = (d // holders, w // d)
    srows = rows - pieces * in_rows
    k, rank, n, taps = heights
    tall = k + rank + n + 8

    def kernel(
        core_ref, mine_ref, other_ref, wide_ref, win_ref, wx_ref, wdt_ref, alog_ref, cw_ref, *refs
    ):
        vectors, (gain1_ref, gain2_ref, router_ref, load_ref, pack_ref) = (refs[:3], refs[3:])
        for ref, side in ((mine_ref, core_ref[0]), (other_ref, 1 - core_ref[0])):
            for i in range(pairs):
                at = pl.ds(pl.multiple_of((2 * i + side) * in_rows, in_rows), in_rows)
                for p in range(pieces):
                    part = ref[i, p * in_rows : (p + 1) * in_rows]
                    win_ref[at, p * d : (p + 1) * d] = part.astype(f32)
                at = pl.ds(pl.multiple_of((2 * i + side) * srows, srows), srows)
                pack_ref[at, :] = ref[i, pieces * in_rows :].astype(f32)
        lines = [pack_ref[p * tall : (p + 1) * tall] for p in range(pieces)]
        lines = jnp.concatenate(lines, axis=1)
        at = 0
        for ref in (wx_ref, wdt_ref, alog_ref):
            ref[...] = lines[at : at + ref.shape[0]]
            at += ref.shape[0]
        tail = lines[at:]
        cw_ref[...] = tail[:taps]
        at = pieces * tall
        vectors[0][...] = tail[taps]
        vectors[1][...] = tail[taps + 1]
        skips = pack_ref[at : at + 8]
        vectors[2][...] = jnp.concatenate([skips[p : p + 1] for p in range(pieces)], axis=1)[0]
        gain1_ref[...] = skips[pieces]
        gain2_ref[...] = skips[pieces + 1]
        count = skips[pieces + 2 : pieces + 3]
        for row in range(2):
            total = 0.0
            for digit in range(digits):
                first = (2 * digit + row) * experts
                total = total + 2.0**digit * count[:, first : first + experts]
            load_ref[row : row + 1, :] = total * scale
        router_ref[...] = pack_ref[at + 8 : at + 8 + experts]

    shapes = [(k, w), (rank, w), (n, w), (taps, w), (w,), (w,), (w,), (d,), (d,), (experts, d), (2, experts)]
    return pl.pallas_call(
        kernel,
        grid=(1,),
        out_shape=(shape_of(wide.shape, f32),) + tuple(shape_of(v, f32) for v in shapes),
        in_specs=[SM, whole(*mine.shape), whole(*mine.shape), pl.BlockSpec(memory_space=pl.ANY)],
        out_specs=(whole(d, w),) + tuple(whole(*v) for v in shapes),
        scratch_shapes=[pltpu.VMEM((holders * srows, d), f32)],
        input_output_aliases={3: 0},
        compiler_params=params(),
    )(core, mine, other, wide)


def blend(pick, near, far, prob, two):
    s, t, d = two.shape

    def kernel(pick_ref, near_ref, far_ref, prob_ref, two_ref, out_ref):
        rows = dot_tn(pick_ref[...], near_ref[...]) + dot_tn(pick_ref[...], far_ref[...])
        for seq in range(s):
            out_ref[seq] = two_ref[seq] + prob_ref[seq] * rows[seq * t : (seq + 1) * t]

    return pl.pallas_call(
        kernel,
        out_shape=shape_of((s, t, d), f32),
        in_specs=[VM] * 5,
        out_specs=VM,
        compiler_params=params(),
    )(pick, near, far, prob, two)


def shifted(value, axis, steps):
    count = lax.axis_size(axis)
    leading, last = (max(0, -steps), min(count, count - steps))
    return lax.ppermute(value, axis, [(source, source + steps) for source in range(leading, last)])


def swapped(value, axis, mask):
    return lax.ppermute(value, axis, [(i, i ^ mask) for i in range(lax.axis_size(axis))])


def after(value, *others):
    return lax.optimization_barrier((value, others))[0]


def together(*values):
    return lax.optimization_barrier(values)


def exchanged(parts, axis):
    return lax.all_to_all(parts, axis, split_axis=0, concat_axis=0, tiled=True)


def added(first, *others):
    total = first.astype(f32)
    for other in others:
        total = total + other.astype(f32)
    return total.astype(bf16)


def bits_of(axis):
    return range(lax.axis_size(axis).bit_length() - 1)


def doubled(block, axis, bit, dim):
    other = swapped(block, axis, 1 << bit)
    low = (lax.axis_index(axis) >> bit) & 1 == 0
    return jnp.where(
        low,
        jnp.concatenate([block, other], axis=dim),
        jnp.concatenate([other, block], axis=dim),
    )


class Gather:
    def __init__(self, block):
        many = len(bits_of("expert")) - 1
        cut = block.shape[1] // 2
        self.many = many
        self.routes = [[*range(1, many + 1)], [*range(many, 0, -1)]]
        self.halves = [
            piece.reshape((2,) * many + piece.shape[1:]) for piece in (block[:, :cut], block[:, cut:])
        ]

    def step(self, place):
        self.pairs = []
        for half, route in zip(self.halves, self.routes):
            bit = route[place]
            side = (lax.axis_index("expert") >> bit) & 1
            dim = self.many - bit
            stays = lax.dynamic_slice_in_dim(half, side, 1, dim)
            goes = lax.dynamic_slice_in_dim(half, 1 - side, 1, dim)
            self.pairs.append((stays, swapped(goes, "expert", 1 << bit)))
        return self.pairs

    def add(self):
        self.halves = [added(*pair) for pair in self.pairs]

    def whole(self):
        return jnp.concatenate([half.reshape(half.shape[self.many :]) for half in self.halves], axis=0)


def group_parts(block):
    count = lax.axis_size("dp")
    mine = lax.axis_index("dp")
    parts = block.reshape(count, -1, block.shape[-1])

    def part(place):
        return lax.dynamic_index_in_dim(parts, place, 0, keepdims=False)

    return [part(mine)] + [swapped(part(mine ^ mask), "dp", mask) for mask in range(1, count)]


def group_blocks(share):
    return [share] + [swapped(share, "dp", mask) for mask in range(1, lax.axis_size("dp"))]


def joined_groups(seen):
    mine = lax.axis_index("dp")
    blocks = []
    for place in range(len(seen)):
        block = seen[0]
        for mask in range(1, len(seen)):
            block = jnp.where(mine ^ mask == place, seen[mask], block)
        blocks.append(block)
    return jnp.concatenate(blocks, axis=0)


class Spread:
    def __init__(self, block):
        many = len(bits_of("expert")) - 1
        cut = block.shape[0] // 2
        self.many = many
        self.routes = [[*range(many, 0, -1)], [*range(1, many + 1)]]
        self.halves = [
            piece.reshape((1,) * many + piece.shape) for piece in (block[:cut], block[cut:])
        ]

    def step(self, place):
        self.halves = [
            doubled(half, "expert", route[place], self.many - route[place])
            for half, route in zip(self.halves, self.routes)
        ]
        return self.halves

    def whole(self):
        blocks = [half.reshape((-1,) + half.shape[self.many :]) for half in self.halves]
        return jnp.concatenate(blocks, axis=1)


def body(
    layer_input,
    norm1_gain,
    w_in,
    conv_weight,
    conv_bias,
    w_xproj,
    w_dt,
    dt_bias,
    a_log,
    d_skip,
    w_out,
    norm2_gain,
    router_weight,
    w_up,
    w_down,
    expert_route,
    capacity,
    output_grad,
):
    seq_count, span_len, model_width = layer_input.shape
    inner_width = w_in.shape[1] // 2
    conv_taps = conv_weight.shape[0]
    rank_dt = w_dt.shape[0]
    state_width = a_log.shape[1]
    experts_all = router_weight.shape[1]
    tokens = seq_count * span_len
    groups, holders = (lax.axis_size("dp"), lax.axis_size("expert"))
    slot_count = max(2, 5 * tokens // (4 * experts_all))
    slots = experts_all * slot_count
    far = max(1, groups // 2)
    w_masks = range(1, far)
    mine = lax.axis_index("expert").astype(jnp.int32).reshape(1)
    reach = 8

    core = mine & 1

    def traded(placed):
        blocks = placed.reshape(experts_all, slot_count, model_width)
        return exchanged(blocks, "expert").reshape(slots, model_width)

    rim = shifted(layer_input[:, span_len - reach :], "expert", 1)
    pick, placed, choose, counts = route(
        expert_route, capacity, after(output_grad, rim), slot_count
    )
    og_own = traded(placed)
    up_mats = [w_up[0]] + [swapped(w_up[0], "dp", mask) for mask in w_masks]
    down_mats = [w_down[0]] + [swapped(w_down[0], "dp", mask) for mask in w_masks]
    router_t = router_weight.T

    normed, conv_in, gate_z, pre_conv, act, sel, selt, dt_pre, step, rate2, ends = front(
        layer_input, rim, norm1_gain, w_in, conv_weight, conv_bias, w_xproj.T, w_dt, dt_bias, a_log.T
    )
    og_own, ends = together(og_own, ends)
    og_other = swapped(og_own, "dp", far)
    every = lax.all_gather(ends, "expert")
    saved, y_full, gated, stream_two, gate_prob, placed = middle(
        mine, every, step, act, sel, selt, rate2, d_skip, gate_z, layer_input, w_out, norm2_gain, pick, choose,
        router_t,
    )
    placed, og_other, up_mats, down_mats = together(placed, og_other, up_mats, down_mats)

    row_own = traded(placed)
    row_other = swapped(row_own, "dp", far)
    fwd_a, bwd_a, grd_a, log_a, hid_a, pre_a = expert_rows(
        mine, row_own, og_own, router_t, up_mats, down_mats, bf16
    )
    near_rows = traded(fwd_a)
    row_other, bwd_a, near_rows = together(row_other, bwd_a, near_rows)
    fwd_b, bwd_b, grd_b, log_b, hid_b, pre_b = expert_rows(
        mine, row_other, og_other, router_t, up_mats, down_mats, bf16
    )
    bwd_back = swapped(bwd_b, "dp", far)
    up_grad, down_grad, lows, router_grad = expert_grads(
        (row_own, row_other), (grd_a, grd_b), (log_a, log_b), (hid_a, hid_b), (pre_a, pre_b)
    )
    far_rows = traded(fwd_b)
    bwd_back, router_grad, far_rows = together(bwd_back, router_grad, far_rows)
    got = traded(added(bwd_a, bwd_back))

    stream_two_grad, mix_grad, gain_two_grad, y_grad, z_grad, skip_grad = back(
        got, pick, stream_two, norm2_gain, output_grad, w_out, gate_z, y_full, act
    )
    far_rows = swapped(far_rows, "dp", far)
    mix_grad, far_rows = together(mix_grad, far_rows)

    def back_from(piece, *others):
        return [swapped(after(low, *others), "dp", mask) for low, mask in zip(lows[piece], w_masks)]

    early, sent = early_pack(
        core, mix_grad, gated.reshape(tokens, inner_width), normed, z_grad.reshape(tokens, inner_width), holders
    )
    y_grad, sent = together(y_grad, sent)
    came = swapped(sent, "expert", 1)
    head = head_of(y_grad, step, selt, rate2)
    head, came = together(head, came)
    backs = [back_from(0, y_grad)]
    heads = lax.all_gather(head, "expert", tiled=False)
    heads, early, came, backs[0] = together(heads, early, came, backs[0])
    backs += [back_from(1, heads), back_from(2, heads)]
    first = Gather(added(early, came))
    pre_grads = []
    for seq in range(seq_count):
        if seq < first.many:
            first.step(seq)
        pre_grad, rim_rows, small = scan_back(
            conv_taps, seq, mine, heads, every, step, act, y_grad, sel, selt, rate2, saved, dt_pre, w_dt,
            w_xproj.T, d_skip, pre_conv, conv_in, (small, rim_rows) if seq else (),
        )
        pre_grads.append(pre_grad)
        if seq < first.many:
            rim_rows, heads, first.pairs = together(rim_rows, heads, first.pairs)
            first.add()
        if seq == 0:
            rim_rows, heads, *backs[1:] = together(rim_rows, heads, *backs[1:])
            backs.append(back_from(3, heads))
    for place in range(seq_count, first.many):
        first.step(place)
        first.add()
    rim_rows, backs[3] = together(rim_rows, backs[3])
    rims = shifted(rim_rows, "expert", -1)
    parts = group_parts(first.whole())
    in_rows = model_width // holders * (inner_width // model_width)
    lines = inner_width // model_width * small.shape[0] + 8 + experts_all
    srows = -(-lines // (16 * holders)) * 16
    srows += -(in_rows + srows) % (8 * groups)
    late, sent, grad_input = finish(
        core, pre_grads, rims, conv_weight, z_grad, w_in, layer_input, norm1_gain, normed,
        stream_two_grad, small, skip_grad, gain_two_grad, counts, router_grad, (holders, srows),
    )
    parts, late, sent = together(parts, late, sent)

    came = swapped(sent, "expert", 1)
    many = len(bits_of("dp"))
    share = added(*parts)
    block = share.reshape((1,) * many + share.shape)
    bits = [*reversed(bits_of("dp"))]
    last = Gather(added(late, came))
    for place in range(last.many):
        last.step(place)
        if bits:
            bit = bits.pop(0)
            block = doubled(block, "dp", bit, many - 1 - bit)
        last.pairs, block = together(last.pairs, block)
        last.add()
    for bit in bits:
        block = doubled(block, "dp", bit, many - 1 - bit)
    parts = group_parts(last.whole())
    spread = Spread(block.reshape(-1, model_width))
    parts, *spread.halves = together(parts, *spread.step(0))
    seen = group_blocks(added(*parts))
    for place in range(1, spread.many):
        spread.step(place)
    seen, *spread.halves = together(seen, *spread.halves)
    early = spread.whole()
    early_far = swapped(early, "expert", 1)
    spread = Spread(joined_groups(seen))
    grad_w_up = up_grad
    for pair in zip(*backs[:2]):
        grad_w_up = grad_w_up + jnp.concatenate(pair, axis=0).astype(f32)
    early, early_far, grad_w_up, *spread.halves = together(
        early, early_far, grad_w_up, *spread.step(0)
    )
    for place in range(1, spread.many):
        spread.step(place)
    grad_w_in, grad_w_out = unpack_early(core, early, early_far, 2 * inner_width)
    grad_w_down = down_grad
    for pair in zip(*backs[2:]):
        grad_w_down = grad_w_down + jnp.concatenate(pair, axis=0).astype(f32)
    result = blend(pick, near_rows, far_rows, gate_prob, stream_two)
    grad_w_in, grad_w_down, result, *spread.halves = together(
        grad_w_in, grad_w_down, result, *spread.halves
    )
    late = spread.whole()
    late_far = swapped(late, "expert", 1)
    grad_w_in, wx_grad, wdt_grad, alog_grad, conv_grad, *vectors, expert_loads = unpack_late(
        core, late, late_far, grad_w_in, (sel.shape[2], rank_dt, state_width, conv_taps), experts_all,
        tokens.bit_length(), experts_all / (tokens * groups * holders),
    )
    conv_b_grad, dt_b_grad, skip_grad, gain_one, gain_two, router_grad = vectors
    return (
        result,
        grad_input,
        gain_one,
        grad_w_in,
        conv_grad,
        conv_b_grad,
        wx_grad.T,
        wdt_grad,
        dt_b_grad,
        alog_grad.T,
        skip_grad,
        grad_w_out,
        gain_two,
        router_grad.T,
        grad_w_up[None],
        grad_w_down[None],
        expert_loads,
    )


def solution(mesh):
    in_specs = (
        P("dp", "expert", None),
        P(),
        P(),
        P(),
        P(),
        P(),
        P(),
        P(),
        P(),
        P(),
        P(),
        P(),
        P(),
        P("expert", None, "dp"),
        P("expert", "dp", None),
        P("dp", "expert"),
        P(),
        P("dp", "expert", None),
    )
    out_specs = (
        P("dp", "expert", None),
        P("dp", "expert", None),
        P(),
        P(),
        P(),
        P(),
        P(),
        P(),
        P(),
        P(),
        P(),
        P(),
        P(),
        P(),
        P("expert", None, "dp"),
        P("expert", "dp", None),
        P(),
    )
    return jax.shard_map(body, mesh=mesh, in_specs=in_specs, out_specs=out_specs, check_vma=False)
```

```python
import jax
import jax.numpy as jnp
from jax import lax
from jax.experimental import pallas as pl
from jax.experimental.pallas import tpu as pltpu
from jax.sharding import PartitionSpec as P

f32 = jnp.float32
bf16 = jnp.bfloat16
LN = 128
SUB = 16
GROUP = 4
BG = 2
EPSILON = 1e-05
LOG2E = 1.4426950408889634
NT = (((1,), (1,)), ((), ()))
TN = (((0,), (0,)), ((), ()))
VM = pl.BlockSpec(memory_space=pltpu.VMEM)
SM = pl.BlockSpec(memory_space=pltpu.SMEM)
HB = pl.BlockSpec(memory_space=pltpu.HBM)


class Copies:
    def __init__(self, sems):
        self.sems = sems
        self.count = 0
        self.under_way = []

    def start(self, source, target):
        copy = pltpu.make_async_copy(source, target, self.sems.at[self.count])
        self.count += 1
        copy.start()
        self.under_way.append(copy)
        return copy

    def arrived(self, copy):
        copy.wait()
        self.under_way.remove(copy)

    def wait(self):
        while self.under_way:
            self.under_way.pop().wait()


FRONT, MIDDLE, BACK, SCAN, FINISH = (28, 30, 34, 32, 28)


def params(mib=24):
    return pltpu.CompilerParams(vmem_limit_bytes=mib << 20)


def shape_of(shape, dtype):
    return jax.ShapeDtypeStruct(shape, dtype)


def in_hbm(shape, dtype):
    return pltpu.HBM(shape, dtype)


def pinned(*values):
    return [pltpu.with_memory_space_constraint(value, pltpu.HBM) for value in values]


def dot(left, right):
    return jnp.dot(left, right, preferred_element_type=f32)


def dot_nt(left, right):
    return lax.dot_general(left, right, NT, preferred_element_type=f32)


def dot_tn(left, right):
    return lax.dot_general(left, right, TN, preferred_element_type=f32)


def spread_lanes(table, out_ref):
    ns, span = table.shape
    for t in range(span):
        out_ref[t] = jnp.broadcast_to(table[:, t : t + 1], (ns, LN))


def row_of(block, i, ns):
    return jnp.broadcast_to(block[i : i + 1], (ns, LN))


def tile_of(ref, seq, t0, j):
    return ref[seq, pl.ds(pl.multiple_of(t0, SUB), SUB), j * LN : (j + 1) * LN].astype(f32)


def tile_groups(tiles, size):
    return [range(g, min(g + size, tiles)) for g in range(0, tiles, size)]


def block_diagonal(part):
    ns = part.shape[1]
    lane = lax.broadcasted_iota(jnp.int32, (ns, SUB * ns), 1)
    copy = ((lane & (ns - 1)) == lax.broadcasted_iota(jnp.int32, (ns, SUB * ns), 0)).astype(bf16)
    high = part.astype(bf16)
    low = (part - high.astype(f32)).astype(bf16)
    block = lax.broadcasted_iota(jnp.int32, (SUB, SUB * ns), 1) // ns
    own = block == lax.broadcasted_iota(jnp.int32, (SUB, SUB * ns), 0)
    pieces = [jnp.where(own, dot(half, copy), 0.0) for half in (high, low)]
    return jnp.concatenate(pieces, axis=0).astype(bf16)


def silu_slope(values):
    logistic = jax.nn.sigmoid(values)
    return logistic * (1.0 + values * (1.0 - logistic))


def inverse_rms(values):
    return lax.rsqrt(jnp.mean(values * values, axis=-1, keepdims=True) + EPSILON)


def norm_backward(values, gain_vec, inv_rms, upstream):
    normal = values * inv_rms
    weighted = upstream * gain_vec
    mean = jnp.mean(weighted * normal, axis=-1, keepdims=True)
    return (
        inv_rms * (weighted - normal * mean),
        jnp.sum(upstream * normal, axis=0, keepdims=True),
    )


def route(expert_route, capacity, og, slot_count):
    s, t = expert_route.shape
    experts = capacity.shape[0]
    d = og.shape[2]
    tokens = s * t
    slots = experts * slot_count
    digits = tokens.bit_length()

    def kernel(
        cap_from, route_from, og_from, pick_to, placed_ref, choose_to, count_to,
        cap_ref, route_ref, og_ref, pick_ref, choose_ref, count_ref, sems,
    ):
        copies = Copies(sems)
        loads = [
            copies.start(source, target)
            for source, target in ((cap_from, cap_ref), (route_from, route_ref), (og_from, og_ref))
        ]
        copies.arrived(loads[0])
        copies.arrived(loads[1])
        flat = jnp.concatenate([route_ref[k : k + 1] for k in range(s)], axis=1)
        rows = lax.broadcasted_iota(jnp.int32, (LN, tokens), 0)
        choose = (rows == flat).astype(f32)
        earlier = lax.broadcasted_iota(jnp.int32, (tokens, tokens), 0)
        earlier = earlier < lax.broadcasted_iota(jnp.int32, (tokens, tokens), 1)
        rank = dot(choose.astype(bf16), earlier.astype(bf16))
        rank = jnp.sum(rank * choose, axis=0, keepdims=True).astype(jnp.int32)
        slot_limit = cap_ref[...].reshape(1, experts).astype(f32).astype(bf16)
        limit = dot(slot_limit, choose[:experts].astype(bf16)).astype(jnp.int32)
        kept = rank < limit
        target = jnp.where(kept, flat * slot_count + rank, slots)
        pick = lax.broadcasted_iota(jnp.int32, (slots, tokens), 0) == target
        pick = pick.astype(f32).astype(bf16)
        pick_ref[...] = pick
        copies.start(pick_ref, pick_to)
        copies.arrived(loads[2])
        every = jnp.concatenate([og_ref[k] for k in range(s)], axis=0)
        placed_ref[...] = dot(pick, every).astype(bf16)
        choose_ref[...] = choose.T[:, :experts]
        copies.start(choose_ref, choose_to)
        kept = kept.astype(f32)
        low = choose[:experts].astype(bf16)
        lines = [dot_nt(v.astype(bf16), low) for v in (kept, 1.0 - kept)]
        count = jnp.concatenate(lines, axis=1).astype(jnp.int32)
        lines = [((count >> k) & 1).astype(f32) for k in range(digits)]
        lines.append(jnp.zeros((1, d - 2 * experts * digits), f32))
        count_ref[...] = jnp.concatenate(lines, axis=1)
        copies.start(count_ref, count_to)
        copies.wait()

    return pl.pallas_call(
        kernel,
        out_shape=(
            in_hbm((slots, tokens), bf16),
            shape_of((slots, d), bf16),
            in_hbm((tokens, experts), f32),
            in_hbm((1, d), f32),
        ),
        in_specs=[HB] * 3,
        out_specs=(HB, VM, HB, HB),
        scratch_shapes=[
            pltpu.VMEM((experts,), jnp.int32),
            pltpu.VMEM((s, t), jnp.int32),
            pltpu.VMEM((s, t, d), bf16),
            pltpu.VMEM((slots, tokens), bf16),
            pltpu.VMEM((tokens, experts), f32),
            pltpu.VMEM((1, d), f32),
            pltpu.SemaphoreType.DMA((6,)),
        ],
        compiler_params=params(),
    )(*pinned(capacity, expert_route, og))


def front_kernel(
    x_from, rim_ref, gain_from, win_from, cw_from, cb_from, wxt_from, wdt_from, dtb_from, alog_from,
    normed_to, conv_to, gate_to, pre_to, act_to, sel_to, selt_to, dtp_to, step_to,
    rate_to, send_ref, bb_ref, cum_ref, rate_ref,
    win_ref, normed_ref, conv_ref, gate_ref, pre_ref, act_ref, dtp_ref, step_ref, sel_ref, selt_ref,
    x_ref, gain_ref, cw_ref, cb_ref, wxt_ref, wdt_ref, dtb_ref, alog_ref, sems,
):
    copies = Copies(sems)
    loads = [
        copies.start(source, target)
        for source, target in (
            (x_from, x_ref), (gain_from, gain_ref), (cw_from, cw_ref), (cb_from, cb_ref),
            (wxt_from, wxt_ref), (wdt_from, wdt_ref), (dtb_from, dtb_ref), (alog_from, alog_ref),
        )
    ]
    seqs, span, model = x_ref.shape
    width = cw_ref.shape[1]
    taps = cw_ref.shape[0]
    rim = rim_ref.shape[1]
    ns = rate_ref.shape[0]
    rank = wdt_ref.shape[0]
    cols = 512
    halves = [
        copies.start(win_from.at[:, cut], win_ref.at[:, cut])
        for cut in (slice(0, width), slice(width, 2 * width))
    ]
    for load in loads:
        copies.arrived(load)
    gain = gain_ref[...].reshape(1, -1)
    conv_b = cb_ref[...].reshape(1, -1)
    dt_b = dtb_ref[...].reshape(1, -1)
    rate_ref[...] = jnp.exp(alog_ref[...]) * (-LOG2E)
    copies.start(rate_ref, rate_to)
    rows = []
    for ref in (x_ref, rim_ref):
        for seq in range(seqs):
            v = ref[seq].astype(f32)
            rows.append((v * inverse_rms(v) * gain).astype(bf16))
    for seq in range(seqs):
        normed_ref[seq * span : (seq + 1) * span] = rows[seq]
    copies.start(normed_ref, normed_to)
    every = jnp.concatenate(rows, axis=0)
    copies.arrived(halves[0])
    for c in range(0, width, cols):
        cut = slice(c, c + cols)
        r = dot(every, win_ref[:, cut]).astype(bf16)
        for seq in range(seqs):
            main = r[seq * span : (seq + 1) * span]
            edge = r[seqs * span + seq * rim : seqs * span + (seq + 1) * rim]
            conv_ref[seq, :rim, cut] = edge
            conv_ref[seq, rim:, cut] = main
            v = jnp.concatenate([edge, main], axis=0).astype(f32)
            pre = conv_b[:, cut]
            for k in range(taps):
                first = rim - taps + 1 + k
                pre = pre + cw_ref[k : k + 1, cut] * v[first : first + span]
            pre_ref[seq, :, cut] = pre
            act_ref[seq, :, cut] = (pre * jax.nn.sigmoid(pre)).astype(bf16)
    for source, target in ((conv_ref, conv_to), (pre_ref, pre_to), (act_ref, act_to)):
        copies.start(source, target)
    own = every[: seqs * span]
    copies.arrived(halves[1])
    for c in range(width, 2 * width, cols):
        r = dot(own, win_ref[:, c : c + cols])
        for seq in range(seqs):
            gate_ref[seq, :, c - width : c - width + cols] = r[seq * span : (seq + 1) * span]
    copies.start(gate_ref, gate_to)
    for seq in range(seqs):
        sel = dot_nt(act_ref[seq], wxt_ref[...])
        sel_ref[seq] = sel
        lanes = sel.shape[1]
        wide = jnp.concatenate([sel, jnp.zeros((span, -lanes % LN), f32)], axis=1)
        selt = wide.T[:lanes]
        selt_ref[seq] = selt
        low = sel[:, :rank].astype(bf16)
        for c in range(0, width, cols):
            cut = slice(c, c + cols)
            pre = dot(low, wdt_ref[:, cut]) + dt_b[:, cut]
            dtp_ref[seq, :, cut] = pre
            step = jnp.maximum(pre, 0.0) + jnp.log1p(jnp.exp(-jnp.abs(pre)))
            step_ref[seq, :, cut] = step
            cum_ref[seq : seq + 1, cut] = jnp.sum(step, axis=0, keepdims=True)
        if seq == seqs - 1:
            copies.start(sel_ref, sel_to)
            copies.start(selt_ref, selt_to)
        copies.start(dtp_ref.at[seq], dtp_to.at[seq])
        copies.start(step_ref.at[seq], step_to.at[seq])
        spread_lanes(selt[rank : rank + ns], bb_ref)
        tiles = width // LN

        def chunk(k, state):
            t0 = k * SUB
            state = list(state)
            for group in tile_groups(tiles, GROUP):
                dt = {j: tile_of(step_ref, seq, t0, j) for j in group}
                dx = {j: dt[j] * tile_of(act_ref, seq, t0, j) for j in group}
                for i in range(SUB):
                    b = bb_ref[t0 + i]
                    for j in group:
                        rate = rate_ref[:, j * LN : (j + 1) * LN]
                        decay = jnp.exp2(row_of(dt[j], i, ns) * rate)
                        state[j] = decay * state[j] + row_of(dx[j], i, ns) * b
            return tuple(state)

        state = lax.fori_loop(
            0, span // SUB, chunk, tuple(jnp.zeros((ns, LN), f32) for _ in range(tiles))
        )
        for j in range(tiles):
            cut = slice(j * LN, (j + 1) * LN)
            send_ref[seq * ns : (seq + 1) * ns, cut] = state[j].astype(bf16)
    cum = cum_ref[...]
    high = cum.astype(bf16).astype(f32)
    tail = [high, cum - high, jnp.zeros((8 - 2 * seqs, width), f32)]
    send_ref[seqs * ns :, :] = jnp.concatenate(tail, axis=0).astype(bf16)
    copies.wait()


def front(x, rim, gain, w_in, conv_w, conv_b, wx_t, w_dt, dt_b, alog_t):
    s, t, d = x.shape
    w = conv_w.shape[1]
    n = alog_t.shape[0]
    k = wx_t.shape[0]
    return pl.pallas_call(
        front_kernel,
        out_shape=(
            in_hbm((s * t, d), bf16),
            in_hbm((s, rim.shape[1] + t, w), bf16),
            in_hbm((s, t, w), f32),
            in_hbm((s, t, w), f32),
            in_hbm((s, t, w), bf16),
            in_hbm((s, t, k), f32),
            in_hbm((s, k, t), f32),
            in_hbm((s, t, w), f32),
            in_hbm((s, t, w), f32),
            in_hbm((n, w), f32),
            shape_of((s * n + 8, w), bf16),
        ),
        in_specs=[HB, VM] + [HB] * 8,
        out_specs=(HB,) * 10 + (VM,),
        scratch_shapes=[
            pltpu.VMEM((t, n, LN), f32),
            pltpu.VMEM((s, w), f32),
            pltpu.VMEM((n, w), f32),
            pltpu.VMEM(w_in.shape, bf16),
            pltpu.VMEM((s * t, d), bf16),
            pltpu.VMEM((s, rim.shape[1] + t, w), bf16),
            pltpu.VMEM((s, t, w), f32),
            pltpu.VMEM((s, t, w), f32),
            pltpu.VMEM((s, t, w), bf16),
            pltpu.VMEM((s, t, w), f32),
            pltpu.VMEM((s, t, w), f32),
            pltpu.VMEM((s, t, k), f32),
            pltpu.VMEM((s, k, t), f32),
        ]
        + [pltpu.VMEM(v.shape, v.dtype) for v in (x, gain, conv_w, conv_b, wx_t, w_dt, dt_b, alog_t)]
        + [
            pltpu.SemaphoreType.DMA((18 + 2 * s,)),
        ],
        compiler_params=params(FRONT),
    )(*pinned(x), rim, *pinned(gain, w_in, conv_w, conv_b, wx_t, w_dt, dt_b, alog_t))


def carry_of(every_ref, rate_ref, seq, seqs, place, stop, step):
    ns, width = rate_ref.shape
    count = jnp.maximum((stop - place) * step, 0)

    def join(u, total):
        block = every_ref[place + u * step].astype(f32)
        row = seqs * ns + seq
        cum = block[row : row + 1] + block[row + seqs : row + seqs + 1]
        return jnp.exp2(rate_ref[...] * cum) * total + block[seq * ns : (seq + 1) * ns]

    return lax.fori_loop(0, count, join, jnp.zeros((ns, width), f32))


def middle_kernel(
    mine_ref, every_ref, step_ref, act_ref, sel_ref, selt_ref, rate_ref, skip_ref, gate_ref,
    x_ref, wout_from, gain_ref, pick_ref, choose_ref, router_ref,
    h_to, y_ref, gated_ref, two_ref, prob_ref, placed_ref, bb_ref, st_ref, acc_ref,
    wout_ref, first_ref, h_ref, sems,
):
    _, span, width = step_ref.shape
    ns = rate_ref.shape[0]
    rank = sel_ref.shape[2] - 2 * ns
    tiles = width // LN
    seqs = pick_ref.shape[1] // span
    mine = mine_ref[0]
    this = pl.program_id(0)
    wout = pltpu.make_async_copy(wout_from, wout_ref, sems.at[0])

    @pl.when(this == 0)
    def _():
        wout.start()

    skip = skip_ref[...].reshape(1, -1)
    for seq in range(seqs):

        @pl.when(pl.program_id(0) == seq)
        def _():
            st_ref[...] = carry_of(every_ref, rate_ref, seq, seqs, 0, mine, 1)

    spread_lanes(selt_ref[0, rank : rank + ns], bb_ref)
    first_ref[...] = st_ref[...].astype(bf16)
    first = pltpu.make_async_copy(first_ref, h_to.at[this, 0:ns, :], sems.at[1])
    first.start()

    def saving(k):
        at = pl.ds(pl.multiple_of((k * SUB + 1) * ns, ns), SUB * ns)
        slot = k & 1
        return pltpu.make_async_copy(h_ref.at[slot], h_to.at[this, at, :], sems.at[2 + slot])

    def chunk(k, carry):
        t0 = k * SUB
        slot = k & 1
        rows = pl.ds(pl.multiple_of(t0, SUB), SUB)

        @pl.when(k >= 2)
        def _():
            saving(k - 2).wait()

        for group in tile_groups(tiles, GROUP):
            state = {j: st_ref[:, j * LN : (j + 1) * LN] for j in group}
            dt = {j: tile_of(step_ref, 0, t0, j) for j in group}
            dx = {j: dt[j] * tile_of(act_ref, 0, t0, j) for j in group}
            for i in range(SUB):
                b = bb_ref[t0 + i]
                for j in group:
                    cut = slice(j * LN, (j + 1) * LN)
                    decay = jnp.exp2(row_of(dt[j], i, ns) * rate_ref[:, cut])
                    state[j] = decay * state[j] + row_of(dx[j], i, ns) * b
                    h_ref[slot, i * ns : (i + 1) * ns, cut] = state[j].astype(bf16)
            for j in group:
                st_ref[:, j * LN : (j + 1) * LN] = state[j]
        diag = block_diagonal(sel_ref[0, rows, rank + ns :])
        saving(k).start()
        r = dot(diag, h_ref[slot])
        y_ref[0, rows, :] = r[:SUB] + r[SUB:] + skip * act_ref[0, rows, :].astype(f32)
        return carry

    chunks = span // SUB
    lax.fori_loop(0, chunks, chunk, 0)
    gate = gate_ref[0]
    gated = (y_ref[0] * (gate * jax.nn.sigmoid(gate))).astype(bf16)
    gated_ref[0] = gated

    @pl.when(this == 0)
    def _():
        wout.wait()

    two = x_ref[0].astype(f32) + dot(gated, wout_ref[...])
    two_ref[0] = two
    moe = (two * inverse_rms(two) * gain_ref[...].reshape(1, -1)).astype(bf16)
    logits = dot_nt(moe, router_ref[...])
    raised = jnp.exp(logits - jnp.max(logits, axis=1, keepdims=True))
    chosen = jnp.sum(raised * choose_ref[...], axis=1, keepdims=True)
    prob_ref[0] = chosen / jnp.sum(raised, axis=1, keepdims=True)
    for seq in range(seqs):

        @pl.when(pl.program_id(0) == seq)
        def _():
            part = dot(pick_ref[:, seq * span : (seq + 1) * span], moe)
            if seq:
                part = part + acc_ref[...]
            if seq < seqs - 1:
                acc_ref[...] = part
            else:
                placed_ref[...] = part.astype(bf16)

    first.wait()
    for k in range(max(0, chunks - 2), chunks):
        saving(k).wait()


def by_sequence(*shape):
    return pl.BlockSpec((1,) + shape, lambda i: (i,) + (0,) * len(shape))


def whole(*shape):
    return pl.BlockSpec(shape, lambda i: (0,) * len(shape))


def middle(
    mine, every, step, act, sel, selt, rate2, skip, gate, x, w_out, gain, pick, choose, router_t
):
    s, t, w = step.shape
    n = rate2.shape[0]
    d = x.shape[2]
    k = sel.shape[2]
    return pl.pallas_call(
        middle_kernel,
        grid=(s,),
        out_shape=(
            in_hbm((s, (t + 1) * n, w), bf16),
            in_hbm((s, t, w), f32),
            in_hbm((s, t, w), bf16),
            in_hbm((s, t, d), f32),
            shape_of((s, t, 1), f32),
            shape_of((pick.shape[0], d), bf16),
        ),
        in_specs=[
            SM,
            whole(*every.shape),
            by_sequence(t, w),
            by_sequence(t, w),
            by_sequence(t, k),
            by_sequence(k, t),
            whole(n, w),
            whole(w),
            by_sequence(t, w),
            by_sequence(t, d),
            HB,
            whole(d),
            whole(*pick.shape),
            pl.BlockSpec((t, choose.shape[1]), lambda i: (i, 0)),
            whole(*router_t.shape),
        ],
        out_specs=(
            HB,
            by_sequence(t, w),
            by_sequence(t, w),
            by_sequence(t, d),
            by_sequence(t, 1),
            whole(pick.shape[0], d),
        ),
        scratch_shapes=[
            pltpu.VMEM((t, n, LN), f32),
            pltpu.VMEM((n, w), f32),
            pltpu.VMEM((pick.shape[0], d), f32),
            pltpu.VMEM((w, d), bf16),
            pltpu.VMEM((n, w), bf16),
            pltpu.VMEM((2, SUB * n, w), bf16),
            pltpu.SemaphoreType.DMA((4,)),
        ],
        compiler_params=params(MIDDLE),
    )(mine, every, *pinned(step, act, sel, selt, rate2, skip, gate, x, w_out, gain, pick, choose), router_t)


def gelu_pair(v):
    root = 0.7978845608028654
    square = v * v
    bend = jnp.tanh(root * (v + 0.044715 * v * square))
    half = 0.5 * (1.0 + bend)
    slope = half + 0.5 * v * (1.0 - bend * bend) * (root * (1.0 + 3.0 * 0.044715 * square))
    return v * half, slope


def expert_kernel(shares, own_ref, rows_ref, og_ref, router_ref, *refs):
    ups, downs, refs = (refs[:shares], refs[shares : 2 * shares], refs[2 * shares :])
    fwd_ref, bwd_ref = refs[:2]
    kept = 2 + 2 * shares
    targets, sources, sems = (refs[2 : 2 + kept], refs[2 + kept : 2 + 2 * kept], refs[-1])
    copies = Copies(sems)
    grd_ref, log_ref = sources[:2]
    hids, pres = (sources[2 : 2 + shares], sources[2 + shares :])
    rows = rows_ref[...]
    logits = dot_nt(rows, router_ref[...])
    top = jnp.max(logits, axis=1, keepdims=True)
    raised = jnp.exp(logits - top)
    probs = raised / jnp.sum(raised, axis=1, keepdims=True)
    own = (lax.broadcasted_iota(jnp.int32, (1, probs.shape[1]), 1) == own_ref[0]).astype(f32)
    gate = jnp.sum(probs * own, axis=1, keepdims=True)
    og = og_ref[...].astype(f32)
    grads = (og * gate).astype(bf16)
    grd_ref[...] = grads
    fwd, bwd = (0.0, 0.0)
    for up_ref, down_ref, hid_ref, pre_ref in zip(ups, downs, hids, pres):
        hidden, slope = gelu_pair(dot(rows, up_ref[...]))
        hidden = hidden.astype(bf16)
        hid_ref[...] = hidden
        fwd = fwd + dot(hidden, down_ref[...])
        pre = (dot_nt(grads, down_ref[...]) * slope).astype(bf16)
        pre_ref[...] = pre
        bwd = bwd + dot_nt(pre, up_ref[...])
    logit = jnp.sum(og * fwd, axis=1, keepdims=True) * gate * (own - probs)
    log_ref[...] = logit
    high = logit.astype(bf16)
    low = (logit - high.astype(f32)).astype(bf16)
    bwd = bwd + dot(high, router_ref[...]) + dot(low, router_ref[...])
    for source, target in zip(sources, targets):
        copies.start(source, target)
    fwd_ref[...] = fwd.astype(fwd_ref.dtype)
    bwd_ref[...] = bwd.astype(bwd_ref.dtype)
    copies.wait()


def expert_rows(own, rows, og, router, ups, downs, dtype):
    m, d = rows.shape
    f = ups[0].shape[1]
    shares = len(ups)

    def kernel(*refs):
        expert_kernel(shares, *refs)

    kept = [((m, d), bf16), ((m, router.shape[0]), f32)] + [((m, f), bf16)] * (2 * shares)
    outs = pl.pallas_call(
        kernel,
        out_shape=(shape_of((m, d), dtype), shape_of((m, d), dtype))
        + tuple(in_hbm(*one) for one in kept),
        in_specs=[SM] + [VM] * (3 + 2 * shares),
        out_specs=(VM, VM) + (HB,) * len(kept),
        scratch_shapes=[pltpu.VMEM(*one) for one in kept] + [pltpu.SemaphoreType.DMA((len(kept),))],
        compiler_params=params(),
    )(own, rows, og, router, *ups, *downs)
    return (*outs[:4], outs[4 : 4 + shares], outs[4 + shares :])


def deal(block_ref, keep_ref, send_ref, core, first, rows):
    for pair in range(keep_ref.shape[0]):
        for ref, side in ((keep_ref, core), (send_ref, 1 - core)):
            at = pl.ds(pl.multiple_of((2 * pair + side) * rows, rows), rows)
            ref[pair, first : first + rows, :] = block_ref[at, :]


def back(core, got, pick, two, gain, og, w_out, gate, y, act, gated, normed, holders):
    s, t, w = y.shape
    d = two.shape[2]
    out_rows, in_rows, pieces = (w // holders, d // holders, w // d)

    def kernel(
        core_ref, got_ref, pick_from, two_from, gain_ref, og_from, wout_from, gate_from, y_from, act_from, gated_from,
        normed_from,
        twog_to, gain2_ref, yg_to, zg_to, skipg_ref, keep_ref, send_ref, yg_ref,
        wout_ref, gate_ref, y_ref, act_ref, twog_ref, zg_ref, pick_ref, two_ref, og_ref, gated_ref, normed_ref,
        mix_ref, block_ref, sems,
    ):
        cols = 512
        copies = Copies(sems)
        firsts = [
            copies.start(source, target)
            for source, target in ((pick_from, pick_ref), (two_from, two_ref), (og_from, og_ref))
        ]
        loads = [
            copies.start(source, target)
            for source, target in (
                (wout_from, wout_ref), (gate_from, gate_ref), (act_from, act_ref), (y_from, y_ref)
            )
        ]
        lasts = [copies.start(gated_from.at[k], gated_ref.at[k * t : (k + 1) * t]) for k in range(s)]
        lasts.append(copies.start(normed_from, normed_ref))
        for load in firsts:
            copies.arrived(load)
        moe_grad = dot_tn(pick_ref[...], got_ref[...])
        gain = gain_ref[...].reshape(1, -1)
        total = 0.0
        for seq in range(s):
            v = two_ref[seq]
            grad, gained = norm_backward(
                v, gain, inverse_rms(v), moe_grad[seq * t : (seq + 1) * t]
            )
            total = total + gained
            grad = grad + og_ref[seq].astype(f32)
            twog_ref[seq] = grad
            mix_ref[seq * t : (seq + 1) * t] = grad.astype(bf16)
        gain2_ref[...] = total
        copies.start(twog_ref, twog_to)
        for load in loads:
            copies.arrived(load)
        for c in range(0, w, cols):
            cut = slice(c, c + cols)
            r = dot_nt(mix_ref[...], wout_ref[cut, :])
            total = 0.0
            for seq in range(s):
                part = r[seq * t : (seq + 1) * t]
                gate = gate_ref[seq, :, cut]
                logistic = jax.nn.sigmoid(gate)
                yg = part * (gate * logistic)
                yg_ref[seq, :, cut] = yg
                slope = logistic * (1.0 + gate * (1.0 - logistic))
                zg = (part * y_ref[seq, :, cut] * slope).astype(bf16)
                zg_ref[seq * t : (seq + 1) * t, cut] = zg
                total = total + jnp.sum(yg * act_ref[seq, :, cut].astype(f32), axis=0, keepdims=True)
            skipg_ref[:, cut] = total
            copies.start(yg_ref.at[:, :, cut], yg_to.at[:, :, cut])
        for k in range(s):
            copies.start(zg_ref.at[k * t : (k + 1) * t], zg_to.at[k])
        for load in lasts:
            copies.arrived(load)
        block_ref[...] = dot_tn(gated_ref[...], mix_ref[...]).astype(bf16)
        deal(block_ref, keep_ref, send_ref, core_ref[0], 0, out_rows)
        for p in range(pieces):
            r = dot_tn(normed_ref[...], zg_ref[:, p * d : (p + 1) * d])
            block_ref[p * d : (p + 1) * d] = r.astype(bf16)
            side = block_ref.at[p * d : (p + 1) * d]
            deal(side, keep_ref, send_ref, core_ref[0], out_rows + p * in_rows, in_rows)
        copies.wait()

    packed = shape_of((holders // 2, out_rows + pieces * in_rows, d), bf16)
    return pl.pallas_call(
        kernel,
        out_shape=(
            in_hbm((s, t, d), f32),
            shape_of((1, d), f32),
            in_hbm((s, t, w), f32),
            in_hbm((s, t, w), bf16),
            shape_of((1, w), f32),
            packed,
            packed,
        ),
        in_specs=[SM, VM, HB, HB, VM] + [HB] * 7,
        out_specs=(HB, VM, HB, HB, VM, VM, VM),
        scratch_shapes=[
            pltpu.VMEM((s, t, w), f32),
            pltpu.VMEM((w, d), bf16),
            pltpu.VMEM((s, t, w), f32),
            pltpu.VMEM((s, t, w), f32),
            pltpu.VMEM((s, t, w), bf16),
            pltpu.VMEM((s, t, d), f32),
            pltpu.VMEM((s * t, w), bf16),
            pltpu.VMEM(pick.shape, bf16),
            pltpu.VMEM(two.shape, f32),
            pltpu.VMEM(og.shape, bf16),
            pltpu.VMEM((s * t, w), bf16),
            pltpu.VMEM(normed.shape, bf16),
            pltpu.VMEM((s * t, d), bf16),
            pltpu.VMEM((w, d), bf16),
            pltpu.SemaphoreType.DMA((9 + 2 * s + w // 512,)),
        ],
        compiler_params=params(BACK),
    )(core, got, *pinned(pick, two), gain, *pinned(og, w_out, gate, y, act, gated, normed))


def head_of(yg, step, selt, rate2):
    s, t, w = step.shape
    n = rate2.shape[0]
    tiles = w // LN

    def kernel(yg_from, step_from, selt_ref, rate_ref, head_ref, cb_ref, step_ref, yg_ref, sems):
        copies = Copies(sems)
        loads = [
            [
                copies.start(source.at[seq], target.at[seq])
                for source, target in ((step_from, step_ref), (yg_from, yg_ref))
            ]
            for seq in range(s)
        ]
        for seq in range(s):
            spread_lanes(selt_ref[seq, selt.shape[1] - n :], cb_ref)
            for load in loads[seq]:
                copies.arrived(load)

            def chunk(u, mu):
                t0 = t - SUB - u * SUB
                mu = list(mu)
                for group in tile_groups(tiles, GROUP):
                    dt = {j: tile_of(step_ref, seq, t0, j) for j in group}
                    yg = {j: tile_of(yg_ref, seq, t0, j) for j in group}
                    for i in reversed(range(SUB)):
                        c = cb_ref[t0 + i]
                        for j in group:
                            rate = rate_ref[:, j * LN : (j + 1) * LN]
                            decay = jnp.exp2(row_of(dt[j], i, n) * rate)
                            mu[j] = decay * (mu[j] + row_of(yg[j], i, n) * c)
                return tuple(mu)

            mu = lax.fori_loop(
                0, t // SUB, chunk, tuple(jnp.zeros((n, LN), f32) for _ in range(tiles))
            )
            for j in range(tiles):
                cut = slice(j * LN, (j + 1) * LN)
                head_ref[seq * n : (seq + 1) * n, cut] = mu[j].astype(bf16)

    return pl.pallas_call(
        kernel,
        out_shape=shape_of((s * n, w), bf16),
        in_specs=[HB, HB, VM, VM],
        out_specs=VM,
        scratch_shapes=[
            pltpu.VMEM((t, n, LN), f32),
            pltpu.VMEM((s, t, w), f32),
            pltpu.VMEM((s, t, w), f32),
            pltpu.SemaphoreType.DMA((2 * s,)),
        ],
        compiler_params=params(12),
    )(*pinned(yg, step), selt, rate2)


def scan_back_kernel(
    taps, seq, seqs, mine_ref, heads_ref, every_ref, step_ref, act_ref, yg_ref, sel_ref, selt_ref, rate_ref, h_from,
    dtp_from, wdt_from, wxt_from, skip_ref, pre_from, conv_from, *refs
):
    prior, refs = (refs[:2], refs[2:]) if seq else ((), refs)
    scan_back_run(
        taps, seq, seqs, mine_ref, heads_ref, every_ref, step_ref, act_ref, yg_ref, sel_ref, selt_ref, rate_ref,
        h_from, dtp_from, wdt_from, wxt_from, skip_ref, pre_from, conv_from, prior, *refs
    )


def scan_back_run(
    taps, seq, seqs, mine_ref, heads_ref, every_ref, step_ref, act_ref, yg_ref, sel_ref, selt_ref, rate_ref,
    h_from, dtp_from, wdt_from, wxt_from, skip_ref, pre_from, conv_from, prior,
    preg_ref, rim_ref, small_ref, cb_ref, mu_ref, al_ref, lam_ref, rdg_ref, s1_ref, adj_ref, ig_ref, og_ref,
    h_ref, dtp_ref, wdt_ref, wxt_ref, pre_ref, conv_ref, sems,
):
    chunks = step_ref.shape[1] // SUB

    def loading(v):
        at = pl.ds(pl.multiple_of((chunks - 1 - v) * SUB * rate_ref.shape[0], 8), h_ref.shape[1])
        return pltpu.make_async_copy(h_from.at[seq, at, :], h_ref.at[v & 1], sems.at[v & 1])

    loading(0).start()
    copies = Copies(sems.at[2:])
    for source, target in (
        (dtp_from.at[seq], dtp_ref), (wdt_from, wdt_ref), (wxt_from, wxt_ref), (pre_from.at[seq], pre_ref),
        (conv_from.at[seq], conv_ref),
    ):
        copies.start(source, target)
    _, span, width = step_ref.shape
    ns = rate_ref.shape[0]
    lanes = sel_ref.shape[2]
    rank = lanes - 2 * ns
    tiles = width // LN
    holders = heads_ref.shape[0]
    rim = conv_ref.shape[0] - span
    count = holders - 1 - mine_ref[0]

    def join(u, total):
        place = holders - 1 - u
        tail = every_ref[place].astype(f32)
        cum = tail[seq : seq + 1] + tail[seqs + seq : seqs + seq + 1]
        return jnp.exp2(rate_ref[...] * cum) * total + heads_ref[place].astype(f32)

    mu_ref[...] = lax.fori_loop(0, count, join, jnp.zeros((ns, width), f32))
    spread_lanes(selt_ref[0, rank + ns :], cb_ref)
    al_ref[...] = jnp.zeros((ns, width), f32)
    block = lax.broadcasted_iota(jnp.int32, (SUB, SUB * ns), 1) // ns
    ones = (block == lax.broadcasted_iota(jnp.int32, (SUB, SUB * ns), 0)).astype(bf16)

    def chunk(v, carry):
        k = chunks - 1 - v
        t0 = k * SUB
        slot = v & 1
        rows = pl.ds(pl.multiple_of(t0, SUB), SUB)

        @pl.when(v + 1 < chunks)
        def _():
            loading(v + 1).start()

        loading(v).wait()
        for group in tile_groups(tiles, BG):
            cuts = {j: slice(j * LN, (j + 1) * LN) for j in group}
            mu = {j: mu_ref[:, cuts[j]] for j in group}
            al = {j: al_ref[:, cuts[j]] for j in group}
            dts = {j: tile_of(step_ref, 0, t0, j) for j in group}
            ygs = {j: tile_of(yg_ref, 0, t0, j) for j in group}
            for i in reversed(range(SUB)):
                c = cb_ref[t0 + i]
                for j in group:
                    rate = rate_ref[:, cuts[j]]
                    dt = row_of(dts[j], i, ns)
                    decay = jnp.exp2(dt * rate)
                    lam = mu[j] + row_of(ygs[j], i, ns) * c
                    mu[j] = decay * lam
                    dg = mu[j] * h_ref[slot, i * ns : (i + 1) * ns, cuts[j]].astype(f32)
                    al[j] = al[j] + dt * dg
                    lam_ref[i * ns : (i + 1) * ns, cuts[j]] = lam.astype(bf16)
                    rdg_ref[i * ns : (i + 1) * ns, cuts[j]] = (rate * dg).astype(bf16)
            for j in group:
                mu_ref[:, cuts[j]] = mu[j]
                al_ref[:, cuts[j]] = al[j]
        lam = lam_ref[...]
        r = dot(block_diagonal(sel_ref[0, rows, rank : rank + ns]), lam)
        adj_ref[rows, :] = r[:SUB] + r[SUB:]
        s1_ref[rows, :] = dot(ones, rdg_ref[...]) * (1.0 / LOG2E)
        up = lax.broadcasted_iota(jnp.int32, (SUB * ns, SUB), 0) // ns
        own = up == lax.broadcasted_iota(jnp.int32, (SUB * ns, SUB), 1)
        dx = (step_ref[0, rows, :] * act_ref[0, rows, :].astype(f32)).astype(bf16)
        d = dot_nt(lam, dx)
        ig_ref[k] = jnp.sum(jnp.where(own, d, 0.0).reshape(SUB, ns, SUB), axis=0)
        d = dot_nt(h_ref[slot, ns:, :], yg_ref[0, rows, :].astype(bf16))
        og_ref[k] = jnp.sum(jnp.where(own, d, 0.0).reshape(SUB, ns, SUB), axis=0)
        return carry

    lax.fori_loop(0, chunks, chunk, 0)
    copies.wait()
    act = act_ref[0].astype(f32)
    adj = adj_ref[...]
    step = step_ref[0]
    dtg = (s1_ref[...] + adj * act) * jax.nn.sigmoid(dtp_ref[...])
    low = dtg.astype(bf16)
    grads = [dot_nt(wdt_ref[...], low)] + [
        jnp.concatenate([ref[k] for k in range(chunks)], axis=1) for ref in (ig_ref, og_ref)
    ]
    grads = jnp.concatenate(grads, axis=0).astype(bf16)
    at = 0

    def put(rows):
        nonlocal at
        cut = slice(at, at + rows.shape[0])
        small_ref[cut, :] = prior[0][cut, :] + rows if seq else rows
        at += rows.shape[0]

    put(dot(grads, act_ref[0]))
    put(dot(selt_ref[0, :rank].astype(bf16), low))
    put(rate_ref[...] * al_ref[...] * (1.0 / LOG2E))
    act_grad = yg_ref[0] * skip_ref[...].reshape(1, -1) + adj * step + dot_tn(grads, wxt_ref[...])
    pre_grad = act_grad * silu_slope(pre_ref[...])
    preg_ref[0] = pre_grad
    rim_ref[seq] = pre_grad[:rim].astype(bf16)
    for place in range(seq):
        rim_ref[place] = prior[1][place]
    inputs = conv_ref[...].astype(f32)
    tail = []
    for k in range(taps):
        first = rim - taps + 1 + k
        tail.append(jnp.sum(pre_grad * inputs[first : first + span], axis=0, keepdims=True))
    tail.append(jnp.sum(pre_grad, axis=0, keepdims=True))
    tail.append(jnp.sum(dtg, axis=0, keepdims=True))
    tail.append(jnp.zeros((8 - len(tail), width), f32))
    put(jnp.concatenate(tail, axis=0))


def scan_back(
    taps, seq, mine, heads, every, step, act, yg, sel, selt, rate2, h, dtp, w_dt, wx_t, skip, pre, conv,
    prior,
):
    s, t, w = step.shape
    n = rate2.shape[0]
    k = sel.shape[2]
    chunks = t // SUB
    rim = conv.shape[1] - t
    small = k + w_dt.shape[0] + n + 8

    def kernel(*refs):
        scan_back_kernel(taps, seq, s, *refs)

    def own(*shape):
        return pl.BlockSpec((1,) + shape, lambda i: (seq,) + (0,) * len(shape))

    return pl.pallas_call(
        kernel,
        grid=(1,),
        out_shape=(
            shape_of((1, t, w), f32),
            shape_of((s, rim, w), bf16),
            shape_of((small, w), f32),
        ),
        in_specs=[
            SM,
            pl.BlockSpec((heads.shape[0], n, w), lambda i: (0, seq, 0)),
            pl.BlockSpec((every.shape[0], 8, w), lambda i: (0, s * n // 8, 0)),
            own(t, w),
            own(t, w),
            own(t, w),
            own(t, k),
            own(k, t),
            whole(n, w),
            HB,
            HB,
            HB,
            HB,
            whole(w),
            HB,
            HB,
            *(whole(*value.shape) for value in prior),
        ],
        out_specs=(whole(1, t, w), whole(s, rim, w), whole(small, w)),
        scratch_shapes=[
            pltpu.VMEM((t, n, LN), f32),
            pltpu.VMEM((n, w), f32),
            pltpu.VMEM((n, w), f32),
            pltpu.VMEM((SUB * n, w), bf16),
            pltpu.VMEM((SUB * n, w), bf16),
            pltpu.VMEM((t, w), f32),
            pltpu.VMEM((t, w), f32),
            pltpu.VMEM((chunks, n, SUB), f32),
            pltpu.VMEM((chunks, n, SUB), f32),
            pltpu.VMEM((2, (SUB + 1) * n, w), bf16),
            pltpu.VMEM((t, w), f32),
            pltpu.VMEM(w_dt.shape, bf16),
            pltpu.VMEM(wx_t.shape, bf16),
            pltpu.VMEM((t, w), f32),
            pltpu.VMEM(conv.shape[1:], bf16),
            pltpu.SemaphoreType.DMA((7,)),
        ],
        compiler_params=params(SCAN),
    )(
        mine, heads, *pinned(every, step, act, yg, sel, selt, rate2, h, dtp, w_dt, wx_t, skip, pre, conv), *prior
    )


def expert_grads(rows, grds, logs, hids, pres):
    blocks = len(rows)
    shares = len(hids[0])
    d = rows[0].shape[1]
    f = hids[0][0].shape[1]
    flat = [*rows, *grds, *logs] + [v for group in (hids, pres) for block in group for v in block]

    def kernel(*refs):
        count, many = (len(flat), len(outs_shape))
        targets = refs[count : count + many]
        ins = refs[count + many : 2 * count + many]
        outs = refs[2 * count + many : 2 * (count + many)]
        copies = Copies(refs[-1])
        for source, target in zip(refs[:count], ins):
            copies.start(source, target)
        copies.wait()
        row, grd, log = (ins[k * blocks : (k + 1) * blocks] for k in range(3))
        hid = ins[3 * blocks : (3 + shares) * blocks]
        pre = ins[(3 + shares) * blocks :]

        def total(lefts, rights):
            parts = [dot_tn(left[...], right[...]) for left, right in zip(lefts, rights)]
            return sum(parts[1:], parts[0])

        at = 0
        for k in range(shares):
            for value in (total(row, pre[k::shares]), total(hid[k::shares], grd)):
                first = 0
                while first < value.shape[0]:
                    ref = outs[at]
                    ref[...] = value[first : first + ref.shape[0]].astype(ref.dtype)
                    copies.start(ref, targets[at])
                    first += ref.shape[0]
                    at += 1
        router = 0.0
        for log_ref, row_ref in zip(log, row):
            high = log_ref[...].astype(bf16)
            low = (log_ref[...] - high.astype(f32)).astype(bf16)
            router = router + dot_tn(high, row_ref[...]) + dot_tn(low, row_ref[...])
        outs[-1][...] = router
        copies.start(outs[-1], targets[-1])
        copies.wait()

    outs_shape = [((d, f), f32), ((f, d), f32)]
    for _ in range(1, shares):
        outs_shape += [((d // 2, f), bf16)] * 2
        outs_shape += [((f // 4, d), bf16), ((f - f // 4, d), bf16)]
    outs_shape.append(((logs[0].shape[1], d), f32))
    got = pl.pallas_call(
        kernel,
        out_shape=tuple(in_hbm(*one) for one in outs_shape),
        in_specs=[HB] * len(flat),
        out_specs=(HB,) * len(outs_shape),
        scratch_shapes=[pltpu.VMEM(v.shape, v.dtype) for v in flat]
        + [pltpu.VMEM(*one) for one in outs_shape]
        + [pltpu.SemaphoreType.DMA((len(flat) + len(outs_shape),))],
        compiler_params=params(),
    )(*pinned(*flat))
    return got[0], got[1], [got[2 + k : -1 : 4] for k in range(4)], got[-1]


def finish(
    core, preg, rim, conv_w, zg, w_in, x, gain, normed, twog, small, skipg, gain2, counts, router,
    plan,
):
    s = len(preg)
    _, t, w = preg[0].shape
    d = x.shape[2]
    holders, srows = plan
    taps = conv_w.shape[0]
    pieces, in_rows = (w // d, d // holders)

    def kernel(core_ref, *refs):
        preg_refs, refs = (refs[:s], refs[s:])
        run(core_ref, preg_refs, *refs)

    def run(
        core_ref, preg_refs, rim_ref, cw_ref, zg_from, win_from, x_from, gain_ref, normed_from, twog_from,
        small_from, skip_ref, gain2_ref, count_ref, router_ref,
        keep_ref, send_ref, input_to, cg_ref, pack_ref, block_ref,
        zg_ref, win_ref, x_ref, normed_ref, twog_ref, input_ref, sems,
    ):
        copies = Copies(sems)
        pack_ref[...] = jnp.zeros(pack_ref.shape, f32)
        tall = small_from.shape[0]
        first = copies.start(normed_from, normed_ref)
        loads = [copies.start(win_from, win_ref), copies.start(zg_from, zg_ref)]
        loads += [copies.start(x_from, x_ref), copies.start(twog_from, twog_ref)]
        smalls = [
            copies.start(
                small_from.at[:, p * d : (p + 1) * d], pack_ref.at[p * tall : (p + 1) * tall]
            )
            for p in range(pieces)
        ]
        cols = 512
        gain = gain_ref[...].reshape(1, -1)
        for seq in range(s):
            for c in range(0, w, cols):
                cut = slice(c, c + cols)
                v = jnp.concatenate(
                    [preg_refs[seq][0, :, cut], rim_ref[seq, :, cut].astype(f32)], axis=0
                )
                total = cw_ref[taps - 1 : taps, cut] * v[:t]
                for k in range(1, taps):
                    total = total + cw_ref[taps - 1 - k : taps - k, cut] * v[k : k + t]
                cg_ref[seq * t : (seq + 1) * t, cut] = total.astype(bf16)
        copies.arrived(first)
        for p in range(pieces):
            block_ref[:d] = dot_tn(normed_ref[...], cg_ref[:, p * d : (p + 1) * d]).astype(bf16)
            deal(block_ref, keep_ref, send_ref, core_ref[0], p * in_rows, in_rows)
        for load in loads:
            copies.arrived(load)
        gain1 = 0.0
        for seq in range(s):
            grad = dot_nt(cg_ref[seq * t : (seq + 1) * t], win_ref[:, :w])
            grad = grad + dot_nt(zg_ref[seq], win_ref[:, w:])
            v = x_ref[seq].astype(f32)
            grad, gained = norm_backward(v, gain, inverse_rms(v), grad)
            gain1 = gain1 + gained
            input_ref[seq] = twog_ref[seq] + grad
        copies.start(input_ref, input_to)
        for load in smalls:
            copies.arrived(load)
        at = pieces * tall
        lines = [skip_ref[:, p * d : (p + 1) * d] for p in range(pieces)] + [gain1, gain2_ref[...], count_ref[...]]
        for line in lines:
            pack_ref[at : at + 1] = line
            at += 1
        at += -at % 8
        pack_ref[at : at + router_ref.shape[0]] = router_ref[...]
        block_ref[: holders * srows] = pack_ref[...].astype(bf16)
        deal(block_ref, keep_ref, send_ref, core_ref[0], pieces * in_rows, srows)
        copies.wait()

    return pl.pallas_call(
        kernel,
        out_shape=(
            shape_of((holders // 2, pieces * in_rows + srows, d), bf16),
            shape_of((holders // 2, pieces * in_rows + srows, d), bf16),
            shape_of((s, t, d), f32),
        ),
        in_specs=[SM]
        + [VM] * (s + 2)
        + [HB] * 3
        + [VM]
        + [HB] * 3
        + [VM] * 4,
        out_specs=(VM, VM, HB),
        scratch_shapes=[
            pltpu.VMEM((s * t, w), bf16),
            pltpu.VMEM((holders * srows, d), f32),
            pltpu.VMEM((max(d, holders * srows), d), bf16),
            pltpu.VMEM(zg.shape, bf16),
            pltpu.VMEM(w_in.shape, bf16),
            pltpu.VMEM(x.shape, bf16),
            pltpu.VMEM(normed.shape, bf16),
            pltpu.VMEM(twog.shape, f32),
            pltpu.VMEM(twog.shape, f32),
            pltpu.SemaphoreType.DMA((6 + pieces,)),
        ],
        compiler_params=params(FINISH),
    )(
        core, *preg, rim, conv_w, *pinned(zg, w_in, x), gain, *pinned(normed, twog, small), skipg, gain2, counts,
        router,
    )


def unpack_early(core, mine, other, width_in):
    pairs, rows, d = mine.shape
    holders = 2 * pairs
    w = width_in // 2
    out_rows, in_rows, pieces = (w // holders, d // holders, w // d)

    def kernel(core_ref, mine_ref, other_ref, win_ref, wout_ref):
        for ref, side in ((mine_ref, core_ref[0]), (other_ref, 1 - core_ref[0])):
            for i in range(pairs):
                at = pl.ds(pl.multiple_of((2 * i + side) * out_rows, out_rows), out_rows)
                wout_ref[at, :] = ref[i, :out_rows].astype(f32)
                at = pl.ds(pl.multiple_of((2 * i + side) * in_rows, in_rows), in_rows)
                for p in range(pieces):
                    first = out_rows + p * in_rows
                    win_ref[at, p * d : (p + 1) * d] = ref[i, first : first + in_rows].astype(f32)

    return pl.pallas_call(
        kernel,
        grid=(1,),
        out_shape=(shape_of((d, width_in), f32), shape_of((w, d), f32)),
        in_specs=[SM, whole(*mine.shape), whole(*mine.shape)],
        out_specs=(pl.BlockSpec((d, w), lambda i: (0, 1)), whole(w, d)),
        compiler_params=params(),
    )(core, mine, other)


def unpack_late(core, mine, other, wide, heights, experts, digits, scale):
    pairs, rows, d = mine.shape
    holders = 2 * pairs
    w = wide.shape[1] // 2
    in_rows, pieces = (d // holders, w // d)
    srows = rows - pieces * in_rows
    k, rank, n, taps = heights
    tall = k + rank + n + 8

    def kernel(
        core_ref, mine_ref, other_ref, wide_ref, win_ref, wx_ref, wdt_ref, alog_ref, cw_ref, *refs
    ):
        vectors, (gain1_ref, gain2_ref, router_ref, load_ref, pack_ref) = (refs[:3], refs[3:])
        for ref, side in ((mine_ref, core_ref[0]), (other_ref, 1 - core_ref[0])):
            for i in range(pairs):
                at = pl.ds(pl.multiple_of((2 * i + side) * in_rows, in_rows), in_rows)
                for p in range(pieces):
                    part = ref[i, p * in_rows : (p + 1) * in_rows]
                    win_ref[at, p * d : (p + 1) * d] = part.astype(f32)
                at = pl.ds(pl.multiple_of((2 * i + side) * srows, srows), srows)
                pack_ref[at, :] = ref[i, pieces * in_rows :].astype(f32)
        lines = [pack_ref[p * tall : (p + 1) * tall] for p in range(pieces)]
        lines = jnp.concatenate(lines, axis=1)
        at = 0
        for ref in (wx_ref, wdt_ref, alog_ref):
            ref[...] = lines[at : at + ref.shape[0]]
            at += ref.shape[0]
        tail = lines[at:]
        cw_ref[...] = tail[:taps]
        at = pieces * tall
        vectors[0][...] = tail[taps]
        vectors[1][...] = tail[taps + 1]
        skips = pack_ref[at : at + 8]
        vectors[2][...] = jnp.concatenate([skips[p : p + 1] for p in range(pieces)], axis=1)[0]
        gain1_ref[...] = skips[pieces]
        gain2_ref[...] = skips[pieces + 1]
        count = skips[pieces + 2 : pieces + 3]
        for row in range(2):
            total = 0.0
            for digit in range(digits):
                first = (2 * digit + row) * experts
                total = total + 2.0**digit * count[:, first : first + experts]
            load_ref[row : row + 1, :] = total * scale
        router_ref[...] = pack_ref[at + 8 : at + 8 + experts]

    shapes = [(k, w), (rank, w), (n, w), (taps, w), (w,), (w,), (w,), (d,), (d,), (experts, d), (2, experts)]
    return pl.pallas_call(
        kernel,
        grid=(1,),
        out_shape=(shape_of(wide.shape, f32),) + tuple(shape_of(v, f32) for v in shapes),
        in_specs=[SM, whole(*mine.shape), whole(*mine.shape), pl.BlockSpec(memory_space=pl.ANY)],
        out_specs=(whole(d, w),) + tuple(whole(*v) for v in shapes),
        scratch_shapes=[pltpu.VMEM((holders * srows, d), f32)],
        input_output_aliases={3: 0},
        compiler_params=params(),
    )(core, mine, other, wide)


def blend(pick, near, far, prob, two):
    s, t, d = two.shape

    def kernel(pick_ref, near_ref, far_ref, prob_ref, two_ref, out_ref):
        rows = dot_tn(pick_ref[...], near_ref[...]) + dot_tn(pick_ref[...], far_ref[...])
        for seq in range(s):
            out_ref[seq] = two_ref[seq] + prob_ref[seq] * rows[seq * t : (seq + 1) * t]

    return pl.pallas_call(
        kernel,
        out_shape=shape_of((s, t, d), f32),
        in_specs=[VM] * 5,
        out_specs=VM,
        compiler_params=params(),
    )(pick, near, far, prob, two)


def shifted(value, axis, steps):
    count = lax.axis_size(axis)
    leading, last = (max(0, -steps), min(count, count - steps))
    return lax.ppermute(value, axis, [(source, source + steps) for source in range(leading, last)])


def swapped(value, axis, mask):
    return lax.ppermute(value, axis, [(i, i ^ mask) for i in range(lax.axis_size(axis))])


def after(value, *others):
    return lax.optimization_barrier((value, others))[0]


def together(*values):
    return lax.optimization_barrier(values)


def exchanged(parts, axis):
    return lax.all_to_all(parts, axis, split_axis=0, concat_axis=0, tiled=True)


def added(first, *others):
    total = first.astype(f32)
    for other in others:
        total = total + other.astype(f32)
    return total.astype(bf16)


def bits_of(axis):
    return range(lax.axis_size(axis).bit_length() - 1)


def doubled(block, axis, bit, dim):
    other = swapped(block, axis, 1 << bit)
    low = (lax.axis_index(axis) >> bit) & 1 == 0
    return jnp.where(
        low,
        jnp.concatenate([block, other], axis=dim),
        jnp.concatenate([other, block], axis=dim),
    )


class Gather:
    def __init__(self, block):
        many = len(bits_of("expert")) - 1
        cut = block.shape[1] // 2
        self.many = many
        self.routes = [[*range(1, many + 1)], [*range(many, 0, -1)]]
        self.halves = [
            piece.reshape((2,) * many + piece.shape[1:]) for piece in (block[:, :cut], block[:, cut:])
        ]

    def step(self, place):
        self.pairs = []
        for half, route in zip(self.halves, self.routes):
            bit = route[place]
            side = (lax.axis_index("expert") >> bit) & 1
            dim = self.many - bit
            stays = lax.dynamic_slice_in_dim(half, side, 1, dim)
            goes = lax.dynamic_slice_in_dim(half, 1 - side, 1, dim)
            self.pairs.append((stays, swapped(goes, "expert", 1 << bit)))
        return self.pairs

    def add(self):
        self.halves = [added(*pair) for pair in self.pairs]

    def whole(self):
        return jnp.concatenate([half.reshape(half.shape[self.many :]) for half in self.halves], axis=0)


def group_parts(block):
    count = lax.axis_size("dp")
    mine = lax.axis_index("dp")
    parts = block.reshape(count, -1, block.shape[-1])

    def part(place):
        return lax.dynamic_index_in_dim(parts, place, 0, keepdims=False)

    return [part(mine)] + [swapped(part(mine ^ mask), "dp", mask) for mask in range(1, count)]


def group_blocks(share):
    return [share] + [swapped(share, "dp", mask) for mask in range(1, lax.axis_size("dp"))]


def joined_groups(seen):
    mine = lax.axis_index("dp")
    blocks = []
    for place in range(len(seen)):
        block = seen[0]
        for mask in range(1, len(seen)):
            block = jnp.where(mine ^ mask == place, seen[mask], block)
        blocks.append(block)
    return jnp.concatenate(blocks, axis=0)


class Spread:
    def __init__(self, block):
        many = len(bits_of("expert")) - 1
        cut = block.shape[0] // 2
        self.many = many
        self.routes = [[*range(many, 0, -1)], [*range(1, many + 1)]]
        self.halves = [
            piece.reshape((1,) * many + piece.shape) for piece in (block[:cut], block[cut:])
        ]

    def step(self, place):
        self.halves = [
            doubled(half, "expert", route[place], self.many - route[place])
            for half, route in zip(self.halves, self.routes)
        ]
        return self.halves

    def whole(self):
        blocks = [half.reshape((-1,) + half.shape[self.many :]) for half in self.halves]
        return jnp.concatenate(blocks, axis=1)


def body(
    layer_input,
    norm1_gain,
    w_in,
    conv_weight,
    conv_bias,
    w_xproj,
    w_dt,
    dt_bias,
    a_log,
    d_skip,
    w_out,
    norm2_gain,
    router_weight,
    w_up,
    w_down,
    expert_route,
    capacity,
    output_grad,
):
    seq_count, span_len, model_width = layer_input.shape
    inner_width = w_in.shape[1] // 2
    conv_taps = conv_weight.shape[0]
    rank_dt = w_dt.shape[0]
    state_width = a_log.shape[1]
    experts_all = router_weight.shape[1]
    tokens = seq_count * span_len
    groups, holders = (lax.axis_size("dp"), lax.axis_size("expert"))
    slot_count = max(2, 5 * tokens // (4 * experts_all))
    slots = experts_all * slot_count
    far = max(1, groups // 2)
    w_masks = range(1, far)
    mine = lax.axis_index("expert").astype(jnp.int32).reshape(1)
    reach = 8

    core = mine & 1

    def traded(placed):
        blocks = placed.reshape(experts_all, slot_count, model_width)
        return exchanged(blocks, "expert").reshape(slots, model_width)

    rim = shifted(layer_input[:, span_len - reach :], "expert", 1)
    pick, placed, choose, counts = route(
        expert_route, capacity, after(output_grad, rim), slot_count
    )
    og_own = traded(placed)
    up_mats = [w_up[0]] + [swapped(w_up[0], "dp", mask) for mask in w_masks]
    down_mats = [w_down[0]] + [swapped(w_down[0], "dp", mask) for mask in w_masks]
    router_t = router_weight.T

    normed, conv_in, gate_z, pre_conv, act, sel, selt, dt_pre, step, rate2, ends = front(
        layer_input, rim, norm1_gain, w_in, conv_weight, conv_bias, w_xproj.T, w_dt, dt_bias, a_log.T
    )
    og_own, ends = together(og_own, ends)
    og_other = swapped(og_own, "dp", far)
    every = lax.all_gather(ends, "expert")
    saved, y_full, gated, stream_two, gate_prob, placed = middle(
        mine, every, step, act, sel, selt, rate2, d_skip, gate_z, layer_input, w_out, norm2_gain, pick, choose,
        router_t,
    )

    row_own = traded(placed)
    row_own, og_other, up_mats, down_mats = together(row_own, og_other, up_mats, down_mats)
    row_other = swapped(row_own, "dp", far)
    fwd_a, bwd_a, grd_a, log_a, hid_a, pre_a = expert_rows(
        mine, row_own, og_own, router_t, up_mats, down_mats, bf16
    )
    near_rows = traded(fwd_a)
    row_other, bwd_a, near_rows = together(row_other, bwd_a, near_rows)
    fwd_b, bwd_b, grd_b, log_b, hid_b, pre_b = expert_rows(
        mine, row_other, og_other, router_t, up_mats, down_mats, bf16
    )
    bwd_back = swapped(bwd_b, "dp", far)
    up_grad, down_grad, lows, router_grad = expert_grads(
        (row_own, row_other), (grd_a, grd_b), (log_a, log_b), (hid_a, hid_b), (pre_a, pre_b)
    )
    far_rows = traded(fwd_b)
    bwd_back, router_grad, far_rows = together(bwd_back, router_grad, far_rows)
    got = traded(added(bwd_a, bwd_back))

    stream_two_grad, gain_two_grad, y_grad, z_grad, skip_grad, early, sent = back(
        core, got, pick, stream_two, norm2_gain, output_grad, w_out, gate_z, y_full, act, gated, normed, holders
    )
    far_rows = swapped(far_rows, "dp", far)
    y_grad, far_rows = together(y_grad, far_rows)

    def back_from(piece, *others):
        return [swapped(after(low, *others), "dp", mask) for low, mask in zip(lows[piece], w_masks)]

    y_grad, sent = together(y_grad, sent)
    came = swapped(sent, "expert", 1)
    head = head_of(y_grad, step, selt, rate2)
    head, came = together(head, came)
    backs = [back_from(0, y_grad)]
    heads = lax.all_gather(head, "expert", tiled=False)
    heads, early, came, backs[0] = together(heads, early, came, backs[0])
    backs += [back_from(1, heads), back_from(2, heads)]
    first = Gather(added(early, came))
    pre_grads = []
    for seq in range(seq_count):
        if seq < first.many:
            first.step(seq)
        pre_grad, rim_rows, small = scan_back(
            conv_taps, seq, mine, heads, every, step, act, y_grad, sel, selt, rate2, saved, dt_pre, w_dt,
            w_xproj.T, d_skip, pre_conv, conv_in, (small, rim_rows) if seq else (),
        )
        pre_grads.append(pre_grad)
        if seq < first.many:
            rim_rows, heads, first.pairs = together(rim_rows, heads, first.pairs)
            first.add()
        if seq == 0:
            rim_rows, heads, *backs[1:] = together(rim_rows, heads, *backs[1:])
            backs.append(back_from(3, heads))
    for place in range(seq_count, first.many):
        first.step(place)
        first.add()
    rim_rows, backs[3] = together(rim_rows, backs[3])
    rims = shifted(rim_rows, "expert", -1)
    parts = group_parts(first.whole())
    in_rows = model_width // holders * (inner_width // model_width)
    lines = inner_width // model_width * small.shape[0] + 8 + experts_all
    srows = -(-lines // (16 * holders)) * 16
    srows += -(in_rows + srows) % (8 * groups)
    late, sent, grad_input = finish(
        core, pre_grads, rims, conv_weight, z_grad, w_in, layer_input, norm1_gain, normed,
        stream_two_grad, small, skip_grad, gain_two_grad, counts, router_grad, (holders, srows),
    )
    parts, late, sent = together(parts, late, sent)

    came = swapped(sent, "expert", 1)
    many = len(bits_of("dp"))
    share = added(*parts)
    block = share.reshape((1,) * many + share.shape)
    bits = [*reversed(bits_of("dp"))]
    last = Gather(added(late, came))
    expert_sums = [(down_grad, backs[2:]), (up_grad, backs[:2])]
    done_sums = []
    for place in range(last.many):
        ready = last.halves
        last.step(place)
        if place < 2:
            total, pieces = expert_sums[place]
            total = after(total, ready)
            for pair in zip(*pieces):
                total = total + jnp.concatenate(pair, axis=0).astype(f32)
            total, last.pairs = together(total, last.pairs)
            done_sums.append(total)
        if bits:
            bit = bits.pop(0)
            block = doubled(block, "dp", bit, many - 1 - bit)
        last.pairs, block = together(last.pairs, block)
        last.add()
    grad_w_down, grad_w_up = done_sums
    for bit in bits:
        block = doubled(block, "dp", bit, many - 1 - bit)
    parts = group_parts(last.whole())
    spread = Spread(block.reshape(-1, model_width))
    parts, *spread.halves = together(parts, *spread.step(0))
    seen = group_blocks(added(*parts))
    for place in range(1, spread.many):
        spread.step(place)
    seen, *spread.halves = together(seen, *spread.halves)
    early = spread.whole()
    early_far = swapped(early, "expert", 1)
    spread = Spread(joined_groups(seen))
    early, early_far, *spread.halves = together(early, early_far, *spread.step(0))
    for place in range(1, spread.many):
        spread.step(place)
    grad_w_in, grad_w_out = unpack_early(core, early, early_far, 2 * inner_width)
    result = blend(pick, near_rows, far_rows, gate_prob, stream_two)
    grad_w_in, result, *spread.halves = together(grad_w_in, result, *spread.halves)
    late = spread.whole()
    late_far = swapped(late, "expert", 1)
    grad_w_in, wx_grad, wdt_grad, alog_grad, conv_grad, *vectors, expert_loads = unpack_late(
        core, late, late_far, grad_w_in, (sel.shape[2], rank_dt, state_width, conv_taps), experts_all,
        tokens.bit_length(), experts_all / (tokens * groups * holders),
    )
    conv_b_grad, dt_b_grad, skip_grad, gain_one, gain_two, router_grad = vectors
    return (
        result,
        grad_input,
        gain_one,
        grad_w_in,
        conv_grad,
        conv_b_grad,
        wx_grad.T,
        wdt_grad,
        dt_b_grad,
        alog_grad.T,
        skip_grad,
        grad_w_out,
        gain_two,
        router_grad.T,
        grad_w_up[None],
        grad_w_down[None],
        expert_loads,
    )


def solution(mesh):
    in_specs = (
        P("dp", "expert", None),
        P(),
        P(),
        P(),
        P(),
        P(),
        P(),
        P(),
        P(),
        P(),
        P(),
        P(),
        P(),
        P("expert", None, "dp"),
        P("expert", "dp", None),
        P("dp", "expert"),
        P(),
        P("dp", "expert", None),
    )
    out_specs = (
        P("dp", "expert", None),
        P("dp", "expert", None),
        P(),
        P(),
        P(),
        P(),
        P(),
        P(),
        P(),
        P(),
        P(),
        P(),
        P(),
        P(),
        P("expert", None, "dp"),
        P("expert", "dp", None),
        P(),
    )
    return jax.shard_map(body, mesh=mesh, in_specs=in_specs, out_specs=out_specs, check_vma=False)
```

```python
import jax
import jax.numpy as jnp
from jax import lax
from jax.experimental import pallas as pl
from jax.experimental.pallas import tpu as pltpu
from jax.sharding import PartitionSpec as P

f32 = jnp.float32
bf16 = jnp.bfloat16
LN = 128
SUB = 16
GROUP = 4
BG = 2
EPSILON = 1e-05
LOG2E = 1.4426950408889634
NT = (((1,), (1,)), ((), ()))
TN = (((0,), (0,)), ((), ()))
VM = pl.BlockSpec(memory_space=pltpu.VMEM)
SM = pl.BlockSpec(memory_space=pltpu.SMEM)
HB = pl.BlockSpec(memory_space=pltpu.HBM)


class Copies:
    def __init__(self, sems):
        self.sems = sems
        self.count = 0
        self.under_way = []

    def start(self, source, target):
        copy = pltpu.make_async_copy(source, target, self.sems.at[self.count])
        self.count += 1
        copy.start()
        self.under_way.append(copy)
        return copy

    def arrived(self, copy):
        copy.wait()
        self.under_way.remove(copy)

    def wait(self):
        while self.under_way:
            self.under_way.pop().wait()


FRONT, MIDDLE, BACK, SCAN, FINISH = (28, 32, 34, 36, 28)


def params(mib=24):
    return pltpu.CompilerParams(vmem_limit_bytes=mib << 20)


def shape_of(shape, dtype):
    return jax.ShapeDtypeStruct(shape, dtype)


def in_hbm(shape, dtype):
    return pltpu.HBM(shape, dtype)


def pinned(*values):
    return [pltpu.with_memory_space_constraint(value, pltpu.HBM) for value in values]


def dot(left, right):
    return jnp.dot(left, right, preferred_element_type=f32)


def dot_nt(left, right):
    return lax.dot_general(left, right, NT, preferred_element_type=f32)


def dot_tn(left, right):
    return lax.dot_general(left, right, TN, preferred_element_type=f32)


def spread_lanes(table, out_ref):
    ns, span = table.shape
    for t in range(span):
        out_ref[t] = jnp.broadcast_to(table[:, t : t + 1], (ns, LN))


def row_of(block, i, ns):
    return jnp.broadcast_to(block[i : i + 1], (ns, LN))


def tile_of(ref, seq, t0, j):
    return ref[seq, pl.ds(pl.multiple_of(t0, SUB), SUB), j * LN : (j + 1) * LN].astype(f32)


def tile_groups(tiles, size):
    return [range(g, min(g + size, tiles)) for g in range(0, tiles, size)]


def block_diagonal(part):
    ns = part.shape[1]
    lane = lax.broadcasted_iota(jnp.int32, (ns, SUB * ns), 1)
    copy = ((lane & (ns - 1)) == lax.broadcasted_iota(jnp.int32, (ns, SUB * ns), 0)).astype(bf16)
    high = part.astype(bf16)
    low = (part - high.astype(f32)).astype(bf16)
    block = lax.broadcasted_iota(jnp.int32, (SUB, SUB * ns), 1) // ns
    own = block == lax.broadcasted_iota(jnp.int32, (SUB, SUB * ns), 0)
    pieces = [jnp.where(own, dot(half, copy), 0.0) for half in (high, low)]
    return jnp.concatenate(pieces, axis=0).astype(bf16)


def silu_slope(values):
    logistic = jax.nn.sigmoid(values)
    return logistic * (1.0 + values * (1.0 - logistic))


def inverse_rms(values):
    return lax.rsqrt(jnp.mean(values * values, axis=-1, keepdims=True) + EPSILON)


def norm_backward(values, gain_vec, inv_rms, upstream):
    normal = values * inv_rms
    weighted = upstream * gain_vec
    mean = jnp.mean(weighted * normal, axis=-1, keepdims=True)
    return (
        inv_rms * (weighted - normal * mean),
        jnp.sum(upstream * normal, axis=0, keepdims=True),
    )


def route(expert_route, capacity, og, slot_count):
    s, t = expert_route.shape
    experts = capacity.shape[0]
    d = og.shape[2]
    tokens = s * t
    slots = experts * slot_count
    digits = tokens.bit_length()

    def kernel(
        cap_from, route_from, og_from, pick_to, placed_ref, choose_to, count_to,
        cap_ref, route_ref, og_ref, pick_ref, choose_ref, count_ref, sems,
    ):
        copies = Copies(sems)
        loads = [
            copies.start(source, target)
            for source, target in ((cap_from, cap_ref), (route_from, route_ref), (og_from, og_ref))
        ]
        copies.arrived(loads[0])
        copies.arrived(loads[1])
        flat = jnp.concatenate([route_ref[k : k + 1] for k in range(s)], axis=1)
        rows = lax.broadcasted_iota(jnp.int32, (LN, tokens), 0)
        choose = (rows == flat).astype(f32)
        earlier = lax.broadcasted_iota(jnp.int32, (tokens, tokens), 0)
        earlier = earlier < lax.broadcasted_iota(jnp.int32, (tokens, tokens), 1)
        rank = dot(choose.astype(bf16), earlier.astype(bf16))
        rank = jnp.sum(rank * choose, axis=0, keepdims=True).astype(jnp.int32)
        slot_limit = cap_ref[...].reshape(1, experts).astype(f32).astype(bf16)
        limit = dot(slot_limit, choose[:experts].astype(bf16)).astype(jnp.int32)
        kept = rank < limit
        target = jnp.where(kept, flat * slot_count + rank, slots)
        pick = lax.broadcasted_iota(jnp.int32, (slots, tokens), 0) == target
        pick = pick.astype(f32).astype(bf16)
        pick_ref[...] = pick
        copies.start(pick_ref, pick_to)
        copies.arrived(loads[2])
        every = jnp.concatenate([og_ref[k] for k in range(s)], axis=0)
        placed_ref[...] = dot(pick, every).astype(bf16)
        choose_ref[...] = choose.T[:, :experts]
        copies.start(choose_ref, choose_to)
        kept = kept.astype(f32)
        low = choose[:experts].astype(bf16)
        lines = [dot_nt(v.astype(bf16), low) for v in (kept, 1.0 - kept)]
        count = jnp.concatenate(lines, axis=1).astype(jnp.int32)
        lines = [((count >> k) & 1).astype(f32) for k in range(digits)]
        lines.append(jnp.zeros((1, d - 2 * experts * digits), f32))
        count_ref[...] = jnp.concatenate(lines, axis=1)
        copies.start(count_ref, count_to)
        copies.wait()

    return pl.pallas_call(
        kernel,
        out_shape=(
            in_hbm((slots, tokens), bf16),
            shape_of((slots, d), bf16),
            in_hbm((tokens, experts), f32),
            in_hbm((1, d), f32),
        ),
        in_specs=[HB] * 3,
        out_specs=(HB, VM, HB, HB),
        scratch_shapes=[
            pltpu.VMEM((experts,), jnp.int32),
            pltpu.VMEM((s, t), jnp.int32),
            pltpu.VMEM((s, t, d), bf16),
            pltpu.VMEM((slots, tokens), bf16),
            pltpu.VMEM((tokens, experts), f32),
            pltpu.VMEM((1, d), f32),
            pltpu.SemaphoreType.DMA((6,)),
        ],
        compiler_params=params(),
    )(*pinned(capacity, expert_route, og))


def front_kernel(
    x_from, rim_ref, gain_from, win_from, cw_from, cb_from, wxt_from, wdt_from, dtb_from, alog_from,
    normed_to, conv_to, gate_to, pre_to, act_to, sel_to, selt_to, dtp_to, step_to,
    rate_to, send_ref, bb_ref, cum_ref, rate_ref,
    win_ref, normed_ref, conv_ref, gate_ref, pre_ref, act_ref, dtp_ref, step_ref, sel_ref, selt_ref,
    x_ref, gain_ref, cw_ref, cb_ref, wxt_ref, wdt_ref, dtb_ref, alog_ref, sems,
):
    copies = Copies(sems)
    loads = [
        copies.start(source, target)
        for source, target in (
            (x_from, x_ref), (gain_from, gain_ref), (cw_from, cw_ref), (cb_from, cb_ref),
            (wxt_from, wxt_ref), (wdt_from, wdt_ref), (dtb_from, dtb_ref), (alog_from, alog_ref),
        )
    ]
    seqs, span, model = x_ref.shape
    width = cw_ref.shape[1]
    taps = cw_ref.shape[0]
    rim = rim_ref.shape[1]
    ns = rate_ref.shape[0]
    rank = wdt_ref.shape[0]
    cols = 512
    halves = [
        copies.start(win_from.at[:, cut], win_ref.at[:, cut])
        for cut in (slice(0, width), slice(width, 2 * width))
    ]
    for load in loads:
        copies.arrived(load)
    gain = gain_ref[...].reshape(1, -1)
    conv_b = cb_ref[...].reshape(1, -1)
    dt_b = dtb_ref[...].reshape(1, -1)
    rate_ref[...] = jnp.exp(alog_ref[...]) * (-LOG2E)
    copies.start(rate_ref, rate_to)
    rows = []
    for ref in (x_ref, rim_ref):
        for seq in range(seqs):
            v = ref[seq].astype(f32)
            rows.append((v * inverse_rms(v) * gain).astype(bf16))
    for seq in range(seqs):
        normed_ref[seq * span : (seq + 1) * span] = rows[seq]
    copies.start(normed_ref, normed_to)
    every = jnp.concatenate(rows, axis=0)
    copies.arrived(halves[0])
    for c in range(0, width, cols):
        cut = slice(c, c + cols)
        r = dot(every, win_ref[:, cut]).astype(bf16)
        for seq in range(seqs):
            main = r[seq * span : (seq + 1) * span]
            edge = r[seqs * span + seq * rim : seqs * span + (seq + 1) * rim]
            conv_ref[seq, :rim, cut] = edge
            conv_ref[seq, rim:, cut] = main
            v = jnp.concatenate([edge, main], axis=0).astype(f32)
            pre = conv_b[:, cut]
            for k in range(taps):
                first = rim - taps + 1 + k
                pre = pre + cw_ref[k : k + 1, cut] * v[first : first + span]
            pre_ref[seq, :, cut] = pre
            act_ref[seq, :, cut] = (pre * jax.nn.sigmoid(pre)).astype(bf16)
    for source, target in ((conv_ref, conv_to), (pre_ref, pre_to), (act_ref, act_to)):
        copies.start(source, target)
    own = every[: seqs * span]
    copies.arrived(halves[1])
    for c in range(width, 2 * width, cols):
        r = dot(own, win_ref[:, c : c + cols])
        for seq in range(seqs):
            gate_ref[seq, :, c - width : c - width + cols] = r[seq * span : (seq + 1) * span]
    copies.start(gate_ref, gate_to)
    for seq in range(seqs):
        sel = dot_nt(act_ref[seq], wxt_ref[...])
        sel_ref[seq] = sel
        lanes = sel.shape[1]
        wide = jnp.concatenate([sel, jnp.zeros((span, -lanes % LN), f32)], axis=1)
        selt = wide.T[:lanes]
        selt_ref[seq] = selt
        low = sel[:, :rank].astype(bf16)
        for c in range(0, width, cols):
            cut = slice(c, c + cols)
            pre = dot(low, wdt_ref[:, cut]) + dt_b[:, cut]
            dtp_ref[seq, :, cut] = pre
            step = jnp.maximum(pre, 0.0) + jnp.log1p(jnp.exp(-jnp.abs(pre)))
            step_ref[seq, :, cut] = step
            cum_ref[seq : seq + 1, cut] = jnp.sum(step, axis=0, keepdims=True)
        if seq == seqs - 1:
            copies.start(sel_ref, sel_to)
            copies.start(selt_ref, selt_to)
        copies.start(dtp_ref.at[seq], dtp_to.at[seq])
        copies.start(step_ref.at[seq], step_to.at[seq])
        spread_lanes(selt[rank : rank + ns], bb_ref)
        tiles = width // LN

        def chunk(k, state):
            t0 = k * SUB
            state = list(state)
            for group in tile_groups(tiles, GROUP):
                dt = {j: tile_of(step_ref, seq, t0, j) for j in group}
                dx = {j: dt[j] * tile_of(act_ref, seq, t0, j) for j in group}
                for i in range(SUB):
                    b = bb_ref[t0 + i]
                    for j in group:
                        rate = rate_ref[:, j * LN : (j + 1) * LN]
                        decay = jnp.exp2(row_of(dt[j], i, ns) * rate)
                        state[j] = decay * state[j] + row_of(dx[j], i, ns) * b
            return tuple(state)

        state = lax.fori_loop(
            0, span // SUB, chunk, tuple(jnp.zeros((ns, LN), f32) for _ in range(tiles))
        )
        for j in range(tiles):
            cut = slice(j * LN, (j + 1) * LN)
            send_ref[seq * ns : (seq + 1) * ns, cut] = state[j].astype(bf16)
    cum = cum_ref[...]
    high = cum.astype(bf16).astype(f32)
    tail = [high, cum - high, jnp.zeros((8 - 2 * seqs, width), f32)]
    send_ref[seqs * ns :, :] = jnp.concatenate(tail, axis=0).astype(bf16)
    copies.wait()


def front(x, rim, gain, w_in, conv_w, conv_b, wx_t, w_dt, dt_b, alog_t):
    s, t, d = x.shape
    w = conv_w.shape[1]
    n = alog_t.shape[0]
    k = wx_t.shape[0]
    return pl.pallas_call(
        front_kernel,
        out_shape=(
            in_hbm((s * t, d), bf16),
            in_hbm((s, rim.shape[1] + t, w), bf16),
            in_hbm((s, t, w), f32),
            in_hbm((s, t, w), f32),
            in_hbm((s, t, w), bf16),
            in_hbm((s, t, k), f32),
            in_hbm((s, k, t), f32),
            in_hbm((s, t, w), f32),
            in_hbm((s, t, w), f32),
            in_hbm((n, w), f32),
            shape_of((s * n + 8, w), bf16),
        ),
        in_specs=[HB, VM] + [HB] * 8,
        out_specs=(HB,) * 10 + (VM,),
        scratch_shapes=[
            pltpu.VMEM((t, n, LN), f32),
            pltpu.VMEM((s, w), f32),
            pltpu.VMEM((n, w), f32),
            pltpu.VMEM(w_in.shape, bf16),
            pltpu.VMEM((s * t, d), bf16),
            pltpu.VMEM((s, rim.shape[1] + t, w), bf16),
            pltpu.VMEM((s, t, w), f32),
            pltpu.VMEM((s, t, w), f32),
            pltpu.VMEM((s, t, w), bf16),
            pltpu.VMEM((s, t, w), f32),
            pltpu.VMEM((s, t, w), f32),
            pltpu.VMEM((s, t, k), f32),
            pltpu.VMEM((s, k, t), f32),
        ]
        + [pltpu.VMEM(v.shape, v.dtype) for v in (x, gain, conv_w, conv_b, wx_t, w_dt, dt_b, alog_t)]
        + [
            pltpu.SemaphoreType.DMA((18 + 2 * s,)),
        ],
        compiler_params=params(FRONT),
    )(*pinned(x), rim, *pinned(gain, w_in, conv_w, conv_b, wx_t, w_dt, dt_b, alog_t))


def carry_of(every_ref, rate_ref, seq, seqs, place, stop, step):
    ns, width = rate_ref.shape
    count = jnp.maximum((stop - place) * step, 0)

    def join(u, total):
        block = every_ref[place + u * step].astype(f32)
        row = seqs * ns + seq
        cum = block[row : row + 1] + block[row + seqs : row + seqs + 1]
        return jnp.exp2(rate_ref[...] * cum) * total + block[seq * ns : (seq + 1) * ns]

    return lax.fori_loop(0, count, join, jnp.zeros((ns, width), f32))


def middle_kernel(
    mine_ref, every_ref, step_ref, act_ref, sel_ref, selt_ref, rate_ref, skip_ref, gate_ref,
    x_ref, wout_from, gain_ref, pick_ref, choose_ref, router_ref,
    h_to, y_ref, gated_ref, two_ref, prob_ref, placed_ref, bb_ref, st_ref, acc_ref,
    wout_ref, first_ref, h_ref, wide_ref, sems,
):
    _, span, width = step_ref.shape
    ns = rate_ref.shape[0]
    rank = sel_ref.shape[2] - 2 * ns
    tiles = width // LN
    seqs = pick_ref.shape[1] // span
    mine = mine_ref[0]
    this = pl.program_id(0)
    wout = pltpu.make_async_copy(wout_from, wout_ref, sems.at[0])

    @pl.when(this == 0)
    def _():
        wout.start()

    skip = skip_ref[...].reshape(1, -1)
    for seq in range(seqs):

        @pl.when(pl.program_id(0) == seq)
        def _():
            st_ref[...] = carry_of(every_ref, rate_ref, seq, seqs, 0, mine, 1)

    spread_lanes(selt_ref[0, rank : rank + ns], bb_ref)
    first_ref[...] = st_ref[...].astype(bf16)
    first = pltpu.make_async_copy(first_ref, h_to.at[this, 0:ns, :], sems.at[1])
    first.start()

    def saving(k):
        at = pl.ds(pl.multiple_of((k * SUB + 1) * ns, ns), SUB * ns)
        slot = k & 1
        return pltpu.make_async_copy(h_ref.at[slot], h_to.at[this, at, :], sems.at[2 + slot])

    def chunk(k, carry):
        t0 = k * SUB
        slot = k & 1
        rows = pl.ds(pl.multiple_of(t0, SUB), SUB)

        @pl.when(k >= 2)
        def _():
            saving(k - 2).wait()

        for group in tile_groups(tiles, GROUP):
            state = {j: st_ref[:, j * LN : (j + 1) * LN] for j in group}
            dt = {j: tile_of(step_ref, 0, t0, j) for j in group}
            dx = {j: dt[j] * tile_of(act_ref, 0, t0, j) for j in group}
            for i in range(SUB):
                b = bb_ref[t0 + i]
                for j in group:
                    cut = slice(j * LN, (j + 1) * LN)
                    decay = jnp.exp2(row_of(dt[j], i, ns) * rate_ref[:, cut])
                    state[j] = decay * state[j] + row_of(dx[j], i, ns) * b
                    wide_ref[i * ns : (i + 1) * ns, cut] = state[j]
            for j in group:
                st_ref[:, j * LN : (j + 1) * LN] = state[j]
        diag = block_diagonal(sel_ref[0, rows, rank + ns :])
        states = wide_ref[...].astype(bf16)
        h_ref[slot] = states
        saving(k).start()
        r = dot(diag, states)
        y_ref[0, rows, :] = r[:SUB] + r[SUB:] + skip * act_ref[0, rows, :].astype(f32)
        return carry

    chunks = span // SUB
    lax.fori_loop(0, chunks, chunk, 0)
    gate = gate_ref[0]
    gated = (y_ref[0] * (gate * jax.nn.sigmoid(gate))).astype(bf16)
    gated_ref[0] = gated

    @pl.when(this == 0)
    def _():
        wout.wait()

    two = x_ref[0].astype(f32) + dot(gated, wout_ref[...])
    two_ref[0] = two
    moe = (two * inverse_rms(two) * gain_ref[...].reshape(1, -1)).astype(bf16)
    logits = dot_nt(moe, router_ref[...])
    raised = jnp.exp(logits - jnp.max(logits, axis=1, keepdims=True))
    chosen = jnp.sum(raised * choose_ref[...], axis=1, keepdims=True)
    prob_ref[0] = chosen / jnp.sum(raised, axis=1, keepdims=True)
    for seq in range(seqs):

        @pl.when(pl.program_id(0) == seq)
        def _():
            part = dot(pick_ref[:, seq * span : (seq + 1) * span], moe)
            if seq:
                part = part + acc_ref[...]
            if seq < seqs - 1:
                acc_ref[...] = part
            else:
                placed_ref[...] = part.astype(bf16)

    first.wait()
    for k in range(max(0, chunks - 2), chunks):
        saving(k).wait()


def by_sequence(*shape):
    return pl.BlockSpec((1,) + shape, lambda i: (i,) + (0,) * len(shape))


def whole(*shape):
    return pl.BlockSpec(shape, lambda i: (0,) * len(shape))


def middle(
    mine, every, step, act, sel, selt, rate2, skip, gate, x, w_out, gain, pick, choose, router_t
):
    s, t, w = step.shape
    n = rate2.shape[0]
    d = x.shape[2]
    k = sel.shape[2]
    return pl.pallas_call(
        middle_kernel,
        grid=(s,),
        out_shape=(
            in_hbm((s, (t + 1) * n, w), bf16),
            in_hbm((s, t, w), f32),
            in_hbm((s, t, w), bf16),
            in_hbm((s, t, d), f32),
            shape_of((s, t, 1), f32),
            shape_of((pick.shape[0], d), bf16),
        ),
        in_specs=[
            SM,
            whole(*every.shape),
            by_sequence(t, w),
            by_sequence(t, w),
            by_sequence(t, k),
            by_sequence(k, t),
            whole(n, w),
            whole(w),
            by_sequence(t, w),
            by_sequence(t, d),
            HB,
            whole(d),
            whole(*pick.shape),
            pl.BlockSpec((t, choose.shape[1]), lambda i: (i, 0)),
            whole(*router_t.shape),
        ],
        out_specs=(
            HB,
            by_sequence(t, w),
            by_sequence(t, w),
            by_sequence(t, d),
            by_sequence(t, 1),
            whole(pick.shape[0], d),
        ),
        scratch_shapes=[
            pltpu.VMEM((t, n, LN), f32),
            pltpu.VMEM((n, w), f32),
            pltpu.VMEM((pick.shape[0], d), f32),
            pltpu.VMEM((w, d), bf16),
            pltpu.VMEM((n, w), bf16),
            pltpu.VMEM((2, SUB * n, w), bf16),
            pltpu.VMEM((SUB * n, w), f32),
            pltpu.SemaphoreType.DMA((4,)),
        ],
        compiler_params=params(MIDDLE),
    )(mine, every, *pinned(step, act, sel, selt, rate2, skip, gate, x, w_out, gain, pick, choose), router_t)


def gelu_pair(v):
    root = 0.7978845608028654
    square = v * v
    bend = jnp.tanh(root * (v + 0.044715 * v * square))
    half = 0.5 * (1.0 + bend)
    slope = half + 0.5 * v * (1.0 - bend * bend) * (root * (1.0 + 3.0 * 0.044715 * square))
    return v * half, slope


def expert_kernel(shares, own_ref, rows_ref, og_ref, router_ref, *refs):
    ups, downs, refs = (refs[:shares], refs[shares : 2 * shares], refs[2 * shares :])
    fwd_ref, bwd_ref = refs[:2]
    kept = 2 + 2 * shares
    targets, sources, sems = (refs[2 : 2 + kept], refs[2 + kept : 2 + 2 * kept], refs[-1])
    copies = Copies(sems)
    grd_ref, log_ref = sources[:2]
    hids, pres = (sources[2 : 2 + shares], sources[2 + shares :])
    rows = rows_ref[...]
    logits = dot_nt(rows, router_ref[...])
    top = jnp.max(logits, axis=1, keepdims=True)
    raised = jnp.exp(logits - top)
    probs = raised / jnp.sum(raised, axis=1, keepdims=True)
    own = (lax.broadcasted_iota(jnp.int32, (1, probs.shape[1]), 1) == own_ref[0]).astype(f32)
    gate = jnp.sum(probs * own, axis=1, keepdims=True)
    og = og_ref[...].astype(f32)
    grads = (og * gate).astype(bf16)
    grd_ref[...] = grads
    fwd, bwd = (0.0, 0.0)
    for up_ref, down_ref, hid_ref, pre_ref in zip(ups, downs, hids, pres):
        hidden, slope = gelu_pair(dot(rows, up_ref[...]))
        hidden = hidden.astype(bf16)
        hid_ref[...] = hidden
        fwd = fwd + dot(hidden, down_ref[...])
        pre = (dot_nt(grads, down_ref[...]) * slope).astype(bf16)
        pre_ref[...] = pre
        bwd = bwd + dot_nt(pre, up_ref[...])
    logit = jnp.sum(og * fwd, axis=1, keepdims=True) * gate * (own - probs)
    log_ref[...] = logit
    high = logit.astype(bf16)
    low = (logit - high.astype(f32)).astype(bf16)
    bwd = bwd + dot(high, router_ref[...]) + dot(low, router_ref[...])
    for source, target in zip(sources, targets):
        copies.start(source, target)
    fwd_ref[...] = fwd.astype(fwd_ref.dtype)
    bwd_ref[...] = bwd.astype(bwd_ref.dtype)
    copies.wait()


def expert_rows(own, rows, og, router, ups, downs, dtype):
    m, d = rows.shape
    f = ups[0].shape[1]
    shares = len(ups)

    def kernel(*refs):
        expert_kernel(shares, *refs)

    kept = [((m, d), bf16), ((m, router.shape[0]), f32)] + [((m, f), bf16)] * (2 * shares)
    outs = pl.pallas_call(
        kernel,
        out_shape=(shape_of((m, d), dtype), shape_of((m, d), dtype))
        + tuple(in_hbm(*one) for one in kept),
        in_specs=[SM] + [VM] * (3 + 2 * shares),
        out_specs=(VM, VM) + (HB,) * len(kept),
        scratch_shapes=[pltpu.VMEM(*one) for one in kept] + [pltpu.SemaphoreType.DMA((len(kept),))],
        compiler_params=params(),
    )(own, rows, og, router, *ups, *downs)
    return (*outs[:4], outs[4 : 4 + shares], outs[4 + shares :])


def deal(block_ref, keep_ref, send_ref, core, first, rows):
    for pair in range(keep_ref.shape[0]):
        for ref, side in ((keep_ref, core), (send_ref, 1 - core)):
            at = pl.ds(pl.multiple_of((2 * pair + side) * rows, rows), rows)
            ref[pair, first : first + rows, :] = block_ref[at, :]


def back(core, got, pick, two, gain, og, w_out, gate, y, act, gated, normed, holders):
    s, t, w = y.shape
    d = two.shape[2]
    out_rows, in_rows, pieces = (w // holders, d // holders, w // d)

    def kernel(
        core_ref, got_ref, pick_from, two_from, gain_ref, og_from, wout_from, gate_from, y_from, act_from, gated_from,
        normed_from,
        twog_to, gain2_ref, yg_to, zg_to, skipg_ref, keep_ref, send_ref, yg_ref,
        wout_ref, gate_ref, y_ref, act_ref, twog_ref, zg_ref, pick_ref, two_ref, og_ref, gated_ref, normed_ref,
        mix_ref, block_ref, sems,
    ):
        cols = 512
        copies = Copies(sems)
        firsts = [
            copies.start(source, target)
            for source, target in ((pick_from, pick_ref), (two_from, two_ref), (og_from, og_ref))
        ]
        loads = [
            copies.start(source, target)
            for source, target in (
                (wout_from, wout_ref), (gate_from, gate_ref), (act_from, act_ref), (y_from, y_ref)
            )
        ]
        lasts = [copies.start(gated_from.at[k], gated_ref.at[k * t : (k + 1) * t]) for k in range(s)]
        lasts.append(copies.start(normed_from, normed_ref))
        for load in firsts:
            copies.arrived(load)
        moe_grad = dot_tn(pick_ref[...], got_ref[...])
        gain = gain_ref[...].reshape(1, -1)
        total = 0.0
        for seq in range(s):
            v = two_ref[seq]
            grad, gained = norm_backward(
                v, gain, inverse_rms(v), moe_grad[seq * t : (seq + 1) * t]
            )
            total = total + gained
            grad = grad + og_ref[seq].astype(f32)
            twog_ref[seq] = grad
            mix_ref[seq * t : (seq + 1) * t] = grad.astype(bf16)
        gain2_ref[...] = total
        copies.start(twog_ref, twog_to)
        for load in loads:
            copies.arrived(load)
        for c in range(0, w, cols):
            cut = slice(c, c + cols)
            r = dot_nt(mix_ref[...], wout_ref[cut, :])
            total = 0.0
            for seq in range(s):
                part = r[seq * t : (seq + 1) * t]
                gate = gate_ref[seq, :, cut]
                logistic = jax.nn.sigmoid(gate)
                yg = part * (gate * logistic)
                yg_ref[seq, :, cut] = yg
                slope = logistic * (1.0 + gate * (1.0 - logistic))
                zg = (part * y_ref[seq, :, cut] * slope).astype(bf16)
                zg_ref[seq * t : (seq + 1) * t, cut] = zg
                total = total + jnp.sum(yg * act_ref[seq, :, cut].astype(f32), axis=0, keepdims=True)
            skipg_ref[:, cut] = total
            copies.start(yg_ref.at[:, :, cut], yg_to.at[:, :, cut])
        for k in range(s):
            copies.start(zg_ref.at[k * t : (k + 1) * t], zg_to.at[k])
        for load in lasts:
            copies.arrived(load)
        block_ref[...] = dot_tn(gated_ref[...], mix_ref[...]).astype(bf16)
        deal(block_ref, keep_ref, send_ref, core_ref[0], 0, out_rows)
        for p in range(pieces):
            r = dot_tn(normed_ref[...], zg_ref[:, p * d : (p + 1) * d])
            block_ref[p * d : (p + 1) * d] = r.astype(bf16)
            side = block_ref.at[p * d : (p + 1) * d]
            deal(side, keep_ref, send_ref, core_ref[0], out_rows + p * in_rows, in_rows)
        copies.wait()

    packed = shape_of((holders // 2, out_rows + pieces * in_rows, d), bf16)
    return pl.pallas_call(
        kernel,
        out_shape=(
            in_hbm((s, t, d), f32),
            shape_of((1, d), f32),
            in_hbm((s, t, w), f32),
            in_hbm((s, t, w), bf16),
            shape_of((1, w), f32),
            packed,
            packed,
        ),
        in_specs=[SM, VM, HB, HB, VM] + [HB] * 7,
        out_specs=(HB, VM, HB, HB, VM, VM, VM),
        scratch_shapes=[
            pltpu.VMEM((s, t, w), f32),
            pltpu.VMEM((w, d), bf16),
            pltpu.VMEM((s, t, w), f32),
            pltpu.VMEM((s, t, w), f32),
            pltpu.VMEM((s, t, w), bf16),
            pltpu.VMEM((s, t, d), f32),
            pltpu.VMEM((s * t, w), bf16),
            pltpu.VMEM(pick.shape, bf16),
            pltpu.VMEM(two.shape, f32),
            pltpu.VMEM(og.shape, bf16),
            pltpu.VMEM((s * t, w), bf16),
            pltpu.VMEM(normed.shape, bf16),
            pltpu.VMEM((s * t, d), bf16),
            pltpu.VMEM((w, d), bf16),
            pltpu.SemaphoreType.DMA((9 + 2 * s + w // 512,)),
        ],
        compiler_params=params(BACK),
    )(core, got, *pinned(pick, two), gain, *pinned(og, w_out, gate, y, act, gated, normed))


def head_of(yg, step, selt, rate2):
    s, t, w = step.shape
    n = rate2.shape[0]
    tiles = w // LN

    def kernel(yg_from, step_from, selt_ref, rate_ref, head_ref, cb_ref, step_ref, yg_ref, sems):
        copies = Copies(sems)
        loads = [
            [
                copies.start(source.at[seq], target.at[seq])
                for source, target in ((step_from, step_ref), (yg_from, yg_ref))
            ]
            for seq in range(s)
        ]
        for seq in range(s):
            spread_lanes(selt_ref[seq, selt.shape[1] - n :], cb_ref)
            for load in loads[seq]:
                copies.arrived(load)

            def chunk(u, mu):
                t0 = t - SUB - u * SUB
                mu = list(mu)
                for group in tile_groups(tiles, GROUP):
                    dt = {j: tile_of(step_ref, seq, t0, j) for j in group}
                    yg = {j: tile_of(yg_ref, seq, t0, j) for j in group}
                    for i in reversed(range(SUB)):
                        c = cb_ref[t0 + i]
                        for j in group:
                            rate = rate_ref[:, j * LN : (j + 1) * LN]
                            decay = jnp.exp2(row_of(dt[j], i, n) * rate)
                            mu[j] = decay * (mu[j] + row_of(yg[j], i, n) * c)
                return tuple(mu)

            mu = lax.fori_loop(
                0, t // SUB, chunk, tuple(jnp.zeros((n, LN), f32) for _ in range(tiles))
            )
            for j in range(tiles):
                cut = slice(j * LN, (j + 1) * LN)
                head_ref[seq * n : (seq + 1) * n, cut] = mu[j].astype(bf16)

    return pl.pallas_call(
        kernel,
        out_shape=shape_of((s * n, w), bf16),
        in_specs=[HB, HB, VM, VM],
        out_specs=VM,
        scratch_shapes=[
            pltpu.VMEM((t, n, LN), f32),
            pltpu.VMEM((s, t, w), f32),
            pltpu.VMEM((s, t, w), f32),
            pltpu.SemaphoreType.DMA((2 * s,)),
        ],
        compiler_params=params(12),
    )(*pinned(yg, step), selt, rate2)


def scan_back_kernel(
    taps, seq, seqs, mine_ref, heads_ref, every_ref, step_ref, act_ref, yg_ref, sel_ref, selt_ref, rate_ref, h_from,
    dtp_from, wdt_from, wxt_from, skip_ref, pre_from, conv_from, *refs
):
    prior, refs = (refs[:2], refs[2:]) if seq else ((), refs)
    scan_back_run(
        taps, seq, seqs, mine_ref, heads_ref, every_ref, step_ref, act_ref, yg_ref, sel_ref, selt_ref, rate_ref,
        h_from, dtp_from, wdt_from, wxt_from, skip_ref, pre_from, conv_from, prior, *refs
    )


def scan_back_run(
    taps, seq, seqs, mine_ref, heads_ref, every_ref, step_ref, act_ref, yg_ref, sel_ref, selt_ref, rate_ref,
    h_from, dtp_from, wdt_from, wxt_from, skip_ref, pre_from, conv_from, prior,
    preg_ref, rim_ref, small_ref, cb_ref, mu_ref, al_ref, lam_ref, rdg_ref, s1_ref, adj_ref, ig_ref, og_ref,
    h_ref, dtp_ref, wdt_ref, wxt_ref, pre_ref, conv_ref, sems,
):
    chunks = step_ref.shape[1] // SUB

    def loading(v):
        at = pl.ds(pl.multiple_of((chunks - 1 - v) * SUB * rate_ref.shape[0], 8), h_ref.shape[1])
        return pltpu.make_async_copy(h_from.at[seq, at, :], h_ref.at[v & 1], sems.at[v & 1])

    loading(0).start()
    copies = Copies(sems.at[2:])
    for source, target in (
        (dtp_from.at[seq], dtp_ref), (wdt_from, wdt_ref), (wxt_from, wxt_ref), (pre_from.at[seq], pre_ref),
        (conv_from.at[seq], conv_ref),
    ):
        copies.start(source, target)
    _, span, width = step_ref.shape
    ns = rate_ref.shape[0]
    lanes = sel_ref.shape[2]
    rank = lanes - 2 * ns
    tiles = width // LN
    holders = heads_ref.shape[0]
    rim = conv_ref.shape[0] - span
    count = holders - 1 - mine_ref[0]

    def join(u, total):
        place = holders - 1 - u
        tail = every_ref[place].astype(f32)
        cum = tail[seq : seq + 1] + tail[seqs + seq : seqs + seq + 1]
        return jnp.exp2(rate_ref[...] * cum) * total + heads_ref[place].astype(f32)

    mu_ref[...] = lax.fori_loop(0, count, join, jnp.zeros((ns, width), f32))
    spread_lanes(selt_ref[0, rank + ns :], cb_ref)
    al_ref[...] = jnp.zeros((ns, width), f32)
    block = lax.broadcasted_iota(jnp.int32, (SUB, SUB * ns), 1) // ns
    ones = (block == lax.broadcasted_iota(jnp.int32, (SUB, SUB * ns), 0)).astype(bf16)

    def chunk(v, carry):
        k = chunks - 1 - v
        t0 = k * SUB
        slot = v & 1
        rows = pl.ds(pl.multiple_of(t0, SUB), SUB)

        @pl.when(v + 1 < chunks)
        def _():
            loading(v + 1).start()

        loading(v).wait()
        for group in tile_groups(tiles, BG):
            cuts = {j: slice(j * LN, (j + 1) * LN) for j in group}
            mu = {j: mu_ref[:, cuts[j]] for j in group}
            al = {j: al_ref[:, cuts[j]] for j in group}
            dts = {j: tile_of(step_ref, 0, t0, j) for j in group}
            ygs = {j: tile_of(yg_ref, 0, t0, j) for j in group}
            for i in reversed(range(SUB)):
                c = cb_ref[t0 + i]
                for j in group:
                    rate = rate_ref[:, cuts[j]]
                    dt = row_of(dts[j], i, ns)
                    decay = jnp.exp2(dt * rate)
                    lam = mu[j] + row_of(ygs[j], i, ns) * c
                    mu[j] = decay * lam
                    dg = mu[j] * h_ref[slot, i * ns : (i + 1) * ns, cuts[j]].astype(f32)
                    al[j] = al[j] + dt * dg
                    lam_ref[i * ns : (i + 1) * ns, cuts[j]] = lam
                    rdg_ref[i * ns : (i + 1) * ns, cuts[j]] = rate * dg
            for j in group:
                mu_ref[:, cuts[j]] = mu[j]
                al_ref[:, cuts[j]] = al[j]
        lam = lam_ref[...].astype(bf16)
        r = dot(block_diagonal(sel_ref[0, rows, rank : rank + ns]), lam)
        adj_ref[rows, :] = r[:SUB] + r[SUB:]
        s1_ref[rows, :] = dot(ones, rdg_ref[...].astype(bf16)) * (1.0 / LOG2E)
        up = lax.broadcasted_iota(jnp.int32, (SUB * ns, SUB), 0) // ns
        own = up == lax.broadcasted_iota(jnp.int32, (SUB * ns, SUB), 1)
        dx = (step_ref[0, rows, :] * act_ref[0, rows, :].astype(f32)).astype(bf16)
        d = dot_nt(lam, dx)
        ig_ref[k] = jnp.sum(jnp.where(own, d, 0.0).reshape(SUB, ns, SUB), axis=0)
        d = dot_nt(h_ref[slot, ns:, :], yg_ref[0, rows, :].astype(bf16))
        og_ref[k] = jnp.sum(jnp.where(own, d, 0.0).reshape(SUB, ns, SUB), axis=0)
        return carry

    lax.fori_loop(0, chunks, chunk, 0)
    copies.wait()
    act = act_ref[0].astype(f32)
    adj = adj_ref[...]
    step = step_ref[0]
    dtg = (s1_ref[...] + adj * act) * jax.nn.sigmoid(dtp_ref[...])
    low = dtg.astype(bf16)
    grads = [dot_nt(wdt_ref[...], low)] + [
        jnp.concatenate([ref[k] for k in range(chunks)], axis=1) for ref in (ig_ref, og_ref)
    ]
    grads = jnp.concatenate(grads, axis=0).astype(bf16)
    at = 0

    def put(rows):
        nonlocal at
        cut = slice(at, at + rows.shape[0])
        small_ref[cut, :] = prior[0][cut, :] + rows if seq else rows
        at += rows.shape[0]

    put(dot(grads, act_ref[0]))
    put(dot(selt_ref[0, :rank].astype(bf16), low))
    put(rate_ref[...] * al_ref[...] * (1.0 / LOG2E))
    act_grad = yg_ref[0] * skip_ref[...].reshape(1, -1) + adj * step + dot_tn(grads, wxt_ref[...])
    pre_grad = act_grad * silu_slope(pre_ref[...])
    preg_ref[0] = pre_grad
    rim_ref[seq] = pre_grad[:rim].astype(bf16)
    for place in range(seq):
        rim_ref[place] = prior[1][place]
    inputs = conv_ref[...].astype(f32)
    tail = []
    for k in range(taps):
        first = rim - taps + 1 + k
        tail.append(jnp.sum(pre_grad * inputs[first : first + span], axis=0, keepdims=True))
    tail.append(jnp.sum(pre_grad, axis=0, keepdims=True))
    tail.append(jnp.sum(dtg, axis=0, keepdims=True))
    tail.append(jnp.zeros((8 - len(tail), width), f32))
    put(jnp.concatenate(tail, axis=0))


def scan_back(
    taps, seq, mine, heads, every, step, act, yg, sel, selt, rate2, h, dtp, w_dt, wx_t, skip, pre, conv,
    prior,
):
    s, t, w = step.shape
    n = rate2.shape[0]
    k = sel.shape[2]
    chunks = t // SUB
    rim = conv.shape[1] - t
    small = k + w_dt.shape[0] + n + 8

    def kernel(*refs):
        scan_back_kernel(taps, seq, s, *refs)

    def own(*shape):
        return pl.BlockSpec((1,) + shape, lambda i: (seq,) + (0,) * len(shape))

    return pl.pallas_call(
        kernel,
        grid=(1,),
        out_shape=(
            shape_of((1, t, w), f32),
            shape_of((s, rim, w), bf16),
            shape_of((small, w), f32),
        ),
        in_specs=[
            SM,
            pl.BlockSpec((heads.shape[0], n, w), lambda i: (0, seq, 0)),
            pl.BlockSpec((every.shape[0], 8, w), lambda i: (0, s * n // 8, 0)),
            own(t, w),
            own(t, w),
            own(t, w),
            own(t, k),
            own(k, t),
            whole(n, w),
            HB,
            HB,
            HB,
            HB,
            whole(w),
            HB,
            HB,
            *(whole(*value.shape) for value in prior),
        ],
        out_specs=(whole(1, t, w), whole(s, rim, w), whole(small, w)),
        scratch_shapes=[
            pltpu.VMEM((t, n, LN), f32),
            pltpu.VMEM((n, w), f32),
            pltpu.VMEM((n, w), f32),
            pltpu.VMEM((SUB * n, w), f32),
            pltpu.VMEM((SUB * n, w), f32),
            pltpu.VMEM((t, w), f32),
            pltpu.VMEM((t, w), f32),
            pltpu.VMEM((chunks, n, SUB), f32),
            pltpu.VMEM((chunks, n, SUB), f32),
            pltpu.VMEM((2, (SUB + 1) * n, w), bf16),
            pltpu.VMEM((t, w), f32),
            pltpu.VMEM(w_dt.shape, bf16),
            pltpu.VMEM(wx_t.shape, bf16),
            pltpu.VMEM((t, w), f32),
            pltpu.VMEM(conv.shape[1:], bf16),
            pltpu.SemaphoreType.DMA((7,)),
        ],
        compiler_params=params(SCAN),
    )(
        mine, heads, *pinned(every, step, act, yg, sel, selt, rate2, h, dtp, w_dt, wx_t, skip, pre, conv), *prior
    )


def expert_grads(rows, grds, logs, hids, pres):
    blocks = len(rows)
    shares = len(hids[0])
    d = rows[0].shape[1]
    f = hids[0][0].shape[1]
    flat = [*rows, *grds, *logs] + [v for group in (hids, pres) for block in group for v in block]

    def kernel(*refs):
        count, many = (len(flat), len(outs_shape))
        targets = refs[count : count + many]
        ins = refs[count + many : 2 * count + many]
        outs = refs[2 * count + many : 2 * (count + many)]
        copies = Copies(refs[-1])
        for source, target in zip(refs[:count], ins):
            copies.start(source, target)
        copies.wait()
        row, grd, log = (ins[k * blocks : (k + 1) * blocks] for k in range(3))
        hid = ins[3 * blocks : (3 + shares) * blocks]
        pre = ins[(3 + shares) * blocks :]

        def total(lefts, rights):
            parts = [dot_tn(left[...], right[...]) for left, right in zip(lefts, rights)]
            return sum(parts[1:], parts[0])

        at = 0
        for k in range(shares):
            for value in (total(row, pre[k::shares]), total(hid[k::shares], grd)):
                first = 0
                while first < value.shape[0]:
                    ref = outs[at]
                    ref[...] = value[first : first + ref.shape[0]].astype(ref.dtype)
                    copies.start(ref, targets[at])
                    first += ref.shape[0]
                    at += 1
        router = 0.0
        for log_ref, row_ref in zip(log, row):
            high = log_ref[...].astype(bf16)
            low = (log_ref[...] - high.astype(f32)).astype(bf16)
            router = router + dot_tn(high, row_ref[...]) + dot_tn(low, row_ref[...])
        outs[-1][...] = router
        copies.start(outs[-1], targets[-1])
        copies.wait()

    outs_shape = [((d, f), f32), ((f, d), f32)]
    for _ in range(1, shares):
        outs_shape += [((d - d // 3, f), bf16), ((d // 3, f), bf16)]
        outs_shape += [((f // 3, d), bf16), ((f - f // 3, d), bf16)]
    outs_shape.append(((logs[0].shape[1], d), f32))
    got = pl.pallas_call(
        kernel,
        out_shape=tuple(in_hbm(*one) for one in outs_shape),
        in_specs=[HB] * len(flat),
        out_specs=(HB,) * len(outs_shape),
        scratch_shapes=[pltpu.VMEM(v.shape, v.dtype) for v in flat]
        + [pltpu.VMEM(*one) for one in outs_shape]
        + [pltpu.SemaphoreType.DMA((len(flat) + len(outs_shape),))],
        compiler_params=params(),
    )(*pinned(*flat))
    return got[0], got[1], [got[2 + k : -1 : 4] for k in range(4)], got[-1]


def finish(
    core, preg, rim, conv_w, zg, w_in, x, gain, normed, twog, small, skipg, gain2, counts, router,
    plan,
):
    s = len(preg)
    _, t, w = preg[0].shape
    d = x.shape[2]
    holders, srows = plan
    taps = conv_w.shape[0]
    pieces, in_rows = (w // d, d // holders)

    def kernel(core_ref, *refs):
        preg_refs, refs = (refs[:s], refs[s:])
        run(core_ref, preg_refs, *refs)

    def run(
        core_ref, preg_refs, rim_ref, cw_ref, zg_from, win_from, x_from, gain_ref, normed_from, twog_from,
        small_from, skip_ref, gain2_ref, count_ref, router_ref,
        keep_ref, send_ref, input_to, cg_ref, pack_ref, block_ref,
        zg_ref, win_ref, x_ref, normed_ref, twog_ref, input_ref, sems,
    ):
        copies = Copies(sems)
        pack_ref[...] = jnp.zeros(pack_ref.shape, f32)
        tall = small_from.shape[0]
        first = copies.start(normed_from, normed_ref)
        loads = [copies.start(win_from, win_ref), copies.start(zg_from, zg_ref)]
        loads += [copies.start(x_from, x_ref), copies.start(twog_from, twog_ref)]
        smalls = [
            copies.start(
                small_from.at[:, p * d : (p + 1) * d], pack_ref.at[p * tall : (p + 1) * tall]
            )
            for p in range(pieces)
        ]
        cols = 512
        gain = gain_ref[...].reshape(1, -1)
        for seq in range(s):
            for c in range(0, w, cols):
                cut = slice(c, c + cols)
                v = jnp.concatenate(
                    [preg_refs[seq][0, :, cut], rim_ref[seq, :, cut].astype(f32)], axis=0
                )
                total = cw_ref[taps - 1 : taps, cut] * v[:t]
                for k in range(1, taps):
                    total = total + cw_ref[taps - 1 - k : taps - k, cut] * v[k : k + t]
                cg_ref[seq * t : (seq + 1) * t, cut] = total.astype(bf16)
        copies.arrived(first)
        for p in range(pieces):
            block_ref[:d] = dot_tn(normed_ref[...], cg_ref[:, p * d : (p + 1) * d]).astype(bf16)
            deal(block_ref, keep_ref, send_ref, core_ref[0], p * in_rows, in_rows)
        for load in loads:
            copies.arrived(load)
        gain1 = 0.0
        for seq in range(s):
            grad = dot_nt(cg_ref[seq * t : (seq + 1) * t], win_ref[:, :w])
            grad = grad + dot_nt(zg_ref[seq], win_ref[:, w:])
            v = x_ref[seq].astype(f32)
            grad, gained = norm_backward(v, gain, inverse_rms(v), grad)
            gain1 = gain1 + gained
            input_ref[seq] = twog_ref[seq] + grad
        copies.start(input_ref, input_to)
        for load in smalls:
            copies.arrived(load)
        at = pieces * tall
        lines = [skip_ref[:, p * d : (p + 1) * d] for p in range(pieces)] + [gain1, gain2_ref[...], count_ref[...]]
        for line in lines:
            pack_ref[at : at + 1] = line
            at += 1
        at += -at % 8
        pack_ref[at : at + router_ref.shape[0]] = router_ref[...]
        block_ref[: holders * srows] = pack_ref[...].astype(bf16)
        deal(block_ref, keep_ref, send_ref, core_ref[0], pieces * in_rows, srows)
        copies.wait()

    return pl.pallas_call(
        kernel,
        out_shape=(
            shape_of((holders // 2, pieces * in_rows + srows, d), bf16),
            shape_of((holders // 2, pieces * in_rows + srows, d), bf16),
            shape_of((s, t, d), f32),
        ),
        in_specs=[SM]
        + [VM] * (s + 2)
        + [HB] * 3
        + [VM]
        + [HB] * 3
        + [VM] * 4,
        out_specs=(VM, VM, HB),
        scratch_shapes=[
            pltpu.VMEM((s * t, w), bf16),
            pltpu.VMEM((holders * srows, d), f32),
            pltpu.VMEM((max(d, holders * srows), d), bf16),
            pltpu.VMEM(zg.shape, bf16),
            pltpu.VMEM(w_in.shape, bf16),
            pltpu.VMEM(x.shape, bf16),
            pltpu.VMEM(normed.shape, bf16),
            pltpu.VMEM(twog.shape, f32),
            pltpu.VMEM(twog.shape, f32),
            pltpu.SemaphoreType.DMA((6 + pieces,)),
        ],
        compiler_params=params(FINISH),
    )(
        core, *preg, rim, conv_w, *pinned(zg, w_in, x), gain, *pinned(normed, twog, small), skipg, gain2, counts,
        router,
    )


def unpack_early(core, mine, other, width_in):
    pairs, rows, d = mine.shape
    holders = 2 * pairs
    w = width_in // 2
    out_rows, in_rows, pieces = (w // holders, d // holders, w // d)

    def kernel(core_ref, mine_ref, other_ref, win_ref, wout_ref):
        for ref, side in ((mine_ref, core_ref[0]), (other_ref, 1 - core_ref[0])):
            for i in range(pairs):
                at = pl.ds(pl.multiple_of((2 * i + side) * out_rows, out_rows), out_rows)
                wout_ref[at, :] = ref[i, :out_rows].astype(f32)
                at = pl.ds(pl.multiple_of((2 * i + side) * in_rows, in_rows), in_rows)
                for p in range(pieces):
                    first = out_rows + p * in_rows
                    win_ref[at, p * d : (p + 1) * d] = ref[i, first : first + in_rows].astype(f32)

    return pl.pallas_call(
        kernel,
        grid=(1,),
        out_shape=(shape_of((d, width_in), f32), shape_of((w, d), f32)),
        in_specs=[SM, whole(*mine.shape), whole(*mine.shape)],
        out_specs=(pl.BlockSpec((d, w), lambda i: (0, 1)), whole(w, d)),
        compiler_params=params(),
    )(core, mine, other)


def unpack_late(core, mine, other, wide, heights, experts, digits, scale):
    pairs, rows, d = mine.shape
    holders = 2 * pairs
    w = wide.shape[1] // 2
    in_rows, pieces = (d // holders, w // d)
    srows = rows - pieces * in_rows
    k, rank, n, taps = heights
    tall = k + rank + n + 8

    def kernel(
        core_ref, mine_ref, other_ref, wide_ref, win_ref, wx_ref, wdt_ref, alog_ref, cw_ref, *refs
    ):
        vectors, (gain1_ref, gain2_ref, router_ref, load_ref, pack_ref) = (refs[:3], refs[3:])
        for ref, side in ((mine_ref, core_ref[0]), (other_ref, 1 - core_ref[0])):
            for i in range(pairs):
                at = pl.ds(pl.multiple_of((2 * i + side) * in_rows, in_rows), in_rows)
                for p in range(pieces):
                    part = ref[i, p * in_rows : (p + 1) * in_rows]
                    win_ref[at, p * d : (p + 1) * d] = part.astype(f32)
                at = pl.ds(pl.multiple_of((2 * i + side) * srows, srows), srows)
                pack_ref[at, :] = ref[i, pieces * in_rows :].astype(f32)
        lines = [pack_ref[p * tall : (p + 1) * tall] for p in range(pieces)]
        lines = jnp.concatenate(lines, axis=1)
        at = 0
        for ref in (wx_ref, wdt_ref, alog_ref):
            ref[...] = lines[at : at + ref.shape[0]]
            at += ref.shape[0]
        tail = lines[at:]
        cw_ref[...] = tail[:taps]
        at = pieces * tall
        vectors[0][...] = tail[taps]
        vectors[1][...] = tail[taps + 1]
        skips = pack_ref[at : at + 8]
        vectors[2][...] = jnp.concatenate([skips[p : p + 1] for p in range(pieces)], axis=1)[0]
        gain1_ref[...] = skips[pieces]
        gain2_ref[...] = skips[pieces + 1]
        count = skips[pieces + 2 : pieces + 3]
        for row in range(2):
            total = 0.0
            for digit in range(digits):
                first = (2 * digit + row) * experts
                total = total + 2.0**digit * count[:, first : first + experts]
            load_ref[row : row + 1, :] = total * scale
        router_ref[...] = pack_ref[at + 8 : at + 8 + experts]

    shapes = [(k, w), (rank, w), (n, w), (taps, w), (w,), (w,), (w,), (d,), (d,), (experts, d), (2, experts)]
    return pl.pallas_call(
        kernel,
        grid=(1,),
        out_shape=(shape_of(wide.shape, f32),) + tuple(shape_of(v, f32) for v in shapes),
        in_specs=[SM, whole(*mine.shape), whole(*mine.shape), pl.BlockSpec(memory_space=pl.ANY)],
        out_specs=(whole(d, w),) + tuple(whole(*v) for v in shapes),
        scratch_shapes=[pltpu.VMEM((holders * srows, d), f32)],
        input_output_aliases={3: 0},
        compiler_params=params(),
    )(core, mine, other, wide)


def blend(pick, near, far, prob, two):
    s, t, d = two.shape

    def kernel(pick_ref, near_ref, far_ref, prob_ref, two_ref, out_ref):
        rows = dot_tn(pick_ref[...], near_ref[...]) + dot_tn(pick_ref[...], far_ref[...])
        for seq in range(s):
            out_ref[seq] = two_ref[seq] + prob_ref[seq] * rows[seq * t : (seq + 1) * t]

    return pl.pallas_call(
        kernel,
        out_shape=shape_of((s, t, d), f32),
        in_specs=[VM] * 5,
        out_specs=VM,
        compiler_params=params(),
    )(pick, near, far, prob, two)


def shifted(value, axis, steps):
    count = lax.axis_size(axis)
    leading, last = (max(0, -steps), min(count, count - steps))
    return lax.ppermute(value, axis, [(source, source + steps) for source in range(leading, last)])


def swapped(value, axis, mask):
    return lax.ppermute(value, axis, [(i, i ^ mask) for i in range(lax.axis_size(axis))])


def after(value, *others):
    return lax.optimization_barrier((value, others))[0]


def together(*values):
    return lax.optimization_barrier(values)


def exchanged(parts, axis):
    return lax.all_to_all(parts, axis, split_axis=0, concat_axis=0, tiled=True)


def added(first, *others):
    total = first.astype(f32)
    for other in others:
        total = total + other.astype(f32)
    return total.astype(bf16)


def bits_of(axis):
    return range(lax.axis_size(axis).bit_length() - 1)


def doubled(block, axis, bit, dim):
    other = swapped(block, axis, 1 << bit)
    low = (lax.axis_index(axis) >> bit) & 1 == 0
    return jnp.where(
        low,
        jnp.concatenate([block, other], axis=dim),
        jnp.concatenate([other, block], axis=dim),
    )


class Gather:
    def __init__(self, block):
        many = len(bits_of("expert")) - 1
        cut = block.shape[1] // 2
        self.many = many
        self.routes = [[*range(1, many + 1)], [*range(many, 0, -1)]]
        self.halves = [
            piece.reshape((2,) * many + piece.shape[1:]) for piece in (block[:, :cut], block[:, cut:])
        ]

    def step(self, place):
        self.pairs = []
        for half, route in zip(self.halves, self.routes):
            bit = route[place]
            side = (lax.axis_index("expert") >> bit) & 1
            dim = self.many - bit
            stays = lax.dynamic_slice_in_dim(half, side, 1, dim)
            goes = lax.dynamic_slice_in_dim(half, 1 - side, 1, dim)
            self.pairs.append((stays, swapped(goes, "expert", 1 << bit)))
        return self.pairs

    def add(self):
        self.halves = [added(*pair) for pair in self.pairs]

    def whole(self):
        return jnp.concatenate([half.reshape(half.shape[self.many :]) for half in self.halves], axis=0)


def group_parts(block):
    count = lax.axis_size("dp")
    mine = lax.axis_index("dp")
    parts = block.reshape(count, -1, block.shape[-1])

    def part(place):
        return lax.dynamic_index_in_dim(parts, place, 0, keepdims=False)

    return [part(mine)] + [swapped(part(mine ^ mask), "dp", mask) for mask in range(1, count)]


def group_blocks(share):
    return [share] + [swapped(share, "dp", mask) for mask in range(1, lax.axis_size("dp"))]


def joined_groups(seen):
    mine = lax.axis_index("dp")
    blocks = []
    for place in range(len(seen)):
        block = seen[0]
        for mask in range(1, len(seen)):
            block = jnp.where(mine ^ mask == place, seen[mask], block)
        blocks.append(block)
    return jnp.concatenate(blocks, axis=0)


class Spread:
    def __init__(self, block):
        many = len(bits_of("expert")) - 1
        cut = block.shape[0] // 2
        self.many = many
        self.routes = [[*range(many, 0, -1)], [*range(1, many + 1)]]
        self.halves = [
            piece.reshape((1,) * many + piece.shape) for piece in (block[:cut], block[cut:])
        ]

    def step(self, place):
        self.halves = [
            doubled(half, "expert", route[place], self.many - route[place])
            for half, route in zip(self.halves, self.routes)
        ]
        return self.halves

    def whole(self):
        blocks = [half.reshape((-1,) + half.shape[self.many :]) for half in self.halves]
        return jnp.concatenate(blocks, axis=1)


def body(
    layer_input,
    norm1_gain,
    w_in,
    conv_weight,
    conv_bias,
    w_xproj,
    w_dt,
    dt_bias,
    a_log,
    d_skip,
    w_out,
    norm2_gain,
    router_weight,
    w_up,
    w_down,
    expert_route,
    capacity,
    output_grad,
):
    seq_count, span_len, model_width = layer_input.shape
    inner_width = w_in.shape[1] // 2
    conv_taps = conv_weight.shape[0]
    rank_dt = w_dt.shape[0]
    state_width = a_log.shape[1]
    experts_all = router_weight.shape[1]
    tokens = seq_count * span_len
    groups, holders = (lax.axis_size("dp"), lax.axis_size("expert"))
    slot_count = max(2, 5 * tokens // (4 * experts_all))
    slots = experts_all * slot_count
    far = max(1, groups // 2)
    w_masks = range(1, far)
    mine = lax.axis_index("expert").astype(jnp.int32).reshape(1)
    reach = 8

    core = mine & 1

    def traded(placed):
        blocks = placed.reshape(experts_all, slot_count, model_width)
        return exchanged(blocks, "expert").reshape(slots, model_width)

    rim = shifted(layer_input[:, span_len - reach :], "expert", 1)
    pick, placed, choose, counts = route(
        expert_route, capacity, after(output_grad, rim), slot_count
    )
    og_own = traded(placed)
    up_mats = [w_up[0]] + [swapped(w_up[0], "dp", mask) for mask in w_masks]
    down_mats = [w_down[0]] + [swapped(w_down[0], "dp", mask) for mask in w_masks]
    router_t = router_weight.T

    normed, conv_in, gate_z, pre_conv, act, sel, selt, dt_pre, step, rate2, ends = front(
        layer_input, rim, norm1_gain, w_in, conv_weight, conv_bias, w_xproj.T, w_dt, dt_bias, a_log.T
    )
    og_own, ends = together(og_own, ends)
    og_other = swapped(og_own, "dp", far)
    every = lax.all_gather(ends, "expert")
    saved, y_full, gated, stream_two, gate_prob, placed = middle(
        mine, every, step, act, sel, selt, rate2, d_skip, gate_z, layer_input, w_out, norm2_gain, pick, choose,
        router_t,
    )

    row_own = traded(placed)
    row_own, og_other, up_mats, down_mats = together(row_own, og_other, up_mats, down_mats)
    row_other = swapped(row_own, "dp", far)
    fwd_a, bwd_a, grd_a, log_a, hid_a, pre_a = expert_rows(
        mine, row_own, og_own, router_t, up_mats, down_mats, bf16
    )
    near_rows = traded(fwd_a)
    row_other, bwd_a, near_rows = together(row_other, bwd_a, near_rows)
    fwd_b, bwd_b, grd_b, log_b, hid_b, pre_b = expert_rows(
        mine, row_other, og_other, router_t, up_mats, down_mats, bf16
    )
    bwd_back = swapped(bwd_b, "dp", far)
    up_grad, down_grad, lows, router_grad = expert_grads(
        (row_own, row_other), (grd_a, grd_b), (log_a, log_b), (hid_a, hid_b), (pre_a, pre_b)
    )
    far_rows = traded(fwd_b)
    bwd_back, router_grad, far_rows = together(bwd_back, router_grad, far_rows)
    got = traded(added(bwd_a, bwd_back))

    stream_two_grad, gain_two_grad, y_grad, z_grad, skip_grad, early, sent = back(
        core, got, pick, stream_two, norm2_gain, output_grad, w_out, gate_z, y_full, act, gated, normed, holders
    )
    far_rows = swapped(far_rows, "dp", far)
    y_grad, far_rows = together(y_grad, far_rows)

    def back_from(piece, *others):
        return [swapped(after(low, *others), "dp", mask) for low, mask in zip(lows[piece], w_masks)]

    y_grad, sent = together(y_grad, sent)
    came = swapped(sent, "expert", 1)
    head = head_of(y_grad, step, selt, rate2)
    head, came = together(head, came)
    backs = [back_from(0, y_grad)]
    heads = lax.all_gather(head, "expert", tiled=False)
    heads, early, came, backs[0] = together(heads, early, came, backs[0])
    backs += [back_from(1, heads), back_from(2, heads)]
    first = Gather(added(early, came))
    pre_grads = []
    for seq in range(seq_count):
        if seq < first.many:
            first.step(seq)
        pre_grad, rim_rows, small = scan_back(
            conv_taps, seq, mine, heads, every, step, act, y_grad, sel, selt, rate2, saved, dt_pre, w_dt,
            w_xproj.T, d_skip, pre_conv, conv_in, (small, rim_rows) if seq else (),
        )
        pre_grads.append(pre_grad)
        if seq < first.many:
            rim_rows, heads, first.pairs = together(rim_rows, heads, first.pairs)
            first.add()
        if seq == 0:
            rim_rows, heads, *backs[1:] = together(rim_rows, heads, *backs[1:])
            backs.append(back_from(3, heads))
    for place in range(seq_count, first.many):
        first.step(place)
        first.add()
    rim_rows, backs[3] = together(rim_rows, backs[3])
    rims = shifted(rim_rows, "expert", -1)
    parts = group_parts(first.whole())
    in_rows = model_width // holders * (inner_width // model_width)
    lines = inner_width // model_width * small.shape[0] + 8 + experts_all
    srows = -(-lines // (16 * holders)) * 16
    srows += -(in_rows + srows) % (8 * groups)
    late, sent, grad_input = finish(
        core, pre_grads, rims, conv_weight, z_grad, w_in, layer_input, norm1_gain, normed,
        stream_two_grad, small, skip_grad, gain_two_grad, counts, router_grad, (holders, srows),
    )
    parts, late, sent = together(parts, late, sent)

    came = swapped(sent, "expert", 1)
    many = len(bits_of("dp"))
    share = added(*parts)
    block = share.reshape((1,) * many + share.shape)
    bits = [*reversed(bits_of("dp"))]
    last = Gather(added(late, came))
    expert_sums = [(down_grad, backs[2:]), (up_grad, backs[:2])]
    done_sums = []
    for place in range(last.many):
        ready = last.halves
        last.step(place)
        if place < 2:
            total, pieces = expert_sums[place]
            total = after(total, ready)
            for pair in zip(*pieces):
                total = total + jnp.concatenate(pair, axis=0).astype(f32)
            total, last.pairs = together(total, last.pairs)
            done_sums.append(total)
        if bits:
            bit = bits.pop(0)
            block = doubled(block, "dp", bit, many - 1 - bit)
        last.pairs, block = together(last.pairs, block)
        last.add()
    grad_w_down, grad_w_up = done_sums
    for bit in bits:
        block = doubled(block, "dp", bit, many - 1 - bit)
    parts = group_parts(last.whole())
    spread = Spread(block.reshape(-1, model_width))
    parts, *spread.halves = together(parts, *spread.step(0))
    seen = group_blocks(added(*parts))
    for place in range(1, spread.many):
        spread.step(place)
    seen, *spread.halves = together(seen, *spread.halves)
    early = spread.whole()
    early_far = swapped(early, "expert", 1)
    spread = Spread(joined_groups(seen))
    early, early_far, *spread.halves = together(early, early_far, *spread.step(0))
    for place in range(1, spread.many):
        spread.step(place)
    grad_w_in, grad_w_out = unpack_early(core, early, early_far, 2 * inner_width)
    result = blend(pick, near_rows, far_rows, gate_prob, stream_two)
    grad_w_in, result, *spread.halves = together(grad_w_in, result, *spread.halves)
    late = spread.whole()
    late_far = swapped(late, "expert", 1)
    grad_w_in, wx_grad, wdt_grad, alog_grad, conv_grad, *vectors, expert_loads = unpack_late(
        core, late, late_far, grad_w_in, (sel.shape[2], rank_dt, state_width, conv_taps), experts_all,
        tokens.bit_length(), experts_all / (tokens * groups * holders),
    )
    conv_b_grad, dt_b_grad, skip_grad, gain_one, gain_two, router_grad = vectors
    return (
        result,
        grad_input,
        gain_one,
        grad_w_in,
        conv_grad,
        conv_b_grad,
        wx_grad.T,
        wdt_grad,
        dt_b_grad,
        alog_grad.T,
        skip_grad,
        grad_w_out,
        gain_two,
        router_grad.T,
        grad_w_up[None],
        grad_w_down[None],
        expert_loads,
    )


def solution(mesh):
    in_specs = (
        P("dp", "expert", None),
        P(),
        P(),
        P(),
        P(),
        P(),
        P(),
        P(),
        P(),
        P(),
        P(),
        P(),
        P(),
        P("expert", None, "dp"),
        P("expert", "dp", None),
        P("dp", "expert"),
        P(),
        P("dp", "expert", None),
    )
    out_specs = (
        P("dp", "expert", None),
        P("dp", "expert", None),
        P(),
        P(),
        P(),
        P(),
        P(),
        P(),
        P(),
        P(),
        P(),
        P(),
        P(),
        P(),
        P("expert", None, "dp"),
        P("expert", "dp", None),
        P(),
    )
    return jax.shard_map(body, mesh=mesh, in_specs=in_specs, out_specs=out_specs, check_vma=False)
```
